32 devices in a mesh: section: 2 (over core), batch: 16 (over z, y, x).
Axes of the slice: x: 2, y: 2, z: 4, core: 2. Of those that a mesh axis runs over, the one named last changes fastest.
Arguments:
- layer_input: bfloat16 [4096, 768], P('batch'), may hold values from -6 to 6
- seq_lengths: int32 [32], P('batch'), may hold values from 64 to 128, as said below
- cotangent: bfloat16 [4096, 768], P('batch'), may hold values from -6 to 6
- project_weight: bfloat16 [2, 768, 2304], P('section'), may hold values from -0.4375 to 0.4375
- project_bias: float32 [2, 1536], P('section'), may hold values from -3 to 3
- conv_kernel: float32 [2, 12, 33], P('section'), may hold values from -0.6 to 0.6
- output_weight: bfloat16 [2, 768, 768], P('section'), may hold values from -0.625 to 0.625
- output_bias: float32 [2, 768], P('section'), may hold values from -3 to 3
- attn_gain: float32 [2, 768], P('section'), may hold values from 0.5 to 1.5
- attn_shift: float32 [2, 768], P('section'), may hold values from -3 to 3
- expand_weight: bfloat16 [2, 768, 3072], P('section'), may hold values from -0.21875 to 0.21875
- expand_bias: float32 [2, 3072], P('section'), may hold values from -3 to 3
- reduce_weight: bfloat16 [2, 3072, 768], P('section'), may hold values from -0.109375 to 0.109375
- reduce_bias: float32 [2, 768], P('section'), may hold values from -3 to 3
- final_gain: float32 [2, 768], P('section'), may hold values from 0.5 to 1.5
- final_shift: float32 [2, 768], P('section'), may hold values from -3 to 3
Outputs:
- activations: bfloat16 [2, 4096, 768], P('section', 'batch')
- input_grads: bfloat16 [2, 4096, 768], P('section', 'batch')
- grad_project_weight: float32 [2, 768, 2304], P('section', 'batch')
- grad_project_bias: float32 [2, 1536], P('section', 'batch')
- grad_conv_kernel: float32 [2, 12, 33], P('section')
- grad_output_weight: float32 [2, 768, 768], P('section', 'batch')
- grad_output_bias: float32 [2, 768], P('section', 'batch')
- grad_attn_gain: float32 [2, 768], P('section', 'batch')
- grad_attn_shift: float32 [2, 768], P('section', 'batch')
- grad_expand_weight: float32 [2, 768, 3072], P('section', 'batch')
- grad_expand_bias: float32 [2, 3072], P('section', 'batch')
- grad_reduce_weight: float32 [2, 3072, 768], P('section', 'batch')
- grad_reduce_bias: float32 [2, 768], P('section', 'batch')
- grad_final_gain: float32 [2, 768], P('section', 'batch')
- grad_final_shift: float32 [2, 768], P('section', 'batch')
- proxies: float32 [2, 6], P('section')
The draws below stay inside these ranges and needn't reach their ends.
Inputs may be any that keep to these rules, and one draw needn't show every extreme that they name: `seq_lengths`: each slot holds one sequence whose length is a multiple of 64; rows at and past the length are padding; slot 0 holds 128 tokens.
All inputs are finite; a program needn't handle non-finite values.
Results may differ from the reference program's by a relative error of at most 0.04.
Values may be sent and summed in bfloat16 or wider, within the bound.
A program may use at most 320 MiB of HBM per device.

```python
import jax
import jax.numpy as jnp
from jax import lax

D = 768
HEADS = 12
FF = 3072
LANDMARKS = 64
KW = 33
NEWTON = 6
MB = 2
ROWS = 128
SLOTS = 32
TOKENS = 4096
N_BATCH = 16


def draw_seq_lengths(key, part):
    key_short, key_long = jax.random.split(key, 2)
    blocks_top = ROWS // 64
    short_span = max(1, min(4, blocks_top - 1))
    short_blocks = 1 + jax.random.randint(key_short, (SLOTS,), 0, short_span + 1)
    short_blocks = jnp.minimum(short_blocks, blocks_top)
    long_pick = jax.random.randint(key_long, (SLOTS,), 0, 8) == 0
    block_count = jnp.where(long_pick, blocks_top, short_blocks)
    block_count = block_count.at[0].set(blocks_top)
    return (block_count * 64).astype(jnp.int32)


def shard_levels(own_key, extent, shards, least, high):
    gain, own = 1.0, jax.random.fold_in(own_key, 6)
    for dim, parts in shards:
        heights = jnp.exp(jax.random.uniform(jax.random.fold_in(own, dim), (parts,), jnp.float32, least / len(shards), high / len(shards)))
        gain = gain * jnp.repeat(heights, extent[dim] // parts).reshape([-1 if axis == dim else 1 for axis in range(len(extent))])
    return gain


def normal_values(key, extent, scale, reach, pieces=(), kind=jnp.bfloat16):
    drawn = scale * jax.random.normal(key, extent, jnp.float32)
    if pieces:
        drawn = drawn * shard_levels(key, extent, pieces, -0.22, 0.18)
    return jnp.clip(drawn, -reach, reach).astype(kind)


def setup_inputs(seed: int = 0) -> dict:
    splits = jax.random.split(jax.random.key(seed), 17)
    layer_input = normal_values(splits[0], (TOKENS, D), 1.0, 6.0, ((0, 16),))
    seq_lengths = draw_seq_lengths(jax.random.fold_in(splits[16], 71), 0)
    cotangent = normal_values(splits[2], (TOKENS, D), 1.0, 6.0, ((0, 16),))
    project_weight = normal_values(splits[3], (2, D, 3 * D), (D // 4) ** -0.5, 0.4375, ((0, 2),))
    project_bias = normal_values(splits[4], (2, 2 * D), 0.5, 3.0, ((0, 2),), jnp.float32)
    conv_kernel = normal_values(splits[5], (2, HEADS, KW), 0.1, 0.6, ((0, 2),), jnp.float32)
    output_weight = normal_values(splits[6], (2, D, D), (D // 8) ** -0.5, 0.625, ((0, 2),))
    output_bias = normal_values(splits[7], (2, D), 0.5, 3.0, ((0, 2),), jnp.float32)
    attn_gain = jnp.clip(1.0 + 0.1 * jax.random.normal(splits[8], (2, D), jnp.float32), 0.5, 1.5)
    attn_shift = normal_values(splits[9], (2, D), 0.5, 3.0, ((0, 2),), jnp.float32)
    expand_weight = normal_values(splits[10], (2, D, FF), D ** -0.5, 0.21875, ((0, 2),))
    expand_bias = normal_values(splits[11], (2, FF), 0.5, 3.0, ((0, 2),), jnp.float32)
    reduce_weight = normal_values(splits[12], (2, FF, D), FF ** -0.5, 0.109375, ((0, 2),))
    reduce_bias = normal_values(splits[13], (2, D), 0.5, 3.0, ((0, 2),), jnp.float32)
    final_gain = jnp.clip(1.0 + 0.1 * jax.random.normal(splits[14], (2, D), jnp.float32), 0.5, 1.5)
    final_shift = normal_values(splits[15], (2, D), 0.5, 3.0, ((0, 2),), jnp.float32)
    return dict(layer_input=layer_input, seq_lengths=seq_lengths, cotangent=cotangent, project_weight=project_weight, project_bias=project_bias, conv_kernel=conv_kernel, output_weight=output_weight, output_bias=output_bias, attn_gain=attn_gain, attn_shift=attn_shift, expand_weight=expand_weight, expand_bias=expand_bias, reduce_weight=reduce_weight, reduce_bias=reduce_bias, final_gain=final_gain, final_shift=final_shift)


MAXIMAL_PRECISION = lax.Precision.HIGHEST
NORM_EPSILON = 1e-05

@jax.custom_vjp
def low(v):
    return lax.optimization_barrier(v.astype(jnp.bfloat16)).astype(jnp.float32)

@jax.custom_vjp
def low_back(v):
    return v

def low_keep(v):
    return (low(v), None)

def low_pass(kept, grad):
    return (grad,)

def back_keep(v):
    return (v, None)

def back_low(kept, grad):
    return (low(grad),)
low.defvjp(low_keep, low_pass)
low_back.defvjp(back_keep, back_low)

def layer_norm(values, gain_vec, shift_vec):
    center = values - lax.optimization_barrier(jnp.mean(values, axis=-1, keepdims=True))
    spread = lax.optimization_barrier(jnp.mean(center * center, axis=-1, keepdims=True))
    return center * lax.rsqrt(spread + NORM_EPSILON) * gain_vec + shift_vec

def newton_inverse(kernel):
    landmark_count = kernel.shape[-1]
    identity = jnp.eye(landmark_count, dtype=jnp.float32)
    frobenius = lax.optimization_barrier(jnp.sum(kernel * kernel, axis=(1, 2), keepdims=True))
    pseudo_inverse = jnp.swapaxes(kernel, 1, 2) / frobenius
    errors = []
    for newton_step in range(NEWTON):
        product = jnp.matmul(kernel, pseudo_inverse, precision=MAXIMAL_PRECISION)
        factor = 7.0 * identity - product
        factor = 15.0 * identity - jnp.matmul(product, factor, precision=MAXIMAL_PRECISION)
        factor = 13.0 * identity - jnp.matmul(product, factor, precision=MAXIMAL_PRECISION)
        pseudo_inverse = 0.25 * jnp.matmul(pseudo_inverse, factor, precision=MAXIMAL_PRECISION)
        residue = identity - jnp.matmul(kernel, pseudo_inverse, precision=MAXIMAL_PRECISION)
        errors.append(jnp.sum(residue * residue))
    return (pseudo_inverse, jnp.stack(errors))

def attention(qkv_rows, kernel_taps, length):
    slot_rows = qkv_rows.shape[0]
    head_count = kernel_taps.shape[0]
    model_width = qkv_rows.shape[1] // 3
    head_size = model_width // head_count
    positions = jnp.arange(slot_rows, dtype=jnp.int32)
    valid_rows = (positions < length).astype(jnp.float32)[:, None]
    score_scale = head_size ** (-0.25)
    queries = (qkv_rows[:, :model_width] * valid_rows * score_scale).reshape(slot_rows, head_count, head_size)
    keys_all = (qkv_rows[:, model_width:2 * model_width] * valid_rows * score_scale).reshape(slot_rows, head_count, head_size)
    values_all = (qkv_rows[:, 2 * model_width:] * valid_rows).reshape(slot_rows, head_count, head_size)
    segment = length // LANDMARKS
    member = positions[None, :] // segment == jnp.arange(LANDMARKS, dtype=jnp.int32)[:, None]
    member = member & (positions[None, :] < length)
    pooling = member.astype(jnp.float32) / segment.astype(jnp.float32)
    landmark_queries = jnp.einsum('lr,rhd->hld', pooling, queries, precision=MAXIMAL_PRECISION)
    landmark_keys = jnp.einsum('lr,rhd->hld', pooling, keys_all, precision=MAXIMAL_PRECISION)
    kernel_first = jax.nn.softmax(jnp.einsum('rhd,hld->hrl', queries, landmark_keys, precision=MAXIMAL_PRECISION), axis=-1)
    middle_kernel = jax.nn.softmax(jnp.einsum('krg,kug->kru', landmark_queries, landmark_keys, precision=MAXIMAL_PRECISION), axis=-1)
    score_last = jnp.einsum('hld,rhd->hlr', landmark_queries, keys_all, precision=MAXIMAL_PRECISION)
    score_last = jnp.where(valid_rows[:, 0][None, None, :] > 0, score_last, -1e+30)
    kernel_last = jax.nn.softmax(score_last, axis=-1)
    pseudo_inverse, errors = newton_inverse(middle_kernel)
    landmark_digest = jnp.einsum('hlr,rhd->hld', kernel_last, values_all, precision=MAXIMAL_PRECISION)
    blended_values = jnp.einsum('pwc,pce->pwe', pseudo_inverse, landmark_digest, precision=MAXIMAL_PRECISION)
    attended = jnp.einsum('hrl,hld->rhd', kernel_first, blended_values, precision=MAXIMAL_PRECISION)
    half_width = (kernel_taps.shape[1] - 1) // 2
    padded = jnp.pad(values_all, ((half_width, half_width), (0, 0), (0, 0)))
    for tap_index in range(kernel_taps.shape[1]):
        attended = attended + kernel_taps[:, tap_index][None, :, None] * padded[tap_index:tap_index + slot_rows]
    return (attended.reshape(slot_rows, model_width), errors)

def layer(hidden, project_weight, project_bias, conv_kernel, output_weight, output_bias, attn_gain, attn_shift, expand_weight, expand_bias, reduce_weight, reduce_bias, final_gain, final_shift, lengths):
    group_count, slot_rows, model_width = hidden.shape
    flat_rows = hidden.reshape(-1, model_width)
    bias_full = jnp.concatenate([project_bias[:model_width], jnp.zeros((model_width,), jnp.float32), project_bias[model_width:]])
    qkv_rows = low_back(jnp.dot(low(flat_rows), project_weight, precision=MAXIMAL_PRECISION) + bias_full)
    attended, errors = jax.vmap(attention, in_axes=(0, None, 0))(qkv_rows.reshape(group_count, slot_rows, -1), conv_kernel, lengths)
    projected = low_back(jnp.dot(low(attended.reshape(-1, model_width)), output_weight, precision=MAXIMAL_PRECISION) + output_bias)
    first = layer_norm(flat_rows + projected, attn_gain, attn_shift)
    up_proj = low_back(jnp.dot(low(first), expand_weight, precision=MAXIMAL_PRECISION) + expand_bias)
    activated = low(jax.nn.gelu(up_proj, approximate=False))
    down_proj = low_back(jnp.dot(activated, reduce_weight, precision=MAXIMAL_PRECISION) + reduce_bias)
    normed = layer_norm(first + down_proj, final_gain, final_shift)
    valid_rows = (jnp.arange(slot_rows, dtype=jnp.int32)[None, :] < lengths[:, None]).astype(jnp.float32)
    return (normed.reshape(group_count, slot_rows, model_width) * valid_rows[:, :, None], lax.optimization_barrier(jnp.sum(errors, axis=0)))

def reference(layer_input, seq_lengths, cotangent, project_weight, project_bias, conv_kernel, output_weight, output_bias, attn_gain, attn_shift, expand_weight, expand_bias, reduce_weight, reduce_bias, final_gain, final_shift):
    stacked = [argument.astype(jnp.float32) for argument in (project_weight, project_bias, conv_kernel, output_weight, output_bias, attn_gain, attn_shift, expand_weight, expand_bias, reduce_weight, reduce_bias, final_gain, final_shift)]
    first_params = tuple((argument[0] for argument in stacked))
    second_params = tuple((argument[1] for argument in stacked))
    group_size = 4 * MB if N_BATCH % 4 == 0 else MB
    group_total = SLOTS // group_size
    inputs_all = layer_input.astype(jnp.float32).reshape(group_total, group_size, ROWS, D)
    cotangents = cotangent.astype(jnp.float32).reshape(group_total, group_size, ROWS, D)
    length_groups = seq_lengths.reshape(group_total, group_size)

    def group_step(totals, group_item):
        inputs_group, cot_group, length_group = group_item

        def apply_layer(hidden, *params):
            return layer(hidden, *params, length_group)
        mid_raw, back_first, errors_first = jax.vjp(apply_layer, inputs_group, *first_params, has_aux=True)
        mid_value = low(mid_raw)
        output_value, back_second, errors_second = jax.vjp(apply_layer, mid_value, *second_params, has_aux=True)
        grads_second = back_second(cot_group)
        grad_mid = low(grads_second[0])
        grads_first = back_first(grad_mid)
        new_totals = (tuple((total + grad for total, grad in zip(totals[0], grads_first[1:]))), tuple((total + grad for total, grad in zip(totals[1], grads_second[1:]))), totals[2] + errors_first, totals[3] + errors_second)
        return (new_totals, (mid_value, output_value, grads_first[0], grad_mid))
    zeros_first = tuple((jnp.zeros_like(argument) for argument in first_params))
    zeros_second = tuple((jnp.zeros_like(argument) for argument in second_params))
    start = (zeros_first, zeros_second, jnp.zeros((NEWTON,), jnp.float32), jnp.zeros((NEWTON,), jnp.float32))
    totals, (mids, outputs, grad_inputs, grad_mids) = lax.scan(group_step, start, (inputs_all, cotangents, length_groups))
    activations = jnp.stack([mids.reshape(TOKENS, D), outputs.reshape(TOKENS, D)]).astype(jnp.bfloat16)
    input_grads = jnp.stack([grad_inputs.reshape(TOKENS, D), grad_mids.reshape(TOKENS, D)]).astype(jnp.bfloat16)
    grads = tuple((jnp.stack([first_grad, second_grad]) for first_grad, second_grad in zip(totals[0], totals[1])))
    proxies = jnp.stack([totals[2], totals[3]])
    return (activations, input_grads, grads[0], grads[1], grads[2], grads[3], grads[4], grads[5], grads[6], grads[7], grads[8], grads[9], grads[10], grads[11], grads[12], proxies)
```

```python
import functools
import math

import jax
import jax.numpy as jnp
from jax import lax
from jax.experimental import pallas as pl
from jax.experimental.pallas import tpu as pltpu
from jax.sharding import PartitionSpec as P

F32 = jnp.float32
BF16 = jnp.bfloat16
NEWTON = 6
LM = 64
PAIR = 128
EPS = 1e-05
MESH = pl.DeviceIdType.MESH


def nn(a, b):
    return lax.dot_general(a, b, (((1,), (0,)), ((), ())), preferred_element_type=F32)


def nt(a, b):
    return lax.dot_general(a, b, (((1,), (1,)), ((), ())), preferred_element_type=F32)


def tn(a, b):
    return lax.dot_general(a, b, (((0,), (0,)), ((), ())), preferred_element_type=F32)


def split(x):
    high = x.astype(BF16)
    return high, (x - high.astype(F32)).astype(BF16)


def cat(parts, axis):
    return jnp.concatenate(parts, axis=axis)


def lane_is_first(rows, width=PAIR):
    return lax.broadcasted_iota(jnp.int32, (rows, width), 1) < width // 2


def spread(y):
    rows = y.shape[0]
    keep = lane_is_first(rows).astype(F32).astype(y.dtype)
    return cat([y * keep, y * (1 - keep)], 0)


def pick(x):
    rows = x.shape[0] // 2
    return jnp.where(lane_is_first(rows), x[:rows], x[rows:])


def nn3(xs, ys):
    (xh, xl), (yh, yl) = xs, ys
    dh, dl = spread(yh), spread(yl)
    return nn(cat([xh, xl], 1), cat([dh, dh], 0)) + nn(xh, dl)


def nt3(xs, ds):
    (xh, xl), (dh, dl) = xs, ds
    return nt(cat([xh, xl], 1), cat([dh, dh], 1)) + nt(xh, dl)


def half_sums(x, ones):
    high, low = split(x)
    return nn(high, ones) + nn(low, ones)


def block_ones():
    row = lax.broadcasted_iota(jnp.int32, (PAIR, PAIR), 0) < LM
    col = lax.broadcasted_iota(jnp.int32, (PAIR, PAIR), 1) < LM
    return (row == col).astype(F32).astype(BF16)


def pair_softmax(scores, ones):
    first = lane_is_first(scores.shape[0])
    top_a = jnp.max(jnp.where(first, scores, -jnp.inf), axis=1, keepdims=True)
    top_b = jnp.max(jnp.where(first, -jnp.inf, scores), axis=1, keepdims=True)
    e = jnp.exp(scores - jnp.where(first, top_a, top_b))
    return e / half_sums(e, ones)


def pair_transpose(x):
    t = x.T
    return cat([t[:LM], t[LM:]], 1)


def pair_eye():
    row = lax.broadcasted_iota(jnp.int32, (LM, PAIR), 0)
    col = lax.broadcasted_iota(jnp.int32, (LM, PAIR), 1)
    return (row == col % LM).astype(F32)


def pool_matrix(length, rows):
    landmark = lax.broadcasted_iota(jnp.int32, (LM, rows), 0)
    row = lax.broadcasted_iota(jnp.int32, (LM, rows), 1)
    segment = length // LM
    inside = (row >= landmark * segment) & (row < (landmark + 1) * segment)
    weight = 1.0 / jnp.full((LM, rows), segment, jnp.int32).astype(F32)
    return jnp.where(inside, weight, 0.0).astype(BF16)


def toeplitz(taps_row, rows, taps):
    half = taps // 2
    wide = jnp.broadcast_to(taps_row, (rows, rows))
    wide = pltpu.roll(wide, rows - half, 1, stride=1, stride_axis=0)
    row = lax.broadcasted_iota(jnp.int32, (rows, rows), 0)
    col = lax.broadcasted_iota(jnp.int32, (rows, rows), 1)
    near = (col - row <= half) & (row - col <= half)
    return jnp.where(near, wide, 0.0)


def attention_forward(
    sel_ref, x_ref, bias_ref, taps_ref, own_ref, other_ref,
    att_ref, qkv_ref, lm_ref, a1_ref, a2_ref, a3_ref, t_ref, newton_ref, db_ref, err_ref,
    w_ref, sem, *, taps):
    rows, width = x_ref.shape
    pairs = width // PAIR
    length = sel_ref[1]

    def part(i, source):
        cols = pl.ds(i * width, width)
        return pltpu.make_async_copy(source.at[:, cols], w_ref.at[:, cols], sem.at[i])

    @pl.when(sel_ref[0] == 1)
    def _():
        for i in range(3):
            part(i, own_ref).start()

    @pl.when(sel_ref[0] == 0)
    def _():
        for i in range(3):
            part(i, other_ref).start()

    ones = block_ones()
    pool = pool_matrix(length, rows)
    eye = pair_eye()
    sl = [pl.ds(p * PAIR, PAIR) for p in range(pairs)]
    for p in range(pairs):
        for j in range(2):
            t_ref[p, :, j * rows:(j + 1) * rows] = toeplitz(
                taps_ref[2 * p + j:2 * p + j + 1, :], rows, taps)
    valid = (lax.broadcasted_iota(jnp.int32, (rows, width), 0) < length).astype(F32)
    scale = LM ** (-0.25)
    x = x_ref[...]
    qkv = []
    for i in range(3):
        part(i, own_ref).wait()
        y = nn(x, w_ref[:, i * width:(i + 1) * width]) + bias_ref[i:i + 1, :]
        qkv.append(y * valid * (scale if i < 2 else 1.0))
    q, k, v = [[m[:, p * PAIR:(p + 1) * PAIR] for p in range(pairs)] for m in qkv]
    qs = [split(m) for m in q]
    ks = [split(m) for m in k]
    vs = [split(m) for m in v]
    for i, ms in enumerate((qs, ks, vs)):
        for p in range(pairs):
            qkv_ref[i, :, sl[p]] = ms[p][0]
    qls = [split(nn(pool, h) + nn(pool, l)) for h, l in qs]
    kls = [split(nn(pool, h) + nn(pool, l)) for h, l in ks]
    for p in range(pairs):
        lm_ref[0, :, sl[p]] = qls[p][0]
        lm_ref[1, :, sl[p]] = kls[p][0]
    kld = [(spread(h), spread(l)) for h, l in kls]
    for p in range(pairs):
        a2_ref[:, sl[p]] = pair_softmax(nt3(qls[p], kld[p]), ones)
    first = lane_is_first(LM)
    for p in range(pairs):
        a = a2_ref[:, sl[p]]
        squares = jnp.sum(a * a, axis=0, keepdims=True)
        fro_a = jnp.sum(jnp.where(first[:1], squares, 0.0), axis=1, keepdims=True)
        fro_b = jnp.sum(jnp.where(first[:1], 0.0, squares), axis=1, keepdims=True)
        newton_ref[0, 0, :, sl[p]] = pair_transpose(a) / jnp.where(first[:1], fro_a, fro_b)
    for p in range(pairs):
        z = split(newton_ref[0, 0, :, sl[p]])
        newton_ref[1, 0, :, sl[p]] = eye - nn3(split(a2_ref[:, sl[p]]), z)

    def newton_step(step, carry):
        s_all, t_all = [], []
        for p in range(pairs):
            r = newton_ref[1, step, :, sl[p]]
            rs = split(r)
            s = nn3(rs, rs)
            newton_ref[2, step, :, sl[p]] = s
            s_all.append((r, rs, s))
        for p in range(pairs):
            r, rs, s = s_all[p]
            t = nn3(split(s), rs)
            newton_ref[3, step, :, sl[p]] = t
            t_all.append(eye + r + s + 0.25 * t)
        for p in range(pairs):
            zn = nn3(split(newton_ref[0, step, :, sl[p]]), split(t_all[p]))
            newton_ref[0, step + 1, :, sl[p]] = zn
            rn = eye - nn3(split(a2_ref[:, sl[p]]), split(zn))
            newton_ref[1, step + 1, :, sl[p]] = rn
            err_ref[step, :, sl[p]] = jnp.sum(rn * rn, axis=0, keepdims=True)
        return carry

    lax.fori_loop(0, NEWTON, newton_step, 0)
    for p in range(pairs):
        wide = slice(p * 2 * rows, (p + 1) * 2 * rows)
        score = nt3(qls[p], (spread(ks[p][0]), spread(ks[p][1])))
        key = lax.broadcasted_iota(jnp.int32, (LM, rows), 1)
        halves = []
        for j in range(2):
            sc = jnp.where(key < length, score[:, j * rows:(j + 1) * rows], -1e30)
            e = jnp.exp(sc - jnp.max(sc, axis=1, keepdims=True))
            halves.append(e / jnp.sum(e, axis=1, keepdims=True))
        a3 = cat(halves, 1)
        a3_ref[:, wide] = a3
        a3h, a3l = split(a3)
        vh, vl = spread(vs[p][0]), spread(vs[p][1])
        d = nn(a3h, vh) + (nn(a3l, vh) + nn(a3h, vl))
        z = split(newton_ref[0, NEWTON, :, sl[p]])
        ds = split(d)
        b = nn3(z, ds)
        bs = split(b)
        db_ref[0, :, sl[p]] = ds[0]
        db_ref[1, :, sl[p]] = bs[0]
        a1 = pair_softmax(nt3(qs[p], kld[p]), ones)
        a1_ref[:, sl[p]] = a1
        th, tl = split(t_ref[p])
        o = nn3(split(a1), bs) + nn(cat([th, tl], 1), cat([vh, vh], 0)) + nn(th, vl)
        att_ref[:, sl[p]] = o.astype(BF16)


def softmax_back(a, da, ones):
    return a * (da - half_sums(a * da, ones))


def attention_backward(
    sel_ref, do_ref, gr_ref, qkv_ref, lm_ref, a1_ref, a2_ref, a3_ref, t_ref, newton_ref, db_ref,
    own_ref, other_ref,
    dqkv_ref, gi_ref, col_ref, dtaps_ref,
    w_ref, dz_ref, dr_ref, da_ref, sem, *, taps):
    rows, width = do_ref.shape
    pairs = width // PAIR
    length = sel_ref[1]

    def part(i, source):
        return pltpu.make_async_copy(source.at[:, pl.ds(i * width, width)], w_ref.at[i], sem.at[i])

    @pl.when(sel_ref[0] == 1)
    def _():
        for i in range(3):
            part(i, own_ref).start()

    @pl.when(sel_ref[0] == 0)
    def _():
        for i in range(3):
            part(i, other_ref).start()

    ones = block_ones()
    eye = pair_eye()
    pool = pool_matrix(length, rows)
    sl = [pl.ds(p * PAIR, PAIR) for p in range(pairs)]
    doh = [do_ref[:, sl[p]].astype(BF16) for p in range(pairs)]
    ddh = []
    for p in range(pairs):
        a1 = a1_ref[:, sl[p]].astype(BF16)
        db = pick(tn(a1, doh[p]))
        dbh = db.astype(BF16)
        z = newton_ref[0, NEWTON, :, sl[p]].astype(BF16)
        dz_ref[:, sl[p]] = nt(dbh, spread(db_ref[0, :, sl[p]]))
        dr_ref[:, sl[p]] = jnp.zeros((LM, PAIR), F32)
        ddh.append(pick(tn(z, dbh)).astype(BF16))

    def newton_back(index, carry):
        step = NEWTON - 1 - index
        keep = []
        for p in range(pairs):
            z = newton_ref[0, step, :, sl[p]]
            zh, zl = split(z)
            dz = dz_ref[:, sl[p]]
            gh, gl = split(dz)
            full = tn(cat([zh, zh, zl], 0), cat([gh, gl, gh], 0))
            df = pick(full + full.T) * 0.5
            keep.append((df, (gh, gl)))
        for p in range(pairs):
            df, g = keep[p]
            r, s, t = [newton_ref[i, step, :, sl[p]] for i in (1, 2, 3)]
            dz_ref[:, sl[p]] = nn3(g, split(eye + r + s + 0.25 * t))
            dr = dr_ref[:, sl[p]]
            dt = 0.25 * df + 0.75 * dr
            rs, ss, dts, drs = split(r), split(s), split(dt), split(0.5 * dr)
            m = nn3(dts, rs) + nn3(drs, ss)
            keep[p] = (df, dts, m, rs, ss)
        for p in range(pairs):
            df, dts, m, rs, ss = keep[p]
            ds = 2.0 * df + (m + pair_transpose(m))
            m = nn3(dts, ss) + nn3(split(ds), rs)
            dr_ref[:, sl[p]] = df + 0.5 * (m + pair_transpose(m))
        return carry

    lax.fori_loop(0, NEWTON, newton_back, 0)
    first = lane_is_first(1)
    for p in range(pairs):
        a = a2_ref[:, sl[p]]
        at = pair_transpose(a)
        dz = dz_ref[:, sl[p]]
        g = nn3(split(dr_ref[:, sl[p]]), split(a))

        def halves(m):
            c = jnp.sum(m, axis=0, keepdims=True)
            ca = jnp.sum(jnp.where(first, c, 0.0), axis=1, keepdims=True)
            cb = jnp.sum(jnp.where(first, 0.0, c), axis=1, keepdims=True)
            return jnp.where(first, ca, cb)

        inv = 1.0 / halves(a * a)
        dc = halves(dz * at) - halves(g * a)
        da_ref[:, sl[p]] = inv * (pair_transpose(dz) - 2.0 * g) - (2.0 * dc * inv * inv) * a
    scale = LM ** (-0.25)
    valid = (lax.broadcasted_iota(jnp.int32, (rows, PAIR), 0) < length).astype(F32)
    half = taps // 2
    row = lax.broadcasted_iota(jnp.int32, (rows, rows), 0)
    col = lax.broadcasted_iota(jnp.int32, (rows, rows), 1)
    flip = (row + col == rows - 1).astype(F32).astype(BF16)
    near = (col + row <= rows - 1 + half) & (col + row >= rows - 1 - half)
    for p in range(pairs):
        q, k, v = [qkv_ref[i, :, sl[p]] for i in range(3)]
        ql, kl = lm_ref[0, :, sl[p]], lm_ref[1, :, sl[p]]
        kld, kd, vd = spread(kl), spread(k), spread(v)
        wide = slice(p * 2 * rows, (p + 1) * 2 * rows)
        ds2 = softmax_back(a2_ref[:, sl[p]], da_ref[:, sl[p]], ones).astype(BF16)
        a1 = a1_ref[:, sl[p]]
        da1 = nt(doh[p], spread(db_ref[1, :, sl[p]]))
        ds1 = softmax_back(a1, da1, ones).astype(BF16)
        a3 = a3_ref[:, wide]
        da3 = nt(ddh[p], vd)
        parts = []
        for j in range(2):
            a, d = a3[:, j * rows:(j + 1) * rows], da3[:, j * rows:(j + 1) * rows]
            parts.append(a * (d - jnp.sum(a * d, axis=1, keepdims=True)))
        ds3 = cat(parts, 1).astype(BF16)
        th = t_ref[p].astype(BF16)
        dv = pick(tn(cat([a3.astype(BF16), th], 0), cat([ddh[p], doh[p]], 0)))
        full = nt(spread(nn(flip, doh[p]).astype(BF16)), v)
        for j in range(2):
            m = jnp.where(near, full[j * rows:(j + 1) * rows], 0.0)
            m = pltpu.roll(m, half + 1, 1, stride=1, stride_axis=0)
            dtaps_ref[2 * p + j:2 * p + j + 1, :] = jnp.sum(m, axis=0, keepdims=True)
        dkl = pick(tn(cat([ds1, ds2], 0), cat([q, ql], 0)))
        dql = nn(cat([ds2, ds3], 1), cat([kld, kd], 0))
        dqlh, dqll = split(dql)
        dklh, dkll = split(dkl)
        dq = nn(ds1, kld) + (tn(pool, dqlh) + tn(pool, dqll))
        dk = pick(tn(ds3, ql)) + (tn(pool, dklh) + tn(pool, dkll))
        for i, m in enumerate((dq * scale, dk * scale, dv)):
            low = (m * valid).astype(BF16)
            dqkv_ref[:, pl.ds(i * width + p * PAIR, PAIR)] = low
    for i in range(3):
        col_ref[i:i + 1, :] = jnp.sum(
            dqkv_ref[:, i * width:(i + 1) * width].astype(F32), axis=0, keepdims=True)
    total = gr_ref[...]
    for i in range(3):
        part(i, own_ref).wait()
        total = total + nt(dqkv_ref[:, i * width:(i + 1) * width], w_ref[i])
    gi_ref[...] = total.astype(BF16)


def weight_copies(groups, own_refs, other_refs, buffers, sem, flag):
    def make(i, refs):
        w, rows, cols = groups[i]
        return pltpu.make_async_copy(refs[w].at[rows, cols], buffers[w].at[rows, cols], sem.at[i])

    @pl.when(flag == 1)
    def _():
        for i in range(len(groups)):
            make(i, own_refs).start()

    @pl.when(flag == 0)
    def _():
        for i in range(len(groups)):
            make(i, other_refs).start()

    return lambda i: make(i, own_refs).wait()


def erf(x):
    return lax.erf(x)


def norm_forward(values):
    center = values - jnp.mean(values, axis=1, keepdims=True)
    rstd = lax.rsqrt(jnp.mean(center * center, axis=1, keepdims=True) + EPS)
    return center * rstd, rstd


def norm_back(grad, hat, rstd):
    mean = jnp.mean(grad, axis=1, keepdims=True)
    slope = jnp.mean(grad * hat, axis=1, keepdims=True)
    return rstd * (grad - mean - hat * slope)


def post_forward(
    sel_ref, att_ref, x_ref, vec_ref, wo_own, we_own, wr_own, wo_oth, we_oth, wr_oth,
    y_ref, first_ref, act_ref, hat1_ref, hat2_ref, rstd_ref, slope_ref,
    wo_ref, we_ref, wr_ref, sem):
    rows, width = x_ref.shape
    chunks = act_ref.shape[1] // width
    every = pl.ds(0, width)
    piece = [pl.ds(c * width, width) for c in range(chunks)]
    groups = [(0, every, every)]
    for c in range(chunks):
        groups += [(1, every, piece[c]), (2, piece[c], every)]
    wait = weight_copies(groups, (wo_own, we_own, wr_own), (wo_oth, we_oth, wr_oth),
                         (wo_ref, we_ref, wr_ref), sem, sel_ref[0])
    row = lambda i: vec_ref[i:i + 1, :]
    wait(0)
    hidden = x_ref[...].astype(F32) + (nn(att_ref[...], wo_ref[...]) + row(0))
    hat, rstd = norm_forward(hidden)
    hat1_ref[...] = hat
    rstd_ref[:, 0:1] = rstd
    first = hat * row(1) + row(2)
    low = first.astype(BF16)
    first_ref[...] = low
    down = first + row(7)
    for c in range(chunks):
        wait(1 + 2 * c)
        up = nn(low, we_ref[:, piece[c]]) + row(3 + c)
        cdf = 0.5 * (1.0 + erf(up * (2.0 ** -0.5)))
        act = (up * cdf).astype(BF16)
        slope_ref[:, piece[c]] = cdf + up * (jnp.exp(-0.5 * up * up) * 0.3989422804014327)
        act_ref[:, piece[c]] = act
        wait(2 + 2 * c)
        down = down + nn(act, wr_ref[piece[c], :])
    hat, rstd = norm_forward(down)
    hat2_ref[...] = hat
    rstd_ref[:, 1:2] = rstd
    valid = lax.broadcasted_iota(jnp.int32, (rows, width), 0) < sel_ref[1]
    y_ref[...] = jnp.where(valid, hat * row(8) + row(9), 0.0).astype(BF16)


def post_backward(
    sel_ref, g_ref, hat1_ref, hat2_ref, rstd_ref, slope_ref, vec_ref,
    wo_own, we_own, wr_own, wo_oth, we_oth, wr_oth,
    gd_ref, gu_ref, gp_ref, gr_ref, do_ref, sums_ref,
    wo_ref, we_ref, wr_ref, sem):
    rows, width = g_ref.shape
    chunks = gu_ref.shape[1] // width
    every = pl.ds(0, width)
    piece = [pl.ds(c * width, width) for c in range(chunks)]
    groups = []
    for c in range(chunks):
        groups += [(2, piece[c], every), (1, every, piece[c])]
    groups.append((0, every, every))
    wait = weight_copies(groups, (wo_own, we_own, wr_own), (wo_oth, we_oth, wr_oth),
                         (wo_ref, we_ref, wr_ref), sem, sel_ref[0])
    row = lambda i: vec_ref[i:i + 1, :]

    def total(i, values):
        sums_ref[i:i + 1, :] = jnp.sum(values, axis=0, keepdims=True)

    valid = lax.broadcasted_iota(jnp.int32, (rows, width), 0) < sel_ref[1]
    g = jnp.where(valid, g_ref[...].astype(F32), 0.0)
    hat2 = hat2_ref[...]
    total(8, g * hat2)
    total(9, g)
    second = norm_back(g * row(8), hat2, rstd_ref[:, 1:2])
    gd = second.astype(BF16)
    gd_ref[...] = gd
    total(7, gd.astype(F32))
    grad = second
    for c in range(chunks):
        wait(2 * c)
        gu = (nt(gd, wr_ref[piece[c], :]) * slope_ref[:, piece[c]]).astype(BF16)
        gu_ref[:, piece[c]] = gu
        total(3 + c, gu.astype(F32))
        wait(2 * c + 1)
        grad = grad + nt(gu, we_ref[:, piece[c]])
    hat1 = hat1_ref[...]
    total(1, grad * hat1)
    total(2, grad)
    residual = norm_back(grad * row(1), hat1, rstd_ref[:, 0:1])
    gr_ref[...] = residual
    gp = residual.astype(BF16)
    gp_ref[...] = gp
    total(0, gp.astype(F32))
    wait(2 * chunks)
    do_ref[...] = nt(gp, wo_ref[...])


def partner_of(bit):
    me = lax.axis_index("batch")
    side = (me // (1 << bit)) % 2
    return me + (1 - 2 * side) * (1 << bit), side


def place_of(block, order):
    last = len(order) - 1
    return sum(((block >> bit) & 1) << (last - k) for k, bit in enumerate(order))


def reduce_weights(*refs, owner, orders):
    count, bits = len(orders), len(orders[0])
    xs, ys = refs[:count], refs[count:2 * count]
    vec_ref = refs[2 * count]
    outs = refs[2 * count + 1:3 * count + 1]
    vec_out = refs[3 * count + 1]
    rest = refs[3 * count + 2:]
    xr, yr = rest[:count], rest[count:2 * count]
    grads = rest[2 * count:3 * count]
    got = rest[3 * count:4 * count]
    vec_got, vec_sum, op_send, op_recv, rs_send, rs_recv, v_send, v_recv = rest[4 * count:]
    mine = lax.axis_index("section") == owner
    barrier = pltpu.get_barrier_semaphore()

    def operand(i, first):
        source, target = (xs[i], xr[i]) if first else (ys[i], yr[i])
        slot = 2 * i + (0 if first else 1)
        return pltpu.make_async_remote_copy(
            src_ref=source, dst_ref=target, send_sem=op_send.at[slot], recv_sem=op_recv.at[slot],
            device_id={"section": owner}, device_id_type=MESH)

    def vec_in():
        return pltpu.make_async_remote_copy(
            src_ref=vec_ref, dst_ref=vec_got.at[bits], send_sem=v_send.at[bits],
            recv_sem=v_recv.at[bits], device_id={"section": owner}, device_id_type=MESH)

    @pl.when(jnp.logical_not(mine))
    def _():
        pl.semaphore_wait(barrier, 1)
        for i in range(count):
            operand(i, True).start()
            operand(i, False).start()
        vec_in().start()
        for i in range(count):
            operand(i, True).wait_send()
            operand(i, False).wait_send()
        vec_in().wait_send()

    @pl.when(mine)
    def _():
        pl.semaphore_signal(barrier, inc=1, device_id={"section": 1 - owner}, device_id_type=MESH)
        for bit in range(bits):
            pl.semaphore_signal(
                barrier, inc=1, device_id={"batch": partner_of(bit)[0]}, device_id_type=MESH)
        pl.semaphore_wait(barrier, bits)

        def spans(i, stage):
            order = orders[i]
            half = 1 << (bits - 1 - stage)
            start = 0
            for k in range(stage):
                start = start + partner_of(order[k])[1] * (1 << (bits - 1 - k))
            side = partner_of(order[stage])[1]
            landing = (1 << bits) - 2 * half
            return half, start + side * half, start + (1 - side) * half, landing

        def hop(i, stage):
            half, _, away, landing = spans(i, stage)
            return pltpu.make_async_remote_copy(
                src_ref=grads[i].at[pl.ds(away, half)], dst_ref=got[i].at[pl.ds(landing, half)],
                send_sem=rs_send.at[i, stage], recv_sem=rs_recv.at[i, stage],
                device_id={"batch": partner_of(orders[i][stage])[0]}, device_id_type=MESH)

        def vec_hop(stage):
            return pltpu.make_async_remote_copy(
                src_ref=vec_sum.at[stage], dst_ref=vec_got.at[stage],
                send_sem=v_send.at[stage], recv_sem=v_recv.at[stage],
                device_id={"batch": partner_of(stage)[0]}, device_id_type=MESH)

        vec_in().wait_recv()
        vec_sum[0] = vec_ref[...] + vec_got[bits]
        vec_hop(0).start()
        for i in range(count):
            operand(i, True).wait_recv()
            operand(i, False).wait_recv()
            depth, columns = xs[i].shape[1], ys[i].shape[1]
            block = grads[i].shape[1]
            rows = block * 128 // math.gcd(block, 128)
            step = min(columns, 768)
            for base in range(0, depth, rows):
                left = cat([xs[i][:, base:base + rows], xr[i][:, base:base + rows]], 0)
                for c in range(0, columns, step):
                    right = cat([ys[i][:, c:c + step], yr[i][:, c:c + step]], 0)
                    value = tn(left, right).astype(BF16)
                    for j in range(rows // block):
                        spot = place_of(base // block + j, orders[i])
                        grads[i][spot, :, c:c + step] = value[j * block:(j + 1) * block]
            hop(i, 0).start()
        for stage in range(bits):
            vec_hop(stage).wait_recv()
            vec_sum[stage + 1] = vec_sum[stage] + vec_got[stage]
            if stage + 1 < bits:
                vec_hop(stage + 1).start()
            for i in range(count):
                half, keep, _, landing = spans(i, stage)
                hop(i, stage).wait_recv()
                if stage + 1 < bits:
                    def add(j, carry):
                        grads[i][keep + j] = (
                            grads[i][keep + j].astype(F32) + got[i][landing + j].astype(F32)
                        ).astype(BF16)
                        return carry

                    lax.fori_loop(0, half, add, 0)
                    hop(i, stage + 1).start()
                else:
                    outs[i][...] = grads[i][keep].astype(F32) + got[i][landing].astype(F32)
        vec_out[...] = vec_sum[bits]
        for stage in range(bits):
            vec_hop(stage).wait_send()
            for i in range(count):
                hop(i, stage).wait_send()


def shape(dims, kind=F32):
    return jax.ShapeDtypeStruct(dims, kind)


IN_VMEM = pl.BlockSpec(memory_space=pltpu.VMEM)
IN_SMEM = pl.BlockSpec(memory_space=pltpu.SMEM)
ANYWHERE = pl.BlockSpec(memory_space=pl.ANY)
VMEM_LIMIT = 60 * 2 ** 20


def call(kernel, name, ins, outs, scratch, args, flops, moved, collective=None):
    extra = {} if collective is None else dict(collective_id=collective, has_side_effects=True)
    return pl.pallas_call(
        kernel, out_shape=tuple(outs), in_specs=ins, out_specs=(IN_VMEM,) * len(outs),
        scratch_shapes=scratch, name=name,
        cost_estimate=pl.CostEstimate(flops=flops, bytes_accessed=moved, transcendentals=0),
        compiler_params=pltpu.CompilerParams(vmem_limit_bytes=VMEM_LIMIT, **extra))(*args)


def forward_layer(sel, x, weights, others, vec, bias, taps_row, taps):
    rows, width = x.shape
    pairs, heads = width // PAIR, width // LM
    hidden = weights[2].shape[1]
    attended, qkv, lm, a1, a2, a3, band, newton, db, err = call(
        functools.partial(attention_forward, taps=taps), "attention_forward",
        [IN_SMEM] + [IN_VMEM] * 3 + [ANYWHERE] * 2,
        [shape((rows, width), BF16), shape((3, rows, width), BF16), shape((2, LM, width), BF16),
         shape((rows, width)), shape((LM, width)), shape((LM, heads * rows)),
         shape((pairs, rows, 2 * rows)), shape((4, NEWTON + 1, LM, width)),
         shape((2, LM, width), BF16), shape((NEWTON, 1, width))],
        [pltpu.VMEM((width, 3 * width), BF16), pltpu.SemaphoreType.DMA((3,))],
        (sel, x, bias, taps_row, weights[0], others[0]), 10 ** 10, 10 ** 7)
    chunks = hidden // width
    y, first, act, hat1, hat2, rstd, slope = call(
        post_forward, "post_forward",
        [IN_SMEM] + [IN_VMEM] * 3 + [ANYWHERE] * 6,
        [shape((rows, width), BF16), shape((rows, width), BF16), shape((rows, hidden), BF16),
         shape((rows, width)), shape((rows, width)), shape((rows, 128)), shape((rows, hidden))],
        [pltpu.VMEM((width, width), BF16), pltpu.VMEM((width, hidden), BF16),
         pltpu.VMEM((hidden, width), BF16), pltpu.SemaphoreType.DMA((1 + 2 * chunks,))],
        (sel, attended, x, vec) + tuple(weights[1:]) + tuple(others[1:]), 2 * 10 ** 9, 10 ** 7)
    kept = dict(x=x, attended=attended, attention=(qkv, lm, a1, a2, a3, band, newton, db),
                first=first, act=act, post=(hat1, hat2, rstd, slope))
    return y, err, kept


def backward_layer(sel, grad, kept, weights, others, vec, taps):
    rows, width = grad.shape
    hidden = weights[2].shape[1]
    chunks = hidden // width
    hat1, hat2, rstd, slope = kept["post"]
    gd, gu, gp, residual, d_attended, sums = call(
        post_backward, "post_backward",
        [IN_SMEM] + [IN_VMEM] * 6 + [ANYWHERE] * 6,
        [shape((rows, width), BF16), shape((rows, hidden), BF16), shape((rows, width), BF16),
         shape((rows, width)), shape((rows, width)), shape((4 + 2 + chunks, width))],
        [pltpu.VMEM((width, width), BF16), pltpu.VMEM((width, hidden), BF16),
         pltpu.VMEM((hidden, width), BF16), pltpu.SemaphoreType.DMA((1 + 2 * chunks,))],
        (sel, grad, hat1, hat2, rstd, slope, vec) + tuple(weights[1:]) + tuple(others[1:]),
        2 * 10 ** 9, 10 ** 7)
    heads = width // LM
    dqkv, gi, cols, dtaps = call(
        functools.partial(attention_backward, taps=taps), "attention_backward",
        [IN_SMEM] + [IN_VMEM] * 10 + [ANYWHERE] * 2,
        [shape((rows, 3 * width), BF16), shape((rows, width), BF16), shape((3, width)),
         shape((16, rows))],
        [pltpu.VMEM((3, width, width), BF16), pltpu.VMEM((LM, width), F32),
         pltpu.VMEM((LM, width), F32), pltpu.VMEM((LM, width), F32), pltpu.SemaphoreType.DMA((3,))],
        (sel, d_attended, residual) + kept["attention"] + (weights[0], others[0]),
        10 ** 10, 10 ** 7)
    xs = (kept["act"], kept["first"], kept["x"], kept["attended"])
    ys = (gd, gu, dqkv, gp)
    return gi, xs, ys, sums, cols, dtaps[:heads]


def small_rows(sums, cols, dtaps, err, width):
    residuals = jnp.pad(jnp.sum(err, axis=(1, 2)), (0, width - NEWTON))
    return jnp.concatenate([
        sums, cols[0:1], cols[2:3], dtaps.reshape(-1, width), residuals[None],
        jnp.zeros((16 - sums.shape[0] - 3 - dtaps.size // width, width), F32)], axis=0)


def reduce_on_slice(owner, xs, ys, small, batch):
    bits = batch.bit_length() - 1
    count = len(xs)
    first = (0, 1, 2)
    orders = []
    for i in (0, 1, 2, 2):
        turned = [first[i], first[(i + 1) % 3], first[(i + 2) % 3]]
        orders.append(tuple(turned + list(range(3, bits))))
    blocks = [x.shape[1] // batch for x in xs]
    outs = [shape((b, y.shape[1])) for b, y in zip(blocks, ys)] + [shape(small.shape)]
    scratch = [pltpu.VMEM(x.shape, BF16) for x in xs] + [pltpu.VMEM(y.shape, BF16) for y in ys]
    scratch += [pltpu.VMEM((batch, b, y.shape[1]), BF16) for b, y in zip(blocks, ys)]
    scratch += [pltpu.VMEM((batch - 1, b, y.shape[1]), BF16) for b, y in zip(blocks, ys)]
    scratch += [pltpu.VMEM((bits + 1,) + small.shape, F32), pltpu.VMEM((bits + 1,) + small.shape, F32)]
    dma = pltpu.SemaphoreType.DMA
    scratch += [dma((2 * count,)), dma((2 * count,)), dma((count, bits)), dma((count, bits)),
                dma((bits + 1,)), dma((bits + 1,))]
    return call(
        functools.partial(reduce_weights, owner=owner, orders=tuple(orders)),
        "reduce_weights", [IN_VMEM] * (2 * count + 1), outs, scratch,
        tuple(xs) + tuple(ys) + (small,), 4 * 10 ** 9, 10 ** 7, collective=owner)


def swap(value):
    return lax.ppermute(value, "section", [(0, 1), (1, 0)])


def body(
    layer_input, seq_lengths, cotangent, project_weight, project_bias, conv_kernel, output_weight,
    output_bias, attn_gain, attn_shift, expand_weight, expand_bias, reduce_weight, reduce_bias,
    final_gain, final_shift):
    section = lax.axis_index("section")
    batch = lax.axis_size("batch")
    lead = section == 0
    total, width = layer_input.shape
    rows = total // seq_lengths.shape[0]
    heads, taps = conv_kernel.shape[1:]
    weights = (project_weight[0], output_weight[0], expand_weight[0], reduce_weight[0])
    others = tuple(swap(w) for w in weights)
    tap_rows = jnp.pad(conv_kernel[0], ((0, 0), (0, 128 - taps)))
    pieces = [output_bias, attn_gain, attn_shift, expand_bias.reshape(-1, width), reduce_bias,
              final_gain, final_shift, project_bias.reshape(2, width),
              tap_rows.reshape(-1, width)]
    vec = jnp.concatenate(pieces, axis=0)
    vec_other = swap(vec)
    count = seq_lengths.shape[0]
    length = lax.dynamic_index_in_dim(seq_lengths, section, keepdims=False)
    own_rows = lambda v: lax.dynamic_slice_in_dim(v, section * rows, rows, 0)
    sels, vecs, biases, tap_list = [], [], [], []
    for layer in range(2):
        here = section == layer
        sels.append(jnp.stack([here.astype(jnp.int32), length]))
        v = jnp.where(here, vec, vec_other)
        vecs.append(v)
        biases.append(jnp.stack([v[10], jnp.zeros_like(v[10]), v[11]]))
        t = v[12:].reshape(heads, 128)
        tap_list.append(jnp.pad(t, ((0, 16 - heads), (0, 0))))
    value = own_rows(layer_input)
    outputs, residuals, kept = [], [], []
    for layer in range(2):
        value, err, saved = forward_layer(
            sels[layer], value, weights, others, vecs[layer], biases[layer], tap_list[layer], taps)
        outputs.append(value)
        residuals.append(err)
        kept.append(saved)
    crossed = swap(jnp.where(lead, outputs[1], outputs[0]))
    activations = jnp.where(
        lead, jnp.concatenate([outputs[0], crossed]), jnp.concatenate([crossed, outputs[1]]))
    grad = own_rows(cotangent)
    shares, grads = [None, None], [None, None]
    for layer in (1, 0):
        grad, xs, ys, sums, cols, dtaps = backward_layer(
            sels[layer], grad, kept[layer], weights, others, vecs[layer], taps)
        grads[layer] = grad
        small = small_rows(sums, cols, dtaps, residuals[layer], width)
        shares[layer] = reduce_layer(layer, xs, ys, small, batch)
    crossed = swap(jnp.where(lead, grads[1], grads[0]))
    input_grads = jnp.where(
        lead, jnp.concatenate([grads[0], crossed]), jnp.concatenate([crossed, grads[1]]))
    g_red, g_exp, g_qkv, g_out, small = [
        jnp.where(lead, a, b) for a, b in zip(shares[0], shares[1])]
    index = lax.axis_index("batch")

    def share(first, many):
        flat = small[first:first + many].reshape(-1)
        size = flat.shape[0] // batch
        return lax.dynamic_slice_in_dim(flat, index * size, size, 0)[None]

    chunks = reduce_weight.shape[1] // width
    at = 6 + chunks
    dtaps = small[at + 2:at + 2 + heads * 128 // width].reshape(heads, 128)[:, :taps]
    proxies = small[at + 2 + heads * 128 // width, :NEWTON]
    return (
        activations[None], input_grads[None], g_qkv[None], share(at, 2), dtaps[None], g_out[None],
        share(0, 1), share(1, 1), share(2, 1), g_exp[None], share(3, chunks), g_red[None],
        share(3 + chunks, 1), share(4 + chunks, 1), share(5 + chunks, 1), proxies[None])


def reduce_layer(layer, xs, ys, small, batch):
    if all((x.shape[1] // batch) % 16 == 0 for x in xs) and batch >= 8:
        return reduce_on_slice(layer, xs, ys, small, batch)
    products = [lax.dot_general(x, y, (((0,), (0,)), ((), ())), preferred_element_type=F32)
                for x, y in zip(xs, ys)]
    return [lax.psum_scatter(lax.psum(p, "section"), "batch", scatter_dimension=0, tiled=True)
            for p in products] + [lax.psum(small, ("section", "batch"))]


def solution(mesh):
    split_rows = P("batch", None)
    two, three = P("section", None), P("section", None, None)
    return jax.shard_map(
        body, mesh=mesh,
        in_specs=(split_rows, P("batch"), split_rows, three, two, three, three, two, two, two,
                  three, two, three, two, two, two),
        out_specs=(P("section", "batch", None), P("section", "batch", None),
                   P("section", "batch", None), P("section", "batch"), three,
                   P("section", "batch", None), P("section", "batch"), P("section", "batch"),
                   P("section", "batch"), P("section", "batch", None), P("section", "batch"),
                   P("section", "batch", None), P("section", "batch"), P("section", "batch"),
                   P("section", "batch"), two),
        check_vma=False)
```

```python
import functools
import math

import jax
import jax.numpy as jnp
from jax import lax
from jax.experimental import pallas as pl
from jax.experimental.pallas import tpu as pltpu
from jax.sharding import PartitionSpec as P

F32 = jnp.float32
BF16 = jnp.bfloat16
NEWTON = 6
LM = 64
PAIR = 128
EPS = 1e-05
MESH = pl.DeviceIdType.MESH


def nn(a, b):
    return lax.dot_general(a, b, (((1,), (0,)), ((), ())), preferred_element_type=F32)


def nt(a, b):
    return lax.dot_general(a, b, (((1,), (1,)), ((), ())), preferred_element_type=F32)


def tn(a, b):
    return lax.dot_general(a, b, (((0,), (0,)), ((), ())), preferred_element_type=F32)


def split(x):
    high = x.astype(BF16)
    return high, (x - high.astype(F32)).astype(BF16)


def cat(parts, axis):
    return jnp.concatenate(parts, axis=axis)


def lane_is_first(rows, width=PAIR):
    return lax.broadcasted_iota(jnp.int32, (rows, width), 1) < width // 2


def spread(y):
    rows = y.shape[0]
    keep = lane_is_first(rows).astype(F32).astype(y.dtype)
    return cat([y * keep, y * (1 - keep)], 0)


def pick(x):
    rows = x.shape[0] // 2
    return jnp.where(lane_is_first(rows), x[:rows], x[rows:])


def nn3(xs, ys):
    (xh, xl), (yh, yl) = xs, ys
    dh, dl = spread(yh), spread(yl)
    return nn(cat([xh, xl], 1), cat([dh, dh], 0)) + nn(xh, dl)


def nt3(xs, ds):
    (xh, xl), (dh, dl) = xs, ds
    return nt(cat([xh, xl], 1), cat([dh, dh], 1)) + nt(xh, dl)


def half_sums(x, ones):
    high, low = split(x)
    return nn(high, ones) + nn(low, ones)


def block_ones():
    row = lax.broadcasted_iota(jnp.int32, (PAIR, PAIR), 0) < LM
    col = lax.broadcasted_iota(jnp.int32, (PAIR, PAIR), 1) < LM
    return (row == col).astype(F32).astype(BF16)


def pair_softmax(scores, ones):
    first = lane_is_first(scores.shape[0])
    top_a = jnp.max(jnp.where(first, scores, -jnp.inf), axis=1, keepdims=True)
    top_b = jnp.max(jnp.where(first, -jnp.inf, scores), axis=1, keepdims=True)
    e = jnp.exp(scores - jnp.where(first, top_a, top_b))
    return e / half_sums(e, ones)


def pair_transpose(x):
    t = x.T
    return cat([t[:LM], t[LM:]], 1)


def pair_eye():
    row = lax.broadcasted_iota(jnp.int32, (LM, PAIR), 0)
    col = lax.broadcasted_iota(jnp.int32, (LM, PAIR), 1)
    return (row == col % LM).astype(F32)


def pool_matrix(length, rows):
    landmark = lax.broadcasted_iota(jnp.int32, (LM, rows), 0)
    row = lax.broadcasted_iota(jnp.int32, (LM, rows), 1)
    segment = length // LM
    inside = (row >= landmark * segment) & (row < (landmark + 1) * segment)
    weight = 1.0 / jnp.full((LM, rows), segment, jnp.int32).astype(F32)
    return jnp.where(inside, weight, 0.0).astype(BF16)


def toeplitz(taps_row, rows, taps):
    half = taps // 2
    wide = jnp.broadcast_to(taps_row, (rows, rows))
    wide = pltpu.roll(wide, rows - half, 1, stride=1, stride_axis=0)
    row = lax.broadcasted_iota(jnp.int32, (rows, rows), 0)
    col = lax.broadcasted_iota(jnp.int32, (rows, rows), 1)
    near = (col - row <= half) & (row - col <= half)
    return jnp.where(near, wide, 0.0)


def attention_forward(
    sel_ref, x_ref, bias_ref, taps_ref, own_ref, other_ref,
    att_ref, qkv_ref, lm_ref, a1_ref, a2_ref, a3_ref, t_ref, newton_ref, db_ref, err_ref,
    w_ref, sem, *, taps):
    rows, width = x_ref.shape
    pairs = width // PAIR
    length = sel_ref[1]

    def part(i, source):
        cols = pl.ds(i * width, width)
        return pltpu.make_async_copy(source.at[:, cols], w_ref.at[:, cols], sem.at[i])

    @pl.when(sel_ref[0] == 1)
    def _():
        for i in range(3):
            part(i, own_ref).start()

    @pl.when(sel_ref[0] == 0)
    def _():
        for i in range(3):
            part(i, other_ref).start()

    ones = block_ones()
    pool = pool_matrix(length, rows)
    eye = pair_eye()
    sl = [pl.ds(p * PAIR, PAIR) for p in range(pairs)]
    for p in range(pairs):
        for j in range(2):
            t_ref[p, :, j * rows:(j + 1) * rows] = toeplitz(
                taps_ref[2 * p + j:2 * p + j + 1, :], rows, taps)
    valid = (lax.broadcasted_iota(jnp.int32, (rows, width), 0) < length).astype(F32)
    scale = LM ** (-0.25)
    x = x_ref[...]
    qkv = []
    for i in range(3):
        part(i, own_ref).wait()
        y = nn(x, w_ref[:, i * width:(i + 1) * width]) + bias_ref[i:i + 1, :]
        qkv.append(y * valid * (scale if i < 2 else 1.0))
    q, k, v = [[m[:, p * PAIR:(p + 1) * PAIR] for p in range(pairs)] for m in qkv]
    qs = [split(m) for m in q]
    ks = [split(m) for m in k]
    vs = [split(m) for m in v]
    for i, ms in enumerate((qs, ks, vs)):
        for p in range(pairs):
            qkv_ref[i, :, sl[p]] = ms[p][0]
    qls = [split(nn(pool, h) + nn(pool, l)) for h, l in qs]
    kls = [split(nn(pool, h) + nn(pool, l)) for h, l in ks]
    for p in range(pairs):
        lm_ref[0, :, sl[p]] = qls[p][0]
        lm_ref[1, :, sl[p]] = kls[p][0]
    kld = [(spread(h), spread(l)) for h, l in kls]
    for p in range(pairs):
        a2_ref[:, sl[p]] = pair_softmax(nt3(qls[p], kld[p]), ones)
    first = lane_is_first(LM)
    for p in range(pairs):
        a = a2_ref[:, sl[p]]
        squares = jnp.sum(a * a, axis=0, keepdims=True)
        fro_a = jnp.sum(jnp.where(first[:1], squares, 0.0), axis=1, keepdims=True)
        fro_b = jnp.sum(jnp.where(first[:1], 0.0, squares), axis=1, keepdims=True)
        newton_ref[0, 0, :, sl[p]] = pair_transpose(a) / jnp.where(first[:1], fro_a, fro_b)
    for p in range(pairs):
        z = split(newton_ref[0, 0, :, sl[p]])
        newton_ref[1, 0, :, sl[p]] = eye - nn3(split(a2_ref[:, sl[p]]), z)

    def newton_step(step, carry):
        s_all, t_all = [], []
        for p in range(pairs):
            r = newton_ref[1, step, :, sl[p]]
            rs = split(r)
            s = nn3(rs, rs)
            newton_ref[2, step, :, sl[p]] = s
            s_all.append((r, rs, s))
        for p in range(pairs):
            r, rs, s = s_all[p]
            t = nn3(split(s), rs)
            newton_ref[3, step, :, sl[p]] = t
            t_all.append(eye + r + s + 0.25 * t)
        for p in range(pairs):
            zn = nn3(split(newton_ref[0, step, :, sl[p]]), split(t_all[p]))
            newton_ref[0, step + 1, :, sl[p]] = zn
            rn = eye - nn3(split(a2_ref[:, sl[p]]), split(zn))
            newton_ref[1, step + 1, :, sl[p]] = rn
            err_ref[step, :, sl[p]] = jnp.sum(rn * rn, axis=0, keepdims=True)
        return carry

    lax.fori_loop(0, NEWTON, newton_step, 0)
    for p in range(pairs):
        wide = slice(p * 2 * rows, (p + 1) * 2 * rows)
        score = nt3(qls[p], (spread(ks[p][0]), spread(ks[p][1])))
        key = lax.broadcasted_iota(jnp.int32, (LM, rows), 1)
        halves = []
        for j in range(2):
            sc = jnp.where(key < length, score[:, j * rows:(j + 1) * rows], -1e30)
            e = jnp.exp(sc - jnp.max(sc, axis=1, keepdims=True))
            halves.append(e / jnp.sum(e, axis=1, keepdims=True))
        a3 = cat(halves, 1)
        a3_ref[:, wide] = a3
        a3h, a3l = split(a3)
        vh, vl = spread(vs[p][0]), spread(vs[p][1])
        d = nn(a3h, vh) + (nn(a3l, vh) + nn(a3h, vl))
        z = split(newton_ref[0, NEWTON, :, sl[p]])
        ds = split(d)
        b = nn3(z, ds)
        bs = split(b)
        db_ref[0, :, sl[p]] = ds[0]
        db_ref[1, :, sl[p]] = bs[0]
        a1 = pair_softmax(nt3(qs[p], kld[p]), ones)
        a1_ref[:, sl[p]] = a1
        th, tl = split(t_ref[p])
        o = nn3(split(a1), bs) + nn(cat([th, tl], 1), cat([vh, vh], 0)) + nn(th, vl)
        att_ref[:, sl[p]] = o.astype(BF16)


def softmax_back(a, da, ones):
    return a * (da - half_sums(a * da, ones))


def attention_backward(
    sel_ref, do_ref, gr_ref, qkv_ref, lm_ref, a1_ref, a2_ref, a3_ref, t_ref, newton_ref, db_ref,
    own_ref, other_ref,
    dqkv_ref, gi_ref, col_ref, dtaps_ref,
    w_ref, dz_ref, dr_ref, da_ref, sem, *, taps):
    rows, width = do_ref.shape
    pairs = width // PAIR
    length = sel_ref[1]

    def part(i, source):
        return pltpu.make_async_copy(source.at[:, pl.ds(i * width, width)], w_ref.at[i], sem.at[i])

    @pl.when(sel_ref[0] == 1)
    def _():
        for i in range(3):
            part(i, own_ref).start()

    @pl.when(sel_ref[0] == 0)
    def _():
        for i in range(3):
            part(i, other_ref).start()

    ones = block_ones()
    eye = pair_eye()
    pool = pool_matrix(length, rows)
    sl = [pl.ds(p * PAIR, PAIR) for p in range(pairs)]
    doh = [do_ref[:, sl[p]].astype(BF16) for p in range(pairs)]
    ddh = []
    for p in range(pairs):
        a1 = a1_ref[:, sl[p]].astype(BF16)
        db = pick(tn(a1, doh[p]))
        dbh = db.astype(BF16)
        z = newton_ref[0, NEWTON, :, sl[p]].astype(BF16)
        dz_ref[:, sl[p]] = nt(dbh, spread(db_ref[0, :, sl[p]]))
        dr_ref[:, sl[p]] = jnp.zeros((LM, PAIR), F32)
        ddh.append(pick(tn(z, dbh)).astype(BF16))

    def newton_back(index, carry):
        step = NEWTON - 1 - index
        keep = []
        for p in range(pairs):
            z = newton_ref[0, step, :, sl[p]]
            zh, zl = split(z)
            dz = dz_ref[:, sl[p]]
            gh, gl = split(dz)
            full = tn(cat([zh, zh, zl], 0), cat([gh, gl, gh], 0))
            df = pick(full + full.T) * 0.5
            keep.append((df, (gh, gl)))
        for p in range(pairs):
            df, g = keep[p]
            r, s, t = [newton_ref[i, step, :, sl[p]] for i in (1, 2, 3)]
            dz_ref[:, sl[p]] = nn3(g, split(eye + r + s + 0.25 * t))
            dr = dr_ref[:, sl[p]]
            dt = 0.25 * df + 0.75 * dr
            rs, ss, dts, drs = split(r), split(s), split(dt), split(0.5 * dr)
            m = nn3(dts, rs) + nn3(drs, ss)
            keep[p] = (df, dts, m, rs, ss)
        for p in range(pairs):
            df, dts, m, rs, ss = keep[p]
            ds = 2.0 * df + (m + pair_transpose(m))
            m = nn3(dts, ss) + nn3(split(ds), rs)
            dr_ref[:, sl[p]] = df + 0.5 * (m + pair_transpose(m))
        return carry

    lax.fori_loop(0, NEWTON, newton_back, 0)
    first = lane_is_first(1)
    for p in range(pairs):
        a = a2_ref[:, sl[p]]
        at = pair_transpose(a)
        dz = dz_ref[:, sl[p]]
        g = nn3(split(dr_ref[:, sl[p]]), split(a))

        def halves(m):
            c = jnp.sum(m, axis=0, keepdims=True)
            ca = jnp.sum(jnp.where(first, c, 0.0), axis=1, keepdims=True)
            cb = jnp.sum(jnp.where(first, 0.0, c), axis=1, keepdims=True)
            return jnp.where(first, ca, cb)

        inv = 1.0 / halves(a * a)
        dc = halves(dz * at) - halves(g * a)
        da_ref[:, sl[p]] = inv * (pair_transpose(dz) - 2.0 * g) - (2.0 * dc * inv * inv) * a
    scale = LM ** (-0.25)
    valid = (lax.broadcasted_iota(jnp.int32, (rows, PAIR), 0) < length).astype(F32)
    half = taps // 2
    row = lax.broadcasted_iota(jnp.int32, (rows, rows), 0)
    col = lax.broadcasted_iota(jnp.int32, (rows, rows), 1)
    flip = (row + col == rows - 1).astype(F32).astype(BF16)
    near = (col + row <= rows - 1 + half) & (col + row >= rows - 1 - half)
    for p in range(pairs):
        q, k, v = [qkv_ref[i, :, sl[p]] for i in range(3)]
        ql, kl = lm_ref[0, :, sl[p]], lm_ref[1, :, sl[p]]
        kld, kd, vd = spread(kl), spread(k), spread(v)
        wide = slice(p * 2 * rows, (p + 1) * 2 * rows)
        ds2 = softmax_back(a2_ref[:, sl[p]], da_ref[:, sl[p]], ones).astype(BF16)
        a1 = a1_ref[:, sl[p]]
        da1 = nt(doh[p], spread(db_ref[1, :, sl[p]]))
        ds1 = softmax_back(a1, da1, ones).astype(BF16)
        a3 = a3_ref[:, wide]
        da3 = nt(ddh[p], vd)
        parts = []
        for j in range(2):
            a, d = a3[:, j * rows:(j + 1) * rows], da3[:, j * rows:(j + 1) * rows]
            parts.append(a * (d - jnp.sum(a * d, axis=1, keepdims=True)))
        ds3 = cat(parts, 1).astype(BF16)
        th = t_ref[p].astype(BF16)
        dv = pick(tn(cat([a3.astype(BF16), th], 0), cat([ddh[p], doh[p]], 0)))
        full = nt(spread(nn(flip, doh[p]).astype(BF16)), v)
        for j in range(2):
            m = jnp.where(near, full[j * rows:(j + 1) * rows], 0.0)
            m = pltpu.roll(m, half + 1, 1, stride=1, stride_axis=0)
            dtaps_ref[2 * p + j:2 * p + j + 1, :] = jnp.sum(m, axis=0, keepdims=True)
        dkl = pick(tn(cat([ds1, ds2], 0), cat([q, ql], 0)))
        dql = nn(cat([ds2, ds3], 1), cat([kld, kd], 0))
        dqlh, dqll = split(dql)
        dklh, dkll = split(dkl)
        dq = nn(ds1, kld) + (tn(pool, dqlh) + tn(pool, dqll))
        dk = pick(tn(ds3, ql)) + (tn(pool, dklh) + tn(pool, dkll))
        for i, m in enumerate((dq * scale, dk * scale, dv)):
            low = (m * valid).astype(BF16)
            dqkv_ref[:, pl.ds(i * width + p * PAIR, PAIR)] = low
    for i in range(3):
        col_ref[i:i + 1, :] = jnp.sum(
            dqkv_ref[:, i * width:(i + 1) * width].astype(F32), axis=0, keepdims=True)
    total = gr_ref[...]
    for i in range(3):
        part(i, own_ref).wait()
        total = total + nt(dqkv_ref[:, i * width:(i + 1) * width], w_ref[i])
    gi_ref[...] = total.astype(BF16)


def weight_copies(groups, own_refs, other_refs, buffers, sem, flag):
    def make(i, refs):
        w, rows, cols = groups[i]
        return pltpu.make_async_copy(refs[w].at[rows, cols], buffers[w].at[rows, cols], sem.at[i])

    @pl.when(flag == 1)
    def _():
        for i in range(len(groups)):
            make(i, own_refs).start()

    @pl.when(flag == 0)
    def _():
        for i in range(len(groups)):
            make(i, other_refs).start()

    return lambda i: make(i, own_refs).wait()


def erf(x):
    return lax.erf(x)


def norm_forward(values):
    center = values - jnp.mean(values, axis=1, keepdims=True)
    rstd = lax.rsqrt(jnp.mean(center * center, axis=1, keepdims=True) + EPS)
    return center * rstd, rstd


def norm_back(grad, hat, rstd):
    mean = jnp.mean(grad, axis=1, keepdims=True)
    slope = jnp.mean(grad * hat, axis=1, keepdims=True)
    return rstd * (grad - mean - hat * slope)


def post_forward(
    sel_ref, att_ref, x_ref, vec_ref, wo_own, we_own, wr_own, wo_oth, we_oth, wr_oth,
    y_ref, first_ref, act_ref, hat1_ref, hat2_ref, rstd_ref, slope_ref,
    wo_ref, we_ref, wr_ref, sem):
    rows, width = x_ref.shape
    chunks = act_ref.shape[1] // width
    every = pl.ds(0, width)
    piece = [pl.ds(c * width, width) for c in range(chunks)]
    groups = [(0, every, every)]
    for c in range(chunks):
        groups += [(1, every, piece[c]), (2, piece[c], every)]
    wait = weight_copies(groups, (wo_own, we_own, wr_own), (wo_oth, we_oth, wr_oth),
                         (wo_ref, we_ref, wr_ref), sem, sel_ref[0])
    row = lambda i: vec_ref[i:i + 1, :]
    wait(0)
    hidden = x_ref[...].astype(F32) + (nn(att_ref[...], wo_ref[...]) + row(0))
    hat, rstd = norm_forward(hidden)
    hat1_ref[...] = hat
    rstd_ref[:, 0:1] = rstd
    first = hat * row(1) + row(2)
    low = first.astype(BF16)
    first_ref[...] = low
    down = first + row(7)
    for c in range(chunks):
        wait(1 + 2 * c)
        up = nn(low, we_ref[:, piece[c]]) + row(3 + c)
        cdf = 0.5 * (1.0 + erf(up * (2.0 ** -0.5)))
        act = (up * cdf).astype(BF16)
        slope_ref[:, piece[c]] = cdf + up * (jnp.exp(-0.5 * up * up) * 0.3989422804014327)
        act_ref[:, piece[c]] = act
        wait(2 + 2 * c)
        down = down + nn(act, wr_ref[piece[c], :])
    hat, rstd = norm_forward(down)
    hat2_ref[...] = hat
    rstd_ref[:, 1:2] = rstd
    valid = lax.broadcasted_iota(jnp.int32, (rows, width), 0) < sel_ref[1]
    y_ref[...] = jnp.where(valid, hat * row(8) + row(9), 0.0).astype(BF16)


def post_backward(
    sel_ref, g_ref, hat1_ref, hat2_ref, rstd_ref, slope_ref, vec_ref,
    wo_own, we_own, wr_own, wo_oth, we_oth, wr_oth,
    gd_ref, gu_ref, gp_ref, gr_ref, do_ref, sums_ref,
    wo_ref, we_ref, wr_ref, sem):
    rows, width = g_ref.shape
    chunks = gu_ref.shape[1] // width
    every = pl.ds(0, width)
    piece = [pl.ds(c * width, width) for c in range(chunks)]
    groups = []
    for c in range(chunks):
        groups += [(2, piece[c], every), (1, every, piece[c])]
    groups.append((0, every, every))
    wait = weight_copies(groups, (wo_own, we_own, wr_own), (wo_oth, we_oth, wr_oth),
                         (wo_ref, we_ref, wr_ref), sem, sel_ref[0])
    row = lambda i: vec_ref[i:i + 1, :]

    def total(i, values):
        sums_ref[i:i + 1, :] = jnp.sum(values, axis=0, keepdims=True)

    valid = lax.broadcasted_iota(jnp.int32, (rows, width), 0) < sel_ref[1]
    g = jnp.where(valid, g_ref[...].astype(F32), 0.0)
    hat2 = hat2_ref[...]
    total(8, g * hat2)
    total(9, g)
    second = norm_back(g * row(8), hat2, rstd_ref[:, 1:2])
    gd = second.astype(BF16)
    gd_ref[...] = gd
    total(7, gd.astype(F32))
    grad = second
    for c in range(chunks):
        wait(2 * c)
        gu = (nt(gd, wr_ref[piece[c], :]) * slope_ref[:, piece[c]]).astype(BF16)
        gu_ref[:, piece[c]] = gu
        total(3 + c, gu.astype(F32))
        wait(2 * c + 1)
        grad = grad + nt(gu, we_ref[:, piece[c]])
    hat1 = hat1_ref[...]
    total(1, grad * hat1)
    total(2, grad)
    residual = norm_back(grad * row(1), hat1, rstd_ref[:, 0:1])
    gr_ref[...] = residual
    gp = residual.astype(BF16)
    gp_ref[...] = gp
    total(0, gp.astype(F32))
    wait(2 * chunks)
    do_ref[...] = nt(gp, wo_ref[...])


def partner_of(bit):
    me = lax.axis_index("batch")
    side = (me // (1 << bit)) % 2
    return me + (1 - 2 * side) * (1 << bit), side


def place_of(block, order):
    last = len(order) - 1
    return sum(((block >> bit) & 1) << (last - k) for k, bit in enumerate(order))


class Weight:
    def __init__(self, owner, order, by_rows):
        self.owner, self.order, self.by_rows = owner, order, by_rows
        self.bits = len(order)
        self.batch = 1 << self.bits
        self.rest = order[1:] if by_rows else order[1:] + order[:1]
        self.stages = self.bits - 1 if by_rows else self.bits

    def sizes(self, x, y):
        self.block = x[1] // self.batch
        self.run = (1 << self.order[0]) * self.block
        self.runs = self.batch >> (self.order[0] + 1) if self.by_rows else 1
        self.rows, self.depth, self.width = x[0], x[1], y[1]
        self.deep = self.depth // 2 if self.by_rows else self.depth
        self.wide = self.width if self.by_rows else self.width // 2
        self.blocks = self.batch // 2 if self.by_rows else self.batch
        return self

    def scratch(self):
        dma = pltpu.SemaphoreType.DMA
        return [
            pltpu.VMEM((3, self.rows, self.deep), BF16), pltpu.VMEM((3, self.rows, self.wide), BF16),
            pltpu.VMEM((self.blocks, self.block, self.wide), BF16),
            pltpu.VMEM((self.blocks - 1 if self.by_rows else self.blocks - 1, self.block, self.wide), BF16),
            dma((2, self.runs + 1)), dma((3, self.runs + 1)), dma((self.stages,)), dma((self.stages,))]

    def bind(self, x, y, out, scratch):
        self.x, self.y, self.out = x, y, out
        (self.xr, self.yr, self.sums, self.got,
         self.op_send, self.op_recv, self.hop_send, self.hop_recv) = scratch
        return self

    def side(self):
        return partner_of(self.order[0])[1]

    def pieces(self, ref, side, first):
        if first and self.by_rows:
            for r in range(self.runs):
                start = pl.multiple_of(2 * r * self.run + side * self.run, 128)
                yield ref.at[:, pl.ds(start, self.run)], pl.ds(r * self.run, self.run)
        elif first or self.by_rows:
            yield ref, pl.ds(0, ref.shape[1])
        else:
            yield ref.at[:, pl.ds(pl.multiple_of(side * self.wide, 128), self.wide)], pl.ds(0, self.wide)

    def operand(self, slot, away):
        other, side = partner_of(self.order[0])
        target = {"section": self.owner, "batch": other} if away else {"section": self.owner}
        side = 1 - side if away else side
        k = 0
        for first, ref, into in ((True, self.x, self.xr), (False, self.y, self.yr)):
            for source, lanes in self.pieces(ref, side, first):
                yield pltpu.make_async_remote_copy(
                    src_ref=source, dst_ref=into.at[slot, :, lanes],
                    send_sem=self.op_send.at[1 if away else 0, k], recv_sem=self.op_recv.at[slot, k],
                    device_id=target, device_id_type=MESH)
                k += 1

    def send_from_owner(self):
        for copy in self.operand(1, True):
            copy.start()

    def send_from_other(self):
        for slot, away in ((0, False), (2, True)):
            for copy in self.operand(slot, away):
                copy.start()

    def sent_from_other(self):
        for slot, away in ((0, False), (2, True)):
            for copy in self.operand(slot, away):
                copy.wait_send()

    def multiply(self):
        for slot, away in ((0, False), (1, True), (2, True)):
            for copy in self.operand(slot, away):
                copy.wait_recv()
        side = self.side()
        rows = self.block * 128 // math.gcd(self.block, 128)
        step = max(s for s in range(128, 1153, 128) if self.wide % s == 0)
        for base in range(0, self.deep, rows):
            if self.by_rows:
                r, inside = base // self.run, base % self.run
                lanes = pl.ds(pl.multiple_of(2 * r * self.run + side * self.run + inside, 128), rows)
            else:
                lanes = pl.ds(base, rows)
            left = cat([self.x[:, lanes]] + [self.xr[s, :, base:base + rows] for s in range(3)], 0)
            for c in range(0, self.wide, step):
                if self.by_rows:
                    near = self.y[:, c:c + step]
                else:
                    near = self.y[:, pl.ds(pl.multiple_of(side * self.wide + c, 128), step)]
                right = cat([near] + [self.yr[s, :, c:c + step] for s in range(3)], 0)
                value = tn(left, right).astype(BF16)
                for j in range(rows // self.block):
                    block = base // self.block + j
                    if self.by_rows:
                        low = 1 << self.order[0]
                        block = block // low * 2 * low + block % low
                    self.sums[place_of(block, self.rest), :, c:c + step] = (
                        value[j * self.block:(j + 1) * self.block])
        self.hop(0).start()

    def spans(self, stage):
        half = self.blocks >> (stage + 1)
        start = 0
        for k in range(stage):
            start = start + partner_of(self.rest[k])[1] * (self.blocks >> (k + 1))
        side = partner_of(self.rest[stage])[1]
        return half, start + side * half, start + (1 - side) * half, self.blocks - 2 * half

    def hop(self, stage):
        half, _, away, landing = self.spans(stage)
        return pltpu.make_async_remote_copy(
            src_ref=self.sums.at[pl.ds(away, half)], dst_ref=self.got.at[pl.ds(landing, half)],
            send_sem=self.hop_send.at[stage], recv_sem=self.hop_recv.at[stage],
            device_id={"batch": partner_of(self.rest[stage])[0]}, device_id_type=MESH)

    def advance(self, stage):
        half, keep, _, landing = self.spans(stage)
        self.hop(stage).wait_recv()
        if self.by_rows or stage + 1 < self.stages:
            if stage + 1 == self.stages:
                self.out[...] = self.sums[keep].astype(F32) + self.got[landing].astype(F32)
                return

            def add(j, carry):
                self.sums[keep + j] = (self.sums[keep + j].astype(F32)
                                       + self.got[landing + j].astype(F32)).astype(BF16)
                return carry

            lax.fori_loop(0, half, add, 0)
            self.hop(stage + 1).start()
        else:
            mine, theirs = self.sums[keep].astype(F32), self.got[landing].astype(F32)
            first = self.side() == 0
            self.out[:, :self.wide] = jnp.where(first, mine, theirs)
            self.out[:, self.wide:] = jnp.where(first, theirs, mine)

    def drain(self):
        for copy in self.operand(1, True):
            copy.wait_send()
        for stage in range(self.stages):
            self.hop(stage).wait_send()


class Small:
    def __init__(self, owner, bits):
        self.owner, self.bits = owner, bits
        self.stages = bits

    def scratch(self, dims):
        dma = pltpu.SemaphoreType.DMA
        return [pltpu.VMEM((self.bits + 1,) + dims, F32), pltpu.VMEM((self.bits + 1,) + dims, F32),
                dma((self.bits + 1,)), dma((self.bits + 1,))]

    def bind(self, x, out, scratch):
        self.x, self.out = x, out
        self.got, self.sums, self.sent, self.came = scratch
        return self

    def arrive(self):
        return pltpu.make_async_remote_copy(
            src_ref=self.x, dst_ref=self.got.at[self.bits], send_sem=self.sent.at[self.bits],
            recv_sem=self.came.at[self.bits], device_id={"section": self.owner}, device_id_type=MESH)

    def hop(self, stage):
        return pltpu.make_async_remote_copy(
            src_ref=self.sums.at[stage], dst_ref=self.got.at[stage], send_sem=self.sent.at[stage],
            recv_sem=self.came.at[stage], device_id={"batch": partner_of(stage)[0]},
            device_id_type=MESH)

    def send_from_owner(self):
        pass

    def send_from_other(self):
        self.arrive().start()

    def sent_from_other(self):
        self.arrive().wait_send()

    def multiply(self):
        self.arrive().wait_recv()
        self.sums[0] = self.x[...] + self.got[self.bits]
        self.hop(0).start()

    def advance(self, stage):
        self.hop(stage).wait_recv()
        self.sums[stage + 1] = self.sums[stage] + self.got[stage]
        if stage + 1 < self.bits:
            self.hop(stage + 1).start()
        else:
            self.out[...] = self.sums[self.bits]

    def drain(self):
        for stage in range(self.bits):
            self.hop(stage).wait_send()


def greet(owner, bits, near):
    barrier = pltpu.get_barrier_semaphore()
    mine = lax.axis_index("section") == owner

    @pl.when(mine)
    def _():
        pl.semaphore_signal(barrier, inc=1, device_id={"section": 1 - owner}, device_id_type=MESH)
        for bit in range(bits):
            pl.semaphore_signal(
                barrier, inc=1, device_id={"batch": partner_of(bit)[0]}, device_id_type=MESH)
        for bit in near:
            pl.semaphore_signal(
                barrier, inc=1, device_id={"section": 1 - owner, "batch": partner_of(bit)[0]},
                device_id_type=MESH)
        pl.semaphore_wait(barrier, bits)

    @pl.when(jnp.logical_not(mine))
    def _():
        pl.semaphore_wait(barrier, 1 + len(near))


def reduce_weights(*refs, weights, small):
    count = len(weights)
    owner, bits = small.owner, small.bits
    xs, ys, vec = refs[:count], refs[count:2 * count], refs[2 * count]
    outs, vec_out = refs[2 * count + 1:3 * count + 1], refs[3 * count + 1]
    rest = refs[3 * count + 2:]
    items = [w.bind(xs[i], ys[i], outs[i], rest[8 * i:8 * i + 8]) for i, w in enumerate(weights)]
    items = [small.bind(vec, vec_out, rest[8 * count:])] + items
    mine = lax.axis_index("section") == owner
    greet(owner, bits, sorted({w.order[0] for w in weights}))

    @pl.when(mine)
    def _():
        for item in items:
            item.send_from_owner()
        for item in items:
            item.multiply()
        for stage in range(bits):
            for item in items:
                if stage < item.stages:
                    item.advance(stage)
        for item in items:
            item.drain()

    @pl.when(jnp.logical_not(mine))
    def _():
        for item in items:
            item.send_from_other()
        for item in items:
            item.sent_from_other()


def shape(dims, kind=F32):
    return jax.ShapeDtypeStruct(dims, kind)


IN_VMEM = pl.BlockSpec(memory_space=pltpu.VMEM)
IN_SMEM = pl.BlockSpec(memory_space=pltpu.SMEM)
ANYWHERE = pl.BlockSpec(memory_space=pl.ANY)
VMEM_LIMIT = 60 * 2 ** 20


def call(kernel, name, ins, outs, scratch, args, flops, moved, collective=None):
    extra = {} if collective is None else dict(collective_id=collective, has_side_effects=True)
    return pl.pallas_call(
        kernel, out_shape=tuple(outs), in_specs=ins, out_specs=(IN_VMEM,) * len(outs),
        scratch_shapes=scratch, name=name,
        cost_estimate=pl.CostEstimate(flops=flops, bytes_accessed=moved, transcendentals=0),
        compiler_params=pltpu.CompilerParams(vmem_limit_bytes=VMEM_LIMIT, **extra))(*args)


def forward_layer(sel, x, weights, others, vec, bias, taps_row, taps):
    rows, width = x.shape
    pairs, heads = width // PAIR, width // LM
    hidden = weights[2].shape[1]
    attended, qkv, lm, a1, a2, a3, band, newton, db, err = call(
        functools.partial(attention_forward, taps=taps), "attention_forward",
        [IN_SMEM] + [IN_VMEM] * 3 + [ANYWHERE] * 2,
        [shape((rows, width), BF16), shape((3, rows, width), BF16), shape((2, LM, width), BF16),
         shape((rows, width)), shape((LM, width)), shape((LM, heads * rows)),
         shape((pairs, rows, 2 * rows)), shape((4, NEWTON + 1, LM, width)),
         shape((2, LM, width), BF16), shape((NEWTON, 1, width))],
        [pltpu.VMEM((width, 3 * width), BF16), pltpu.SemaphoreType.DMA((3,))],
        (sel, x, bias, taps_row, weights[0], others[0]), 10 ** 10, 10 ** 7)
    chunks = hidden // width
    y, first, act, hat1, hat2, rstd, slope = call(
        post_forward, "post_forward",
        [IN_SMEM] + [IN_VMEM] * 3 + [ANYWHERE] * 6,
        [shape((rows, width), BF16), shape((rows, width), BF16), shape((rows, hidden), BF16),
         shape((rows, width)), shape((rows, width)), shape((rows, 128)), shape((rows, hidden))],
        [pltpu.VMEM((width, width), BF16), pltpu.VMEM((width, hidden), BF16),
         pltpu.VMEM((hidden, width), BF16), pltpu.SemaphoreType.DMA((1 + 2 * chunks,))],
        (sel, attended, x, vec) + tuple(weights[1:]) + tuple(others[1:]), 2 * 10 ** 9, 10 ** 7)
    kept = dict(x=x, attended=attended, attention=(qkv, lm, a1, a2, a3, band, newton, db),
                first=first, act=act, post=(hat1, hat2, rstd, slope))
    return y, err, kept


def backward_layer(sel, grad, kept, weights, others, vec, taps):
    rows, width = grad.shape
    hidden = weights[2].shape[1]
    chunks = hidden // width
    hat1, hat2, rstd, slope = kept["post"]
    gd, gu, gp, residual, d_attended, sums = call(
        post_backward, "post_backward",
        [IN_SMEM] + [IN_VMEM] * 6 + [ANYWHERE] * 6,
        [shape((rows, width), BF16), shape((rows, hidden), BF16), shape((rows, width), BF16),
         shape((rows, width)), shape((rows, width)), shape((4 + 2 + chunks, width))],
        [pltpu.VMEM((width, width), BF16), pltpu.VMEM((width, hidden), BF16),
         pltpu.VMEM((hidden, width), BF16), pltpu.SemaphoreType.DMA((1 + 2 * chunks,))],
        (sel, grad, hat1, hat2, rstd, slope, vec) + tuple(weights[1:]) + tuple(others[1:]),
        2 * 10 ** 9, 10 ** 7)
    heads = width // LM
    dqkv, gi, cols, dtaps = call(
        functools.partial(attention_backward, taps=taps), "attention_backward",
        [IN_SMEM] + [IN_VMEM] * 10 + [ANYWHERE] * 2,
        [shape((rows, 3 * width), BF16), shape((rows, width), BF16), shape((3, width)),
         shape((16, rows))],
        [pltpu.VMEM((3, width, width), BF16), pltpu.VMEM((LM, width), F32),
         pltpu.VMEM((LM, width), F32), pltpu.VMEM((LM, width), F32), pltpu.SemaphoreType.DMA((3,))],
        (sel, d_attended, residual) + kept["attention"] + (weights[0], others[0]),
        10 ** 10, 10 ** 7)
    xs = (kept["act"], kept["first"], kept["x"], kept["attended"])
    ys = (gd, gu, dqkv, gp)
    return gi, xs, ys, sums, cols, dtaps[:heads]


def small_rows(sums, cols, dtaps, err, width):
    residuals = jnp.pad(jnp.sum(err, axis=(1, 2)), (0, width - NEWTON))
    return jnp.concatenate([
        sums, cols[0:1], cols[2:3], dtaps.reshape(-1, width), residuals[None],
        jnp.zeros((16 - sums.shape[0] - 3 - dtaps.size // width, width), F32)], axis=0)


def plan(owner, bits):
    tail = tuple(range(3, bits))
    return [Weight(owner, (1, 0, 2) + tail, True), Weight(owner, (0, 1, 2) + tail, False),
            Weight(owner, (1, 0, 2) + tail, False), Weight(owner, (2, 1, 0) + tail, False)]


def reduce_on_slice(owner, xs, ys, small, batch):
    bits = batch.bit_length() - 1
    weights = [w.sizes(x.shape, y.shape) for w, x, y in zip(plan(owner, bits), xs, ys)]
    outs = [shape((w.block, w.width)) for w in weights] + [shape(small.shape)]
    little = Small(owner, bits)
    scratch = [s for w in weights for s in w.scratch()] + little.scratch(small.shape)
    return call(
        functools.partial(reduce_weights, weights=weights, small=little),
        "reduce_weights", [IN_VMEM] * (2 * len(xs) + 1), outs, scratch,
        tuple(xs) + tuple(ys) + (small,), 4 * 10 ** 9, 10 ** 7, collective=owner)


def swap(value):
    return lax.ppermute(value, "section", [(0, 1), (1, 0)])


def body(
    layer_input, seq_lengths, cotangent, project_weight, project_bias, conv_kernel, output_weight,
    output_bias, attn_gain, attn_shift, expand_weight, expand_bias, reduce_weight, reduce_bias,
    final_gain, final_shift):
    section = lax.axis_index("section")
    batch = lax.axis_size("batch")
    lead = section == 0
    total, width = layer_input.shape
    rows = total // seq_lengths.shape[0]
    heads, taps = conv_kernel.shape[1:]
    weights = (project_weight[0], output_weight[0], expand_weight[0], reduce_weight[0])
    others = tuple(swap(w) for w in weights)
    tap_rows = jnp.pad(conv_kernel[0], ((0, 0), (0, 128 - taps)))
    pieces = [output_bias, attn_gain, attn_shift, expand_bias.reshape(-1, width), reduce_bias,
              final_gain, final_shift, project_bias.reshape(2, width),
              tap_rows.reshape(-1, width)]
    vec = jnp.concatenate(pieces, axis=0)
    vec_other = swap(vec)
    count = seq_lengths.shape[0]
    length = lax.dynamic_index_in_dim(seq_lengths, section, keepdims=False)
    own_rows = lambda v: lax.dynamic_slice_in_dim(v, section * rows, rows, 0)
    sels, vecs, biases, tap_list = [], [], [], []
    for layer in range(2):
        here = section == layer
        sels.append(jnp.stack([here.astype(jnp.int32), length]))
        v = jnp.where(here, vec, vec_other)
        vecs.append(v)
        biases.append(jnp.stack([v[10], jnp.zeros_like(v[10]), v[11]]))
        t = v[12:].reshape(heads, 128)
        tap_list.append(jnp.pad(t, ((0, 16 - heads), (0, 0))))
    value = own_rows(layer_input)
    outputs, residuals, kept = [], [], []
    for layer in range(2):
        value, err, saved = forward_layer(
            sels[layer], value, weights, others, vecs[layer], biases[layer], tap_list[layer], taps)
        outputs.append(value)
        residuals.append(err)
        kept.append(saved)
    crossed = swap(jnp.where(lead, outputs[1], outputs[0]))
    activations = jnp.where(
        lead, jnp.concatenate([outputs[0], crossed]), jnp.concatenate([crossed, outputs[1]]))
    grad = own_rows(cotangent)
    shares, grads = [None, None], [None, None]
    for layer in (1, 0):
        grad, xs, ys, sums, cols, dtaps = backward_layer(
            sels[layer], grad, kept[layer], weights, others, vecs[layer], taps)
        grads[layer] = grad
        small = small_rows(sums, cols, dtaps, residuals[layer], width)
        shares[layer] = reduce_layer(layer, xs, ys, small, batch)
    crossed = swap(jnp.where(lead, grads[1], grads[0]))
    input_grads = jnp.where(
        lead, jnp.concatenate([grads[0], crossed]), jnp.concatenate([crossed, grads[1]]))
    g_red, g_exp, g_qkv, g_out, small = [
        jnp.where(lead, a, b) for a, b in zip(shares[0], shares[1])]
    index = lax.axis_index("batch")

    def share(first, many):
        flat = small[first:first + many].reshape(-1)
        size = flat.shape[0] // batch
        return lax.dynamic_slice_in_dim(flat, index * size, size, 0)[None]

    chunks = reduce_weight.shape[1] // width
    at = 6 + chunks
    dtaps = small[at + 2:at + 2 + heads * 128 // width].reshape(heads, 128)[:, :taps]
    proxies = small[at + 2 + heads * 128 // width, :NEWTON]
    return (
        activations[None], input_grads[None], g_qkv[None], share(at, 2), dtaps[None], g_out[None],
        share(0, 1), share(1, 1), share(2, 1), g_exp[None], share(3, chunks), g_red[None],
        share(3 + chunks, 1), share(4 + chunks, 1), share(5 + chunks, 1), proxies[None])


def reduce_layer(layer, xs, ys, small, batch):
    if all((x.shape[1] // batch) % 16 == 0 for x in xs) and batch >= 8:
        return reduce_on_slice(layer, xs, ys, small, batch)
    products = [lax.dot_general(x, y, (((0,), (0,)), ((), ())), preferred_element_type=F32)
                for x, y in zip(xs, ys)]
    return [lax.psum_scatter(lax.psum(p, "section"), "batch", scatter_dimension=0, tiled=True)
            for p in products] + [lax.psum(small, ("section", "batch"))]


def solution(mesh):
    split_rows = P("batch", None)
    two, three = P("section", None), P("section", None, None)
    return jax.shard_map(
        body, mesh=mesh,
        in_specs=(split_rows, P("batch"), split_rows, three, two, three, three, two, two, two,
                  three, two, three, two, two, two),
        out_specs=(P("section", "batch", None), P("section", "batch", None),
                   P("section", "batch", None), P("section", "batch"), three,
                   P("section", "batch", None), P("section", "batch"), P("section", "batch"),
                   P("section", "batch"), P("section", "batch", None), P("section", "batch"),
                   P("section", "batch", None), P("section", "batch"), P("section", "batch"),
                   P("section", "batch"), two),
        check_vma=False)
```

```python
import functools
import math

import jax
import jax.numpy as jnp
from jax import lax
from jax.experimental import pallas as pl
from jax.experimental.pallas import tpu as pltpu
from jax.sharding import PartitionSpec as P

F32 = jnp.float32
BF16 = jnp.bfloat16
NEWTON = 6
LM = 64
PAIR = 128
EPS = 1e-05
MESH = pl.DeviceIdType.MESH


def nn(a, b):
    return lax.dot_general(a, b, (((1,), (0,)), ((), ())), preferred_element_type=F32)


def nt(a, b):
    return lax.dot_general(a, b, (((1,), (1,)), ((), ())), preferred_element_type=F32)


def tn(a, b):
    return lax.dot_general(a, b, (((0,), (0,)), ((), ())), preferred_element_type=F32)


def split(x):
    high = x.astype(BF16)
    return high, (x - high.astype(F32)).astype(BF16)


def cat(parts, axis):
    return jnp.concatenate(parts, axis=axis)


def lane_is_first(rows, width=PAIR):
    return lax.broadcasted_iota(jnp.int32, (rows, width), 1) < width // 2


def spread(y):
    rows = y.shape[0]
    keep = lane_is_first(rows).astype(F32).astype(y.dtype)
    return cat([y * keep, y * (1 - keep)], 0)


def pick(x):
    rows = x.shape[0] // 2
    return jnp.where(lane_is_first(rows), x[:rows], x[rows:])


def nn3(xs, ys):
    (xh, xl), (yh, yl) = xs, ys
    dh, dl = spread(yh), spread(yl)
    return nn(cat([xh, xl], 1), cat([dh, dh], 0)) + nn(xh, dl)


def nt3(xs, ds):
    (xh, xl), (dh, dl) = xs, ds
    return nt(cat([xh, xl], 1), cat([dh, dh], 1)) + nt(xh, dl)


def half_sums(x, ones):
    high, low = split(x)
    return nn(high, ones) + nn(low, ones)


def block_ones():
    row = lax.broadcasted_iota(jnp.int32, (PAIR, PAIR), 0) < LM
    col = lax.broadcasted_iota(jnp.int32, (PAIR, PAIR), 1) < LM
    return (row == col).astype(F32).astype(BF16)


def pair_softmax(scores, ones):
    first = lane_is_first(scores.shape[0])
    top_a = jnp.max(jnp.where(first, scores, -jnp.inf), axis=1, keepdims=True)
    top_b = jnp.max(jnp.where(first, -jnp.inf, scores), axis=1, keepdims=True)
    e = jnp.exp(scores - jnp.where(first, top_a, top_b))
    return e / half_sums(e, ones)


def pair_transpose(x):
    t = x.T
    return cat([t[:LM], t[LM:]], 1)


def pair_eye():
    row = lax.broadcasted_iota(jnp.int32, (LM, PAIR), 0)
    col = lax.broadcasted_iota(jnp.int32, (LM, PAIR), 1)
    return (row == col % LM).astype(F32)


def pool_matrix(length, rows):
    landmark = lax.broadcasted_iota(jnp.int32, (LM, rows), 0)
    row = lax.broadcasted_iota(jnp.int32, (LM, rows), 1)
    segment = length // LM
    inside = (row >= landmark * segment) & (row < (landmark + 1) * segment)
    weight = 1.0 / jnp.full((LM, rows), segment, jnp.int32).astype(F32)
    return jnp.where(inside, weight, 0.0).astype(BF16)


def toeplitz(taps_row, rows, taps):
    half = taps // 2
    wide = jnp.broadcast_to(taps_row, (rows, rows))
    wide = pltpu.roll(wide, rows - half, 1, stride=1, stride_axis=0)
    row = lax.broadcasted_iota(jnp.int32, (rows, rows), 0)
    col = lax.broadcasted_iota(jnp.int32, (rows, rows), 1)
    near = (col - row <= half) & (row - col <= half)
    return jnp.where(near, wide, 0.0)


def attention_forward(
    sel_ref, x_ref, bias_ref, taps_ref, own_ref, other_ref,
    att_ref, qkv_ref, lm_ref, a1_ref, a2_ref, a3_ref, t_ref, newton_ref, db_ref, err_ref,
    w_ref, sem, *, taps):
    rows, width = x_ref.shape
    pairs = width // PAIR
    length = sel_ref[1]

    def part(i, source):
        cols = pl.ds(i * width, width)
        return pltpu.make_async_copy(source.at[:, cols], w_ref.at[:, cols], sem.at[i])

    @pl.when(sel_ref[0] == 1)
    def _():
        for i in range(3):
            part(i, own_ref).start()

    @pl.when(sel_ref[0] == 0)
    def _():
        for i in range(3):
            part(i, other_ref).start()

    ones = block_ones()
    pool = pool_matrix(length, rows)
    eye = pair_eye()
    sl = [pl.ds(p * PAIR, PAIR) for p in range(pairs)]
    valid = (lax.broadcasted_iota(jnp.int32, (rows, width), 0) < length).astype(F32)
    scale = LM ** (-0.25)
    x = x_ref[...]
    qkv = []
    for i in range(3):
        part(i, own_ref).wait()
        y = nn(x, w_ref[:, i * width:(i + 1) * width]) + bias_ref[i:i + 1, :]
        qkv.append(y * valid * (scale if i < 2 else 1.0))
    q, k, v = [[m[:, p * PAIR:(p + 1) * PAIR] for p in range(pairs)] for m in qkv]
    qs = [split(m) for m in q]
    ks = [split(m) for m in k]
    vs = [split(m) for m in v]
    for i, ms in enumerate((qs, ks, vs)):
        for p in range(pairs):
            qkv_ref[i, :, sl[p]] = ms[p][0]
    qls = [split(nn(pool, h) + nn(pool, l)) for h, l in qs]
    kls = [split(nn(pool, h) + nn(pool, l)) for h, l in ks]
    for p in range(pairs):
        lm_ref[0, :, sl[p]] = qls[p][0]
        lm_ref[1, :, sl[p]] = kls[p][0]
    kld = [(spread(h), spread(l)) for h, l in kls]
    for p in range(pairs):
        a2_ref[:, sl[p]] = pair_softmax(nt3(qls[p], kld[p]), ones)
    first = lane_is_first(LM)
    for p in range(pairs):
        a = a2_ref[:, sl[p]]
        squares = jnp.sum(a * a, axis=0, keepdims=True)
        fro_a = jnp.sum(jnp.where(first[:1], squares, 0.0), axis=1, keepdims=True)
        fro_b = jnp.sum(jnp.where(first[:1], 0.0, squares), axis=1, keepdims=True)
        newton_ref[0, 0, :, sl[p]] = pair_transpose(a) / jnp.where(first[:1], fro_a, fro_b)
    for p in range(pairs):
        z = split(newton_ref[0, 0, :, sl[p]])
        newton_ref[1, 0, :, sl[p]] = eye - nn3(split(a2_ref[:, sl[p]]), z)

    def newton_step(step, carry):
        s_all, t_all = [], []
        for p in range(pairs):
            r = newton_ref[1, step, :, sl[p]]
            rs = split(r)
            s = nn3(rs, rs)
            newton_ref[2, step, :, sl[p]] = s
            s_all.append((r, rs, s))
        for p in range(pairs):
            r, rs, s = s_all[p]
            t = nn3(split(s), rs)
            newton_ref[3, step, :, sl[p]] = t
            t_all.append(eye + r + s + 0.25 * t)
        for p in range(pairs):
            zn = nn3(split(newton_ref[0, step, :, sl[p]]), split(t_all[p]))
            newton_ref[0, step + 1, :, sl[p]] = zn
            rn = eye - nn3(split(a2_ref[:, sl[p]]), split(zn))
            newton_ref[1, step + 1, :, sl[p]] = rn
            err_ref[step, :, sl[p]] = jnp.sum(rn * rn, axis=0, keepdims=True)
        return carry

    lax.fori_loop(0, NEWTON, newton_step, 0)
    for p in range(pairs):
        wide = slice(p * 2 * rows, (p + 1) * 2 * rows)
        score = nt3(qls[p], (spread(ks[p][0]), spread(ks[p][1])))
        key = lax.broadcasted_iota(jnp.int32, (LM, rows), 1)
        halves = []
        for j in range(2):
            sc = jnp.where(key < length, score[:, j * rows:(j + 1) * rows], -1e30)
            e = jnp.exp(sc - jnp.max(sc, axis=1, keepdims=True))
            halves.append(e / jnp.sum(e, axis=1, keepdims=True))
        a3 = cat(halves, 1)
        a3_ref[:, wide] = a3
        a3h, a3l = split(a3)
        vh, vl = spread(vs[p][0]), spread(vs[p][1])
        d = nn(a3h, vh) + (nn(a3l, vh) + nn(a3h, vl))
        z = split(newton_ref[0, NEWTON, :, sl[p]])
        ds = split(d)
        b = nn3(z, ds)
        bs = split(b)
        db_ref[0, :, sl[p]] = ds[0]
        db_ref[1, :, sl[p]] = bs[0]
        a1 = pair_softmax(nt3(qs[p], kld[p]), ones)
        a1_ref[:, sl[p]] = a1
        band = cat([toeplitz(taps_ref[2 * p + j:2 * p + j + 1, :], rows, taps) for j in range(2)], 1)
        th, tl = split(band)
        t_ref[p] = th
        o = nn3(split(a1), bs) + nn(cat([th, tl], 1), cat([vh, vh], 0)) + nn(th, vl)
        att_ref[:, sl[p]] = o.astype(BF16)


def softmax_back(a, da, ones):
    return a * (da - half_sums(a * da, ones))


def weight_copies(groups, own_refs, other_refs, buffers, sem, flag):
    def make(i, refs):
        w, rows, cols = groups[i]
        return pltpu.make_async_copy(refs[w].at[rows, cols], buffers[w].at[rows, cols], sem.at[i])

    @pl.when(flag == 1)
    def _():
        for i in range(len(groups)):
            make(i, own_refs).start()

    @pl.when(flag == 0)
    def _():
        for i in range(len(groups)):
            make(i, other_refs).start()

    return lambda i: make(i, own_refs).wait()


def erf(x):
    return lax.erf(x)


def norm_forward(values):
    center = values - jnp.mean(values, axis=1, keepdims=True)
    rstd = lax.rsqrt(jnp.mean(center * center, axis=1, keepdims=True) + EPS)
    return center * rstd, rstd


def norm_back(grad, hat, rstd):
    mean = jnp.mean(grad, axis=1, keepdims=True)
    slope = jnp.mean(grad * hat, axis=1, keepdims=True)
    return rstd * (grad - mean - hat * slope)


def post_forward(
    sel_ref, att_ref, x_ref, vec_ref, wo_own, we_own, wr_own, wo_oth, we_oth, wr_oth,
    y_ref, first_ref, act_ref, hat1_ref, hat2_ref, rstd_ref, slope_ref,
    wo_ref, we_ref, wr_ref, sem):
    rows, width = x_ref.shape
    chunks = act_ref.shape[1] // width
    every = pl.ds(0, width)
    piece = [pl.ds(c * width, width) for c in range(chunks)]
    groups = [(0, every, every)]
    for c in range(chunks):
        groups += [(1, every, piece[c]), (2, piece[c], every)]
    wait = weight_copies(groups, (wo_own, we_own, wr_own), (wo_oth, we_oth, wr_oth),
                         (wo_ref, we_ref, wr_ref), sem, sel_ref[0])
    row = lambda i: vec_ref[i:i + 1, :]
    wait(0)
    hidden = x_ref[...].astype(F32) + (nn(att_ref[...], wo_ref[...]) + row(0))
    hat, rstd = norm_forward(hidden)
    hat1_ref[...] = hat
    rstd_ref[:, 0:1] = rstd
    first = hat * row(1) + row(2)
    low = first.astype(BF16)
    first_ref[...] = low
    down = first + row(7)
    for c in range(chunks):
        wait(1 + 2 * c)
        up = nn(low, we_ref[:, piece[c]]) + row(3 + c)
        cdf = 0.5 * (1.0 + erf(up * (2.0 ** -0.5)))
        act = (up * cdf).astype(BF16)
        slope_ref[:, piece[c]] = cdf + up * (jnp.exp(-0.5 * up * up) * 0.3989422804014327)
        act_ref[:, piece[c]] = act
        wait(2 + 2 * c)
        down = down + nn(act, wr_ref[piece[c], :])
    hat, rstd = norm_forward(down)
    hat2_ref[...] = hat
    rstd_ref[:, 1:2] = rstd
    valid = lax.broadcasted_iota(jnp.int32, (rows, width), 0) < sel_ref[1]
    y_ref[...] = jnp.where(valid, hat * row(8) + row(9), 0.0).astype(BF16)


def partner_of(bit):
    me = lax.axis_index("batch")
    side = (me // (1 << bit)) % 2
    return me + (1 - 2 * side) * (1 << bit), side


def place_of(block, order):
    last = len(order) - 1
    return sum(((block >> bit) & 1) << (last - k) for k, bit in enumerate(order))


class Weight:
    def __init__(self, owner, order, by_rows):
        self.owner, self.order, self.by_rows = owner, order, by_rows
        self.bits = len(order)
        self.batch = 1 << self.bits
        self.rest = order[1:] if by_rows else order[1:] + order[:1]
        self.stages = self.bits - 1 if by_rows else self.bits

    def sizes(self, x, y):
        self.block = x[1] // self.batch
        self.run = (1 << self.order[0]) * self.block
        self.runs = self.batch >> (self.order[0] + 1) if self.by_rows else 1
        self.rows, self.depth, self.width = x[0], x[1], y[1]
        self.deep = self.depth // 2 if self.by_rows else self.depth
        self.wide = self.width if self.by_rows else self.width // 2
        self.blocks = self.batch // 2 if self.by_rows else self.batch
        return self

    def scratch(self):
        dma = pltpu.SemaphoreType.DMA
        return [
            pltpu.VMEM((3, self.rows, self.deep), BF16), pltpu.VMEM((3, self.rows, self.wide), BF16),
            pltpu.VMEM((self.blocks, self.block, self.wide), BF16),
            pltpu.VMEM((self.blocks - 1 if self.by_rows else self.blocks - 1, self.block, self.wide), BF16),
            dma((3, self.runs + 1)), dma((3, self.runs + 1)), dma((self.stages,)), dma((self.stages,))]

    def bind(self, x, y, out, scratch):
        self.x, self.y, self.out = x, y, out
        (self.xr, self.yr, self.sums, self.got,
         self.op_send, self.op_recv, self.hop_send, self.hop_recv) = scratch
        return self

    def side(self):
        return partner_of(self.order[0])[1]

    def pieces(self, ref, side, first):
        if first and self.by_rows:
            for r in range(self.runs):
                start = pl.multiple_of(2 * r * self.run + side * self.run, 128)
                yield ref.at[:, pl.ds(start, self.run)], pl.ds(r * self.run, self.run)
        elif first or self.by_rows:
            yield ref, pl.ds(0, ref.shape[1])
        else:
            yield ref.at[:, pl.ds(pl.multiple_of(side * self.wide, 128), self.wide)], pl.ds(0, self.wide)

    def operand(self, slot, away):
        other, side = partner_of(self.order[0])
        target = {"section": self.owner, "batch": other} if away else {"section": self.owner}
        side = 1 - side if away else side
        k = 0
        for first, ref, into in ((True, self.x, self.xr), (False, self.y, self.yr)):
            for source, lanes in self.pieces(ref, side, first):
                yield pltpu.make_async_remote_copy(
                    src_ref=source, dst_ref=into.at[slot, :, lanes],
                    send_sem=self.op_send.at[(0, 2, 1)[slot], k], recv_sem=self.op_recv.at[slot, k],
                    device_id=target, device_id_type=MESH)
                k += 1

    def send_from_owner(self):
        for copy in self.operand(1, True):
            copy.start()

    def send_from_other(self):
        for slot, away in ((0, False), (2, True)):
            for copy in self.operand(slot, away):
                copy.start()

    def sent_from_other(self):
        for slot, away in ((0, False), (2, True)):
            for copy in self.operand(slot, away):
                copy.wait_send()

    def multiply(self):
        for slot, away in ((0, False), (1, True), (2, True)):
            for copy in self.operand(slot, away):
                copy.wait_recv()
        side = self.side()
        rows = self.block * 128 // math.gcd(self.block, 128)
        step = max(s for s in range(128, 1153, 128) if self.wide % s == 0)
        for base in range(0, self.deep, rows):
            if self.by_rows:
                r, inside = base // self.run, base % self.run
                lanes = pl.ds(pl.multiple_of(2 * r * self.run + side * self.run + inside, 128), rows)
            else:
                lanes = pl.ds(base, rows)
            left = cat([self.x[:, lanes]] + [self.xr[s, :, base:base + rows] for s in range(3)], 0)
            for c in range(0, self.wide, step):
                if self.by_rows:
                    near = self.y[:, c:c + step]
                else:
                    near = self.y[:, pl.ds(pl.multiple_of(side * self.wide + c, 128), step)]
                right = cat([near] + [self.yr[s, :, c:c + step] for s in range(3)], 0)
                value = tn(left, right).astype(BF16)
                for j in range(rows // self.block):
                    block = base // self.block + j
                    if self.by_rows:
                        low = 1 << self.order[0]
                        block = block // low * 2 * low + block % low
                    self.sums[place_of(block, self.rest), :, c:c + step] = (
                        value[j * self.block:(j + 1) * self.block])
        self.hop(0).start()

    def spans(self, stage):
        half = self.blocks >> (stage + 1)
        start = 0
        for k in range(stage):
            start = start + partner_of(self.rest[k])[1] * (self.blocks >> (k + 1))
        side = partner_of(self.rest[stage])[1]
        return half, start + side * half, start + (1 - side) * half, self.blocks - 2 * half

    def hop(self, stage):
        half, _, away, landing = self.spans(stage)
        return pltpu.make_async_remote_copy(
            src_ref=self.sums.at[pl.ds(away, half)], dst_ref=self.got.at[pl.ds(landing, half)],
            send_sem=self.hop_send.at[stage], recv_sem=self.hop_recv.at[stage],
            device_id={"batch": partner_of(self.rest[stage])[0]}, device_id_type=MESH)

    def advance(self, stage):
        half, keep, _, landing = self.spans(stage)
        self.hop(stage).wait_recv()
        if self.by_rows or stage + 1 < self.stages:
            if stage + 1 == self.stages:
                self.out[...] = self.sums[keep].astype(F32) + self.got[landing].astype(F32)
                return

            def add(j, carry):
                self.sums[keep + j] = (self.sums[keep + j].astype(F32)
                                       + self.got[landing + j].astype(F32)).astype(BF16)
                return carry

            lax.fori_loop(0, half, add, 0)
            self.hop(stage + 1).start()
        else:
            mine, theirs = self.sums[keep].astype(F32), self.got[landing].astype(F32)
            first = self.side() == 0
            self.out[:, :self.wide] = jnp.where(first, mine, theirs)
            self.out[:, self.wide:] = jnp.where(first, theirs, mine)

    def drain(self):
        for copy in self.operand(1, True):
            copy.wait_send()
        for stage in range(self.stages):
            self.hop(stage).wait_send()


class Small:
    def __init__(self, owner, bits):
        self.owner, self.bits = owner, bits
        self.stages = bits

    def scratch(self, dims):
        dma = pltpu.SemaphoreType.DMA
        return [pltpu.VMEM((self.bits + 1,) + dims, F32), pltpu.VMEM((self.bits + 1,) + dims, F32),
                dma((self.bits + 1,)), dma((self.bits + 1,))]

    def bind(self, x, out, scratch):
        self.x, self.out = x, out
        self.got, self.sums, self.sent, self.came = scratch
        return self

    def arrive(self):
        return pltpu.make_async_remote_copy(
            src_ref=self.x, dst_ref=self.got.at[self.bits], send_sem=self.sent.at[self.bits],
            recv_sem=self.came.at[self.bits], device_id={"section": self.owner}, device_id_type=MESH)

    def hop(self, stage):
        return pltpu.make_async_remote_copy(
            src_ref=self.sums.at[stage], dst_ref=self.got.at[stage], send_sem=self.sent.at[stage],
            recv_sem=self.came.at[stage], device_id={"batch": partner_of(stage)[0]},
            device_id_type=MESH)

    def send_from_owner(self):
        pass

    def send_from_other(self):
        self.arrive().start()

    def sent_from_other(self):
        self.arrive().wait_send()

    def multiply(self):
        self.arrive().wait_recv()
        self.sums[0] = self.x[...] + self.got[self.bits]
        self.hop(0).start()

    def advance(self, stage):
        self.hop(stage).wait_recv()
        self.sums[stage + 1] = self.sums[stage] + self.got[stage]
        if stage + 1 < self.bits:
            self.hop(stage + 1).start()
        else:
            self.out[...] = self.sums[self.bits]

    def drain(self):
        for stage in range(self.bits):
            self.hop(stage).wait_send()


class Stream:
    def __init__(self, groups, slots, own_refs, other_refs, ring, sem):
        self.groups, self.slots = groups, slots
        self.own, self.other, self.ring, self.sem = own_refs, other_refs, ring, sem

    def copy(self, i, refs):
        _, w, row, col = self.groups[i]
        size = self.ring.shape[1]
        source = refs[w].at[pl.ds(row * size, size), pl.ds(col * size, size)]
        slot = i % self.slots
        return pltpu.make_async_copy(source, self.ring.at[slot], self.sem.at[slot])

    def start(self, i):
        if i >= len(self.groups):
            return
        own = lax.axis_index("section") == self.groups[i][0]

        @pl.when(own)
        def _():
            self.copy(i, self.own).start()

        @pl.when(jnp.logical_not(own))
        def _():
            self.copy(i, self.other).start()

    def begin(self):
        for i in range(self.slots):
            self.start(i)

    def take(self, i):
        self.copy(i, self.own).wait()
        return self.ring[i % self.slots]

    def release(self, i):
        self.start(i + self.slots)


def softmax_back(a, da, ones):
    return a * (da - half_sums(a * da, ones))


def attention_backward(
    length, do_ref, gr_ref, kept, newton_ref, newton_copy, dqkv_ref, gi_ref, small_ref, at,
    work, stream, first_group, hook, taps):
    qkv_ref, lm_ref, a1_ref, a2_ref, a3_ref, t_ref, db_ref = kept
    dz_ref, dr_ref, da_ref = work
    rows, width = do_ref.shape
    pairs = width // PAIR
    ones = block_ones()
    eye = pair_eye()
    pool = pool_matrix(length, rows)
    sl = [pl.ds(p * PAIR, PAIR) for p in range(pairs)]
    doh = [do_ref[:, sl[p]].astype(BF16) for p in range(pairs)]
    newton_copy.wait()
    ddh = []
    for p in range(pairs):
        a1 = a1_ref[:, sl[p]].astype(BF16)
        db = pick(tn(a1, doh[p]))
        dbh = db.astype(BF16)
        z = newton_ref[0, NEWTON, :, sl[p]].astype(BF16)
        dz_ref[:, sl[p]] = nt(dbh, spread(db_ref[0, :, sl[p]]))
        dr_ref[:, sl[p]] = jnp.zeros((LM, PAIR), F32)
        ddh.append(pick(tn(z, dbh)).astype(BF16))
    hook(0)

    def newton_back(index, carry):
        step = NEWTON - 1 - index
        keep = []
        for p in range(pairs):
            z = newton_ref[0, step, :, sl[p]]
            zh, zl = split(z)
            dz = dz_ref[:, sl[p]]
            gh, gl = split(dz)
            full = tn(cat([zh, zh, zl], 0), cat([gh, gl, gh], 0))
            df = pick(full + full.T) * 0.5
            keep.append((df, (gh, gl)))
        for p in range(pairs):
            df, g = keep[p]
            r, s, t = [newton_ref[i, step, :, sl[p]] for i in (1, 2, 3)]
            dz_ref[:, sl[p]] = nn3(g, split(eye + r + s + 0.25 * t))
            dr = dr_ref[:, sl[p]]
            dt = 0.25 * df + 0.75 * dr
            rs, ss, dts, drs = split(r), split(s), split(dt), split(0.5 * dr)
            m = nn3(dts, rs) + nn3(drs, ss)
            keep[p] = (df, dts, m, rs, ss)
        for p in range(pairs):
            df, dts, m, rs, ss = keep[p]
            ds = 2.0 * df + (m + pair_transpose(m))
            m = nn3(dts, ss) + nn3(split(ds), rs)
            dr_ref[:, sl[p]] = df + 0.5 * (m + pair_transpose(m))
        return carry

    for half in range(2):
        lax.fori_loop(half * NEWTON // 2, (half + 1) * NEWTON // 2, newton_back, 0)
        hook(1 + half)
    first = lane_is_first(1)
    for p in range(pairs):
        a = a2_ref[:, sl[p]]
        at_ = pair_transpose(a)
        dz = dz_ref[:, sl[p]]
        g = nn3(split(dr_ref[:, sl[p]]), split(a))

        def halves(m):
            c = jnp.sum(m, axis=0, keepdims=True)
            ca = jnp.sum(jnp.where(first, c, 0.0), axis=1, keepdims=True)
            cb = jnp.sum(jnp.where(first, 0.0, c), axis=1, keepdims=True)
            return jnp.where(first, ca, cb)

        inv = 1.0 / halves(a * a)
        dc = halves(dz * at_) - halves(g * a)
        da_ref[:, sl[p]] = inv * (pair_transpose(dz) - 2.0 * g) - (2.0 * dc * inv * inv) * a
    scale = LM ** (-0.25)
    valid = (lax.broadcasted_iota(jnp.int32, (rows, PAIR), 0) < length).astype(F32)
    half = taps // 2
    row = lax.broadcasted_iota(jnp.int32, (rows, rows), 0)
    col = lax.broadcasted_iota(jnp.int32, (rows, rows), 1)
    flip = (row + col == rows - 1).astype(F32).astype(BF16)
    near = (col + row <= rows - 1 + half) & (col + row >= rows - 1 - half)
    per_row = width // rows
    for p in range(pairs):
        q, k, v = [qkv_ref[i, :, sl[p]] for i in range(3)]
        ql, kl = lm_ref[0, :, sl[p]], lm_ref[1, :, sl[p]]
        kld, kd, vd = spread(kl), spread(k), spread(v)
        wide = slice(p * 2 * rows, (p + 1) * 2 * rows)
        ds2 = softmax_back(a2_ref[:, sl[p]], da_ref[:, sl[p]], ones).astype(BF16)
        a1 = a1_ref[:, sl[p]]
        da1 = nt(doh[p], spread(db_ref[1, :, sl[p]]))
        ds1 = softmax_back(a1, da1, ones).astype(BF16)
        a3 = a3_ref[:, wide]
        da3 = nt(ddh[p], vd)
        parts = []
        for j in range(2):
            a, d = a3[:, j * rows:(j + 1) * rows], da3[:, j * rows:(j + 1) * rows]
            parts.append(a * (d - jnp.sum(a * d, axis=1, keepdims=True)))
        ds3 = cat(parts, 1).astype(BF16)
        dv = pick(tn(cat([a3.astype(BF16), t_ref[p]], 0), cat([ddh[p], doh[p]], 0)))
        full = nt(spread(nn(flip, doh[p]).astype(BF16)), v)
        for j in range(2):
            m = jnp.where(near, full[j * rows:(j + 1) * rows], 0.0)
            m = pltpu.roll(m, half + 1, 1, stride=1, stride_axis=0)
            head = 2 * p + j
            line, lane = at + 2 + head // per_row, head % per_row * rows
            small_ref[line:line + 1, lane:lane + rows] = jnp.sum(m, axis=0, keepdims=True)
        dkl = pick(tn(cat([ds1, ds2], 0), cat([q, ql], 0)))
        dql = nn(cat([ds2, ds3], 1), cat([kld, kd], 0))
        dqlh, dqll = split(dql)
        dklh, dkll = split(dkl)
        dq = nn(ds1, kld) + (tn(pool, dqlh) + tn(pool, dqll))
        dk = pick(tn(ds3, ql)) + (tn(pool, dklh) + tn(pool, dkll))
        for i, m in enumerate((dq * scale, dk * scale, dv)):
            low = (m * valid).astype(BF16)
            dqkv_ref[:, pl.ds(i * width + p * PAIR, PAIR)] = low
    for i, line in ((0, at), (2, at + 1)):
        small_ref[line:line + 1, :] = jnp.sum(
            dqkv_ref[:, i * width:(i + 1) * width].astype(F32), axis=0, keepdims=True)
    hook(3)
    total = gr_ref[...]
    for i in range(3):
        total = total + nt(dqkv_ref[:, i * width:(i + 1) * width], stream.take(first_group + i))
        stream.release(first_group + i)
    gi_ref[...] = total.astype(BF16)
    hook(4)


def post_backward(
    length, g, kept, vec_ref, gd_ref, gu_ref, gp_ref, gr_ref, do_ref, sums_ref, stream,
    first_group, hook):
    hat1_ref, hat2_ref, rstd_ref, slope_ref = kept
    rows, width = hat1_ref.shape
    chunks = gu_ref.shape[1] // width
    row = lambda i: vec_ref[i:i + 1, :]

    def total(i, values):
        sums_ref[i:i + 1, :] = jnp.sum(values, axis=0, keepdims=True)

    valid = lax.broadcasted_iota(jnp.int32, (rows, width), 0) < length
    g = jnp.where(valid, g.astype(F32), 0.0)
    hat2 = hat2_ref[...]
    total(8, g * hat2)
    total(9, g)
    second = norm_back(g * row(8), hat2, rstd_ref[:, 1:2])
    gd = second.astype(BF16)
    gd_ref[...] = gd
    total(7, gd.astype(F32))
    grad = second
    for c in range(chunks):
        lanes = slice(c * width, (c + 1) * width)
        gu = (nt(gd, stream.take(first_group + 2 * c)) * slope_ref[:, lanes]).astype(BF16)
        stream.release(first_group + 2 * c)
        gu_ref[:, lanes] = gu
        total(3 + c, gu.astype(F32))
        grad = grad + nt(gu, stream.take(first_group + 2 * c + 1))
        stream.release(first_group + 2 * c + 1)
    hat1 = hat1_ref[...]
    total(1, grad * hat1)
    total(2, grad)
    residual = norm_back(grad * row(1), hat1, rstd_ref[:, 0:1])
    gr_ref[...] = residual
    gp = residual.astype(BF16)
    gp_ref[...] = gp
    total(0, gp.astype(F32))
    do_ref[...] = nt(gp, stream.take(first_group + 2 * chunks))
    stream.release(first_group + 2 * chunks)
    hook()


def post_groups(layer, chunks):
    groups = []
    for c in range(chunks):
        groups += [(layer, 3, c, 0), (layer, 2, 0, c)]
    return groups + [(layer, 1, 0, 0)]


def post_backward_alone(
    length_ref, g_ref, hat1_ref, hat2_ref, rstd_ref, slope_ref, vec_ref, *refs, layer):
    own, other = (None,) + refs[:3], (None,) + refs[3:6]
    gd_ref, gu_ref, gp_ref, gr_ref, do_ref, sums_ref, ring, sem = refs[6:]
    chunks = gu_ref.shape[1] // g_ref.shape[1]
    groups = post_groups(layer, chunks)
    stream = Stream(groups, ring.shape[0], own, other, ring, sem)
    stream.begin()
    post_backward(length_ref[0], g_ref[...], (hat1_ref, hat2_ref, rstd_ref, slope_ref), vec_ref,
                  gd_ref, gu_ref, gp_ref, gr_ref, do_ref, sums_ref, stream, 0, lambda: None)


def greet_all(bits, near):
    barrier = pltpu.get_barrier_semaphore()
    other = 1 - lax.axis_index("section")
    targets = [{"section": other}]
    targets += [{"batch": partner_of(bit)[0]} for bit in range(bits)]
    targets += [{"section": other, "batch": partner_of(bit)[0]} for bit in near]
    for target in targets:
        pl.semaphore_signal(barrier, inc=1, device_id=target, device_id_type=MESH)
    pl.semaphore_wait(barrier, len(targets))


class Take:
    def __init__(self, refs):
        self.refs, self.at = refs, 0

    def __call__(self, count):
        self.at += count
        return self.refs[self.at - count:self.at]


def backward(*refs, plans, littles, taps):
    take = Take(refs)
    (length_ref,) = take(1)
    do2, gr2, sums2 = take(3)
    factors2 = take(7)
    factors1 = take(4)
    kept2, kept1 = take(7), take(7)
    newton2, newton1 = take(2)
    errs = take(2)
    post1, (vec1,) = take(4), take(1)
    own, other = take(4), take(4)
    count = len(plans[0])
    outs = take(count)
    small_out, ig_ref = take(2)
    ring, ring_sem, newton_ref, newton_sem, gi_ref, gi_send, gi_recv = take(7)
    dqkv2, gd1, gu1, gp1, dqkv1, gr1, do1 = take(7)
    work, smalls = take(3), take(2)
    weight_scratch = [take(8) for _ in range(count)]
    small_scratch = take(4)
    length = length_ref[0]
    section = lax.axis_index("section")
    rows, width = do2.shape
    chunks = gu1.shape[1] // width
    at = 6 + chunks
    x2, y2 = factors2[:4], (factors2[4], factors2[5], dqkv2, factors2[6])
    x1, y1 = factors1, (gd1, gu1, dqkv1, gp1)
    items = []
    for layer, xs, ys in ((0, x1, y1), (1, x2, y2)):
        items.append([w.bind(xs[i], ys[i], outs[i], weight_scratch[i])
                      for i, w in enumerate(plans[layer])]
                     + [littles[layer].bind(smalls[layer], small_out, small_scratch)])
    early, late = (0, 1, 3), (2, 4)

    def newton_load(source):
        return pltpu.make_async_copy(source, newton_ref, newton_sem)

    groups = [(1, 0, 0, i) for i in range(3)] + post_groups(0, chunks) + [(0, 0, 0, i) for i in range(3)]
    stream = Stream(groups, ring.shape[0], own, other, ring, ring_sem)
    stream.begin()
    newton_load(newton2).start()
    greet_all(littles[0].bits, sorted({w.order[0] for w in plans[0]}))

    def on(layer, owner_steps, other_steps):
        @pl.when(section == layer)
        def _():
            for item, name, args in owner_steps:
                getattr(items[layer][item], name)(*args)

        @pl.when(section != layer)
        def _():
            for item, name, args in other_steps:
                getattr(items[layer][item], name)(*args)

    def send(layer, which):
        on(layer, [(i, "send_from_owner", ()) for i in which],
           [(i, "send_from_other", ()) for i in which])

    def step(layer, which, name, *args):
        on(layer, [(i, name, args) for i in which if not args or args[0] < items[layer][i].stages], [])

    def share_gradient(layer):
        def copy():
            return pltpu.make_async_remote_copy(
                src_ref=gi_ref.at[layer], dst_ref=ig_ref.at[pl.ds((1 - layer) * rows, rows)],
                send_sem=gi_send.at[layer], recv_sem=gi_recv.at[layer],
                device_id={"section": layer}, device_id_type=MESH)

        @pl.when(section == layer)
        def _():
            ig_ref[layer * rows:(layer + 1) * rows, :] = gi_ref[layer]

        @pl.when(section != layer)
        def _():
            copy().start()
        return copy

    send(1, early)
    smalls[0][...] = jnp.zeros(smalls[0].shape, F32)
    smalls[1][...] = jnp.zeros(smalls[1].shape, F32)
    smalls[1][:at, :] = sums2[...]
    for layer in range(2):
        for i in range(NEWTON):
            smalls[layer][at + 4 + i:at + 5 + i, :] = errs[layer][i]

    def hook2(slot):
        if slot == 3:
            send(1, late)
            newton_load(newton1).start()
            step(1, (3, 0, 1), "multiply")

    def hook1(slot):
        if slot == 1:
            step(1, (3, 0, 1), "advance", 0)
            step(1, (4,), "multiply")
        if slot == 2:
            step(1, (3, 0, 1), "advance", 1)
            step(1, (2,), "multiply")
            step(1, (4,), "advance", 0)
        if slot == 3:
            send(0, late)
            step(0, (3, 0, 1), "multiply")
            step(1, (3, 0, 1), "advance", 2)
            step(1, (4,), "advance", 1)

    attention_backward(
        length, do2, gr2, kept2, newton_ref, newton_load(newton2), dqkv2, gi_ref.at[1], smalls[1],
        at, work, stream, 0, hook2, taps)
    shared2 = share_gradient(1)
    post_backward(length, gi_ref[1], post1, vec1, gd1, gu1, gp1, gr1, do1, smalls[0], stream, 3,
                  lambda: send(0, early))
    attention_backward(
        length, do1, gr1, kept1, newton_ref, newton_load(newton1), dqkv1, gi_ref.at[0], smalls[0],
        at, work, stream, 3 + len(post_groups(0, chunks)), hook1, taps)
    shared1 = share_gradient(0)
    bits = littles[0].bits
    step(1, (2,), "advance", 0)
    step(0, (4,), "multiply")
    step(0, (3, 0, 1), "advance", 0)
    step(1, (4,), "advance", 2)
    step(1, (0, 1, 3), "advance", 3)
    step(0, (2,), "multiply")
    for stage in range(1, bits):
        step(0, (4,), "advance", stage - 1)
        step(0, (3, 0, 1), "advance", stage)
        step(1, (2,), "advance", stage)
        step(0, (2,), "advance", stage - 1)
    step(1, (4,), "advance", bits - 1)
    step(0, (4,), "advance", bits - 1)
    step(0, (2,), "advance", bits - 1)
    for layer in range(2):
        on(layer, [(i, "drain", ()) for i in range(count + 1)],
           [(i, "sent_from_other", ()) for i in range(count + 1)])
    for layer, copy in ((0, shared1), (1, shared2)):
        @pl.when(section == layer)
        def _():
            copy().wait_recv()

        @pl.when(section != layer)
        def _():
            copy().wait_send()


def attention_backward_alone(
    length_ref, do_ref, gr_ref, qkv_ref, lm_ref, a1_ref, a2_ref, a3_ref, t_ref, db_ref, newton_in,
    own, other, dqkv_ref, gi_ref, small_ref, ring, ring_sem, newton_ref, newton_sem, dz_ref, dr_ref,
    da_ref, *, layer, at, taps):
    stream = Stream([(layer, 0, 0, i) for i in range(3)], ring.shape[0], (own,), (other,), ring, ring_sem)
    stream.begin()
    load = pltpu.make_async_copy(newton_in, newton_ref, newton_sem)
    load.start()
    small_ref[...] = jnp.zeros(small_ref.shape, F32)
    attention_backward(
        length_ref[0], do_ref, gr_ref, (qkv_ref, lm_ref, a1_ref, a2_ref, a3_ref, t_ref, db_ref),
        newton_ref, load, dqkv_ref, gi_ref, small_ref, at, (dz_ref, dr_ref, da_ref), stream, 0,
        lambda slot: None, taps)


def shape(dims, kind=F32):
    return jax.ShapeDtypeStruct(dims, kind)


IN_VMEM = pl.BlockSpec(memory_space=pltpu.VMEM)
IN_SMEM = pl.BlockSpec(memory_space=pltpu.SMEM)
ANYWHERE = pl.BlockSpec(memory_space=pl.ANY)
VMEM_LIMIT = 60 * 2 ** 20


def call(kernel, name, ins, outs, scratch, args, flops, moved, collective=None):
    extra = {} if collective is None else dict(collective_id=collective, has_side_effects=True)
    return pl.pallas_call(
        kernel, out_shape=tuple(outs), in_specs=ins, out_specs=(IN_VMEM,) * len(outs),
        scratch_shapes=scratch, name=name,
        cost_estimate=pl.CostEstimate(flops=flops, bytes_accessed=moved, transcendentals=0),
        compiler_params=pltpu.CompilerParams(vmem_limit_bytes=VMEM_LIMIT, **extra))(*args)


def forward_layer(sel, x, weights, others, vec, bias, taps_row, taps):
    rows, width = x.shape
    pairs, heads = width // PAIR, width // LM
    hidden = weights[2].shape[1]
    attended, qkv, lm, a1, a2, a3, band, newton, db, err = call(
        functools.partial(attention_forward, taps=taps), "attention_forward",
        [IN_SMEM] + [IN_VMEM] * 3 + [ANYWHERE] * 2,
        [shape((rows, width), BF16), shape((3, rows, width), BF16), shape((2, LM, width), BF16),
         shape((rows, width)), shape((LM, width)), shape((LM, heads * rows)),
         shape((pairs, rows, 2 * rows), BF16), shape((4, NEWTON + 1, LM, width)),
         shape((2, LM, width), BF16), shape((NEWTON, 1, width))],
        [pltpu.VMEM((width, 3 * width), BF16), pltpu.SemaphoreType.DMA((3,))],
        (sel, x, bias, taps_row, weights[0], others[0]), 10 ** 10, 10 ** 7)
    chunks = hidden // width
    y, first, act, hat1, hat2, rstd, slope = call(
        post_forward, "post_forward",
        [IN_SMEM] + [IN_VMEM] * 3 + [ANYWHERE] * 6,
        [shape((rows, width), BF16), shape((rows, width), BF16), shape((rows, hidden), BF16),
         shape((rows, width)), shape((rows, width)), shape((rows, 128)), shape((rows, hidden))],
        [pltpu.VMEM((width, width), BF16), pltpu.VMEM((width, hidden), BF16),
         pltpu.VMEM((hidden, width), BF16), pltpu.SemaphoreType.DMA((1 + 2 * chunks,))],
        (sel, attended, x, vec) + tuple(weights[1:]) + tuple(others[1:]), 2 * 10 ** 9, 10 ** 7)
    kept = dict(x=x, attended=attended, attention=(qkv, lm, a1, a2, a3, band, db), newton=newton,
                first=first, act=act, post=(hat1, hat2, rstd, slope), err=err)
    return y, kept


def ring_scratch(slots, width):
    return [pltpu.VMEM((slots, width, width), BF16), pltpu.SemaphoreType.DMA((slots,))]


def post_backward_call(layer, length, grad, kept, weights, others, vec):
    rows, width = grad.shape
    hidden = weights[2].shape[1]
    chunks = hidden // width
    return call(
        functools.partial(post_backward_alone, layer=layer), "post_backward",
        [IN_SMEM] + [IN_VMEM] * 6 + [ANYWHERE] * 6,
        [shape((rows, width), BF16), shape((rows, hidden), BF16), shape((rows, width), BF16),
         shape((rows, width)), shape((rows, width)), shape((4 + 2 + chunks, width))],
        ring_scratch(9, width),
        (length, grad) + kept["post"] + (vec,) + tuple(weights[1:]) + tuple(others[1:]),
        2 * 10 ** 9, 10 ** 7)


def plan(owner, bits):
    tail = tuple(range(3, bits))
    return [Weight(owner, (1, 0, 2) + tail, True), Weight(owner, (0, 1, 2) + tail, False),
            Weight(owner, (1, 0, 2) + tail, False), Weight(owner, (2, 1, 0) + tail, False)]


def small_shape(width, hidden, heads):
    rows = 6 + hidden // width + 2 + heads * 128 // width + NEWTON
    return (rows + 7) // 8 * 8, width


def backward_on_slice(length, post2, kept, weights, others, vec, batch, taps):
    gd, gu, gp, residual, d_attended, sums = post2
    bits = batch.bit_length() - 1
    rows, width = d_attended.shape
    hidden, heads = gu.shape[1], width // LM
    plans, littles = [], []
    for layer in range(2):
        xs = [kept[layer][n].shape for n in ("act", "first", "x", "attended")]
        ys = [(rows, n) for n in (width, hidden, 3 * width, width)]
        plans.append([w.sizes(a, b) for w, a, b in zip(plan(layer, bits), xs, ys)])
        littles.append(Small(layer, bits))
    dims = small_shape(width, hidden, heads)
    factors = lambda k: tuple(k[n] for n in ("act", "first", "x", "attended"))
    args = ((length, d_attended, residual, sums) + factors(kept[1]) + (gd, gu, gp)
            + factors(kept[0]) + kept[1]["attention"] + kept[0]["attention"]
            + (kept[1]["newton"], kept[0]["newton"], kept[0]["err"], kept[1]["err"])
            + kept[0]["post"] + (vec,) + tuple(weights) + tuple(others))
    ins = ([IN_SMEM] + [IN_VMEM] * 28 + [ANYWHERE] * 2 + [IN_VMEM] * 7 + [ANYWHERE] * 8)
    outs = [shape((w.block, w.width)) for w in plans[0]] + [shape(dims), shape((2 * rows, width), BF16)]
    dma = pltpu.SemaphoreType.DMA
    low = lambda n: pltpu.VMEM((rows, n), BF16)
    wide = lambda n: pltpu.VMEM((rows, n), F32)
    scratch = ring_scratch(6, width) + [
        pltpu.VMEM(kept[0]["newton"].shape, F32), dma(()), pltpu.VMEM((2, rows, width), BF16),
        dma((2,)), dma((2,)), low(3 * width), low(width), low(hidden), low(width), low(3 * width),
        wide(width), wide(width)]
    scratch += [pltpu.VMEM((LM, width), F32)] * 3 + [pltpu.VMEM(dims, F32)] * 2
    scratch += [s for w in plans[0] for s in w.scratch()] + littles[0].scratch(dims)
    return call(
        functools.partial(backward, plans=plans, littles=littles, taps=taps), "backward",
        ins, outs, scratch, args, 3 * 10 ** 10, 5 * 10 ** 7, collective=0)


def backward_apart(length, post2, kept, weights, others, vecs, taps):
    post, grads, shares = post2, [None, None], [None, None]
    grad = None
    for layer in (1, 0):
        if layer == 0:
            post = post_backward_call(0, length, grads[1], kept[0], weights, others, vecs[0])
        gd, gu, gp, residual, d_attended, sums = post
        rows, width = d_attended.shape
        hidden = gu.shape[1]
        dims = small_shape(width, hidden, width // LM)
        at = sums.shape[0]
        dqkv, grads[layer], small = call(
            functools.partial(attention_backward_alone, layer=layer, at=at, taps=taps),
            "attention_backward", [IN_SMEM] + [IN_VMEM] * 9 + [ANYWHERE] * 3,
            [shape((rows, 3 * width), BF16), shape((rows, width), BF16), shape(dims)],
            ring_scratch(3, width) + [pltpu.VMEM(kept[layer]["newton"].shape, F32),
                                      pltpu.SemaphoreType.DMA(())]
            + [pltpu.VMEM((LM, width), F32)] * 3,
            (length, d_attended, residual) + kept[layer]["attention"]
            + (kept[layer]["newton"], weights[0], others[0]), 10 ** 10, 10 ** 7)
        errs = kept[layer]["err"].reshape(NEWTON, width)
        end = at + 2 + width // LM * 128 // width
        small = small.at[:at].set(sums).at[end:end + NEWTON].set(errs)
        xs = [kept[layer][n] for n in ("act", "first", "x", "attended")]
        products = [lax.dot_general(x, y, (((0,), (0,)), ((), ())), preferred_element_type=F32)
                    for x, y in zip(xs, (gd, gu, dqkv, gp))]
        shares[layer] = [
            lax.psum_scatter(lax.psum(p, "section"), "batch", scatter_dimension=0, tiled=True)
            for p in products] + [lax.psum(small, ("section", "batch"))]
    lead = lax.axis_index("section") == 0
    crossed = swap(jnp.where(lead, grads[1], grads[0]))
    together = jnp.where(
        lead, jnp.concatenate([grads[0], crossed]), jnp.concatenate([crossed, grads[1]]))
    return [jnp.where(lead, a, b) for a, b in zip(*shares)] + [together]


def swap(value):
    return lax.ppermute(value, "section", [(0, 1), (1, 0)])


def body(
    layer_input, seq_lengths, cotangent, project_weight, project_bias, conv_kernel, output_weight,
    output_bias, attn_gain, attn_shift, expand_weight, expand_bias, reduce_weight, reduce_bias,
    final_gain, final_shift):
    section = lax.axis_index("section")
    batch = lax.axis_size("batch")
    lead = section == 0
    total, width = layer_input.shape
    rows = total // seq_lengths.shape[0]
    heads, taps = conv_kernel.shape[1:]
    weights = (project_weight[0], output_weight[0], expand_weight[0], reduce_weight[0])
    others = tuple(swap(w) for w in weights)
    tap_rows = jnp.pad(conv_kernel[0], ((0, 0), (0, 128 - taps)))
    pieces = [output_bias, attn_gain, attn_shift, expand_bias.reshape(-1, width), reduce_bias,
              final_gain, final_shift, project_bias.reshape(2, width),
              tap_rows.reshape(-1, width)]
    vec = jnp.concatenate(pieces, axis=0)
    vec_other = swap(vec)
    length = lax.dynamic_index_in_dim(seq_lengths, section, keepdims=False)
    own_rows = lambda v: lax.dynamic_slice_in_dim(v, section * rows, rows, 0)
    sels, vecs, biases, tap_list = [], [], [], []
    for layer in range(2):
        here = section == layer
        sels.append(jnp.stack([here.astype(jnp.int32), length]))
        v = jnp.where(here, vec, vec_other)
        vecs.append(v)
        biases.append(jnp.stack([v[10], jnp.zeros_like(v[10]), v[11]]))
        t = v[12:].reshape(heads, 128)
        tap_list.append(jnp.pad(t, ((0, 16 - heads), (0, 0))))
    value = own_rows(layer_input)
    outputs, kept = [], []
    for layer in range(2):
        value, saved = forward_layer(
            sels[layer], value, weights, others, vecs[layer], biases[layer], tap_list[layer], taps)
        outputs.append(value)
        kept.append(saved)
    crossed = swap(jnp.where(lead, outputs[1], outputs[0]))
    activations = jnp.where(
        lead, jnp.concatenate([outputs[0], crossed]), jnp.concatenate([crossed, outputs[1]]))
    length = length[None]
    post2 = post_backward_call(1, length, own_rows(cotangent), kept[1], weights, others, vecs[1])
    blocks = [w.shape[0] // batch for w in weights]
    if batch >= 8 and all(b % 16 == 0 for b in blocks):
        result = backward_on_slice(length, post2, kept, weights, others, vecs[0], batch, taps)
    else:
        result = backward_apart(length, post2, kept, weights, others, vecs, taps)
    g_red, g_exp, g_qkv, g_out, small, input_grads = result
    index = lax.axis_index("batch")

    def share(first, many):
        flat = small[first:first + many].reshape(-1)
        size = flat.shape[0] // batch
        return lax.dynamic_slice_in_dim(flat, index * size, size, 0)[None]

    chunks = reduce_weight.shape[1] // width
    at = 6 + chunks
    end = at + 2 + heads * 128 // width
    dtaps = small[at + 2:end].reshape(heads, 128)[:, :taps]
    proxies = jnp.sum(small[end:end + NEWTON], axis=1)
    return (
        activations[None], input_grads[None], g_qkv[None], share(at, 2), dtaps[None], g_out[None],
        share(0, 1), share(1, 1), share(2, 1), g_exp[None], share(3, chunks), g_red[None],
        share(3 + chunks, 1), share(4 + chunks, 1), share(5 + chunks, 1), proxies[None])


def solution(mesh):
    split_rows = P("batch", None)
    two, three = P("section", None), P("section", None, None)
    return jax.shard_map(
        body, mesh=mesh,
        in_specs=(split_rows, P("batch"), split_rows, three, two, three, three, two, two, two,
                  three, two, three, two, two, two),
        out_specs=(P("section", "batch", None), P("section", "batch", None),
                   P("section", "batch", None), P("section", "batch"), three,
                   P("section", "batch", None), P("section", "batch"), P("section", "batch"),
                   P("section", "batch"), P("section", "batch", None), P("section", "batch"),
                   P("section", "batch", None), P("section", "batch"), P("section", "batch"),
                   P("section", "batch"), two),
        check_vma=False)
```

```python
import functools
import math

import jax
import jax.numpy as jnp
from jax import lax
from jax.experimental import pallas as pl
from jax.experimental.pallas import tpu as pltpu
from jax.sharding import PartitionSpec as P

F32 = jnp.float32
BF16 = jnp.bfloat16
NEWTON = 6
LM = 64
PAIR = 128
EPS = 1e-05
MESH = pl.DeviceIdType.MESH
QKV, OUT, EXPAND, REDUCE = range(4)


def nn(a, b):
    return lax.dot_general(a, b, (((1,), (0,)), ((), ())), preferred_element_type=F32)


def nt(a, b):
    return lax.dot_general(a, b, (((1,), (1,)), ((), ())), preferred_element_type=F32)


def tn(a, b):
    return lax.dot_general(a, b, (((0,), (0,)), ((), ())), preferred_element_type=F32)


def split(x):
    high = x.astype(BF16)
    return high, (x - high.astype(F32)).astype(BF16)


def cat(parts, axis):
    return jnp.concatenate(parts, axis=axis)


def lane_is_first(rows, width=PAIR):
    return lax.broadcasted_iota(jnp.int32, (rows, width), 1) < width // 2


def spread(y):
    rows = y.shape[0]
    keep = lane_is_first(rows).astype(F32).astype(y.dtype)
    return cat([y * keep, y * (1 - keep)], 0)


def pick(x):
    rows = x.shape[0] // 2
    return jnp.where(lane_is_first(rows), x[:rows], x[rows:])


def nn3(xs, ys):
    (xh, xl), (yh, yl) = xs, ys
    dh, dl = spread(yh), spread(yl)
    return nn(cat([xh, xl], 1), cat([dh, dh], 0)) + nn(xh, dl)


def nt3(xs, ds):
    (xh, xl), (dh, dl) = xs, ds
    return nt(cat([xh, xl], 1), cat([dh, dh], 1)) + nt(xh, dl)


def half_sums(x, ones):
    high, low = split(x)
    return nn(high, ones) + nn(low, ones)


def block_ones():
    row = lax.broadcasted_iota(jnp.int32, (PAIR, PAIR), 0) < LM
    col = lax.broadcasted_iota(jnp.int32, (PAIR, PAIR), 1) < LM
    return (row == col).astype(F32).astype(BF16)


def pair_softmax(scores, ones):
    first = lane_is_first(scores.shape[0])
    top_a = jnp.max(jnp.where(first, scores, -jnp.inf), axis=1, keepdims=True)
    top_b = jnp.max(jnp.where(first, -jnp.inf, scores), axis=1, keepdims=True)
    e = jnp.exp(scores - jnp.where(first, top_a, top_b))
    return e / half_sums(e, ones)


def pair_transpose(x):
    t = x.T
    return cat([t[:LM], t[LM:]], 1)


def pair_eye():
    row = lax.broadcasted_iota(jnp.int32, (LM, PAIR), 0)
    col = lax.broadcasted_iota(jnp.int32, (LM, PAIR), 1)
    return (row == col % LM).astype(F32)


def pool_matrix(length, rows):
    landmark = lax.broadcasted_iota(jnp.int32, (LM, rows), 0)
    row = lax.broadcasted_iota(jnp.int32, (LM, rows), 1)
    segment = length // LM
    inside = (row >= landmark * segment) & (row < (landmark + 1) * segment)
    weight = 1.0 / jnp.full((LM, rows), segment, jnp.int32).astype(F32)
    return jnp.where(inside, weight, 0.0).astype(BF16)


def toeplitz(taps_row, rows, taps):
    half = taps // 2
    wide = jnp.broadcast_to(taps_row, (rows, rows))
    wide = pltpu.roll(wide, rows - half, 1, stride=1, stride_axis=0)
    row = lax.broadcasted_iota(jnp.int32, (rows, rows), 0)
    col = lax.broadcasted_iota(jnp.int32, (rows, rows), 1)
    near = (col - row <= half) & (row - col <= half)
    return jnp.where(near, wide, 0.0)


def attention_forward(length, x, bias, taps_ref, kept, err_at, stream, group, hook, taps):
    rows, width = x.shape
    pairs = width // PAIR
    z_ref, r_ref, s_ref, t_ref = kept["z"], kept["r"], kept["s"], kept["t"]
    a1_ref, a2_ref, a3_ref, band_ref = kept["a1"], kept["a2"], kept["a3"], kept["band"]
    qkv_ref, lm_ref, db_ref = kept["qkv"], kept["lm"], kept["db"]
    ones = block_ones()
    pool = pool_matrix(length, rows)
    eye = pair_eye()
    sl = [pl.ds(p * PAIR, PAIR) for p in range(pairs)]
    valid = (lax.broadcasted_iota(jnp.int32, (rows, width), 0) < length).astype(F32)
    scale = LM ** (-0.25)
    qkv = []
    for i in range(3):
        y = nn(x, stream.take(group + i))
        if bias[i] is not None:
            y = y + bias[i]
        qkv.append(y * (valid * scale if i < 2 else valid))
        stream.release(group + i)
    q, k, v = [[m[:, p * PAIR:(p + 1) * PAIR] for p in range(pairs)] for m in qkv]
    qs = [split(m) for m in q]
    ks = [split(m) for m in k]
    vs = [split(m) for m in v]
    for i, ms in enumerate((qs, ks, vs)):
        for p in range(pairs):
            qkv_ref[i, :, sl[p]] = ms[p][0]
    qls = [split(nn(pool, h) + nn(pool, l)) for h, l in qs]
    kls = [split(nn(pool, h) + nn(pool, l)) for h, l in ks]
    for p in range(pairs):
        lm_ref[0, :, sl[p]] = qls[p][0]
        lm_ref[1, :, sl[p]] = kls[p][0]
    kld = [(spread(h), spread(l)) for h, l in kls]
    for p in range(pairs):
        a2_ref[:, sl[p]] = pair_softmax(nt3(qls[p], kld[p]), ones)
    first = lane_is_first(LM)
    for p in range(pairs):
        a = a2_ref[:, sl[p]]
        squares = jnp.sum(a * a, axis=0, keepdims=True)
        fro_a = jnp.sum(jnp.where(first[:1], squares, 0.0), axis=1, keepdims=True)
        fro_b = jnp.sum(jnp.where(first[:1], 0.0, squares), axis=1, keepdims=True)
        z_ref[0, :, sl[p]] = pair_transpose(a) / jnp.where(first[:1], fro_a, fro_b)
    for p in range(pairs):
        z = split(z_ref[0, :, sl[p]])
        r_ref[0, :, sl[p]] = eye - nn3(split(a2_ref[:, sl[p]]), z)
    hook(0)
    small_ref, line, err_ref = err_at

    def newton_step(step, carry):
        s_all, t_all = [], []
        for p in range(pairs):
            r = r_ref[step, :, sl[p]]
            rs = split(r)
            s = nn3(rs, rs)
            s_ref[step, :, sl[p]] = s
            s_all.append((r, rs, s))
        for p in range(pairs):
            r, rs, s = s_all[p]
            t = nn3(split(s), rs)
            t_ref[step, :, sl[p]] = t
            t_all.append(eye + r + s + 0.25 * t)
        for p in range(pairs):
            zn = nn3(split(z_ref[step, :, sl[p]]), split(t_all[p]))
            z_ref[step + 1, :, sl[p]] = zn
            rn = eye - nn3(split(a2_ref[:, sl[p]]), split(zn))
            r_ref[step + 1, :, sl[p]] = rn
            err_ref[step, :, sl[p]] = jnp.sum(rn * rn, axis=0, keepdims=True)
        return carry

    lax.fori_loop(0, NEWTON, newton_step, 0)
    for i in range(NEWTON):
        small_ref[line + i:line + i + 1, :] = err_ref[i]
    hook(1)
    for p in range(pairs):
        wide = slice(p * 2 * rows, (p + 1) * 2 * rows)
        score = nt3(qls[p], (spread(ks[p][0]), spread(ks[p][1])))
        key = lax.broadcasted_iota(jnp.int32, (LM, rows), 1)
        halves = []
        for j in range(2):
            sc = jnp.where(key < length, score[:, j * rows:(j + 1) * rows], -1e30)
            e = jnp.exp(sc - jnp.max(sc, axis=1, keepdims=True))
            halves.append(e / jnp.sum(e, axis=1, keepdims=True))
        a3 = cat(halves, 1)
        a3_ref[:, wide] = a3
        a3h, a3l = split(a3)
        vh, vl = spread(vs[p][0]), spread(vs[p][1])
        d = nn(a3h, vh) + (nn(a3l, vh) + nn(a3h, vl))
        z = split(z_ref[NEWTON, :, sl[p]])
        ds = split(d)
        b = nn3(z, ds)
        bs = split(b)
        db_ref[0, :, sl[p]] = ds[0]
        db_ref[1, :, sl[p]] = bs[0]
        a1 = pair_softmax(nt3(qs[p], kld[p]), ones)
        a1_ref[:, sl[p]] = a1
        band = cat([toeplitz(taps_ref[2 * p + j:2 * p + j + 1, :], rows, taps) for j in range(2)], 1)
        th, tl = split(band)
        band_ref[p] = th
        o = nn3(split(a1), bs) + nn(cat([th, tl], 1), cat([vh, vh], 0)) + nn(th, vl)
        kept["att"][:, sl[p]] = o.astype(BF16)
    hook(2)


def norm_forward(values):
    center = values - jnp.mean(values, axis=1, keepdims=True)
    rstd = lax.rsqrt(jnp.mean(center * center, axis=1, keepdims=True) + EPS)
    return center * rstd, rstd


def norm_back(grad, hat, rstd):
    mean = jnp.mean(grad, axis=1, keepdims=True)
    slope = jnp.mean(grad * hat, axis=1, keepdims=True)
    return rstd * (grad - mean - hat * slope)


def post_forward(length, x, vec, kept, stream, group):
    rows, width = x.shape
    chunks = kept["act"].shape[1] // width
    row = lambda i: vec[i:i + 1, :]
    hidden = x.astype(F32) + (nn(kept["att"][...], stream.take(group)) + row(0))
    stream.release(group)
    hat, rstd = norm_forward(hidden)
    kept["hat1"][...] = hat
    kept["rstd"][:, 0:1] = rstd
    first = hat * row(1) + row(2)
    low = first.astype(BF16)
    kept["first"][...] = low
    down = first + row(3 + chunks)
    for c in range(chunks):
        lanes = slice(c * width, (c + 1) * width)
        up = nn(low, stream.take(group + 1 + 2 * c)) + row(3 + c)
        stream.release(group + 1 + 2 * c)
        cdf = 0.5 * (1.0 + lax.erf(up * (2.0 ** -0.5)))
        act = (up * cdf).astype(BF16)
        slope = cdf + up * (jnp.exp(-0.5 * up * up) * 0.3989422804014327)
        kept["slope"][:, lanes] = slope.astype(kept["slope"].dtype)
        kept["act"][:, lanes] = act
        down = down + nn(act, stream.take(group + 2 + 2 * c))
        stream.release(group + 2 + 2 * c)
    hat, rstd = norm_forward(down)
    kept["hat2"][...] = hat
    kept["rstd"][:, 1:2] = rstd
    valid = lax.broadcasted_iota(jnp.int32, (rows, width), 0) < length
    return jnp.where(valid, hat * row(4 + chunks) + row(5 + chunks), 0.0).astype(BF16)


def softmax_back(a, da, ones):
    return a * (da - half_sums(a * da, ones))


def attention_backward(
    length, do_ref, gr_ref, kept, dqkv_ref, small_ref, at, work, stream, group, hook, taps):
    dz_ref, dr_ref, da_ref = work
    a1_ref, a2_ref, a3_ref, band_ref = kept["a1"], kept["a2"], kept["a3"], kept["band"]
    qkv_ref, lm_ref, db_ref = kept["qkv"], kept["lm"], kept["db"]
    rows, width = do_ref.shape
    pairs = width // PAIR
    ones = block_ones()
    eye = pair_eye()
    pool = pool_matrix(length, rows)
    sl = [pl.ds(p * PAIR, PAIR) for p in range(pairs)]
    doh = [do_ref[:, sl[p]].astype(BF16) for p in range(pairs)]
    ddh = []
    for p in range(pairs):
        a1 = a1_ref[:, sl[p]].astype(BF16)
        db = pick(tn(a1, doh[p]))
        dbh = db.astype(BF16)
        z = kept["z"][NEWTON, :, sl[p]].astype(BF16)
        dz_ref[:, sl[p]] = nt(dbh, spread(db_ref[0, :, sl[p]]))
        dr_ref[:, sl[p]] = jnp.zeros((LM, PAIR), F32)
        ddh.append(pick(tn(z, dbh)).astype(BF16))
    hook(0)

    def newton_back(index, carry):
        step = NEWTON - 1 - index
        keep = []
        for p in range(pairs):
            z = kept["z"][step, :, sl[p]]
            zh, zl = split(z)
            dz = dz_ref[:, sl[p]]
            gh, gl = split(dz)
            full = tn(cat([zh, zh, zl], 0), cat([gh, gl, gh], 0))
            df = pick(full + full.T) * 0.5
            keep.append((df, (gh, gl)))
        for p in range(pairs):
            df, g = keep[p]
            r, s, t = [kept[n][step, :, sl[p]] for n in ("r", "s", "t")]
            dz_ref[:, sl[p]] = nn3(g, split(eye + r + s + 0.25 * t))
            dr = dr_ref[:, sl[p]]
            dt = 0.25 * df + 0.75 * dr
            rs, ss, dts, drs = split(r), split(s), split(dt), split(0.5 * dr)
            m = nn3(dts, rs) + nn3(drs, ss)
            keep[p] = (df, dts, m, rs, ss)
        for p in range(pairs):
            df, dts, m, rs, ss = keep[p]
            ds = 2.0 * df + (m + pair_transpose(m))
            m = nn3(dts, ss) + nn3(split(ds), rs)
            dr_ref[:, sl[p]] = df + 0.5 * (m + pair_transpose(m))
        return carry

    for third in range(3):
        lax.fori_loop(third * NEWTON // 3, (third + 1) * NEWTON // 3, newton_back, 0)
        hook(1 + third)
    first = lane_is_first(1)
    for p in range(pairs):
        a = a2_ref[:, sl[p]]
        turned = pair_transpose(a)
        dz = dz_ref[:, sl[p]]
        g = nn3(split(dr_ref[:, sl[p]]), split(a))

        def halves(m):
            c = jnp.sum(m, axis=0, keepdims=True)
            ca = jnp.sum(jnp.where(first, c, 0.0), axis=1, keepdims=True)
            cb = jnp.sum(jnp.where(first, 0.0, c), axis=1, keepdims=True)
            return jnp.where(first, ca, cb)

        inv = 1.0 / halves(a * a)
        dc = halves(dz * turned) - halves(g * a)
        da_ref[:, sl[p]] = inv * (pair_transpose(dz) - 2.0 * g) - (2.0 * dc * inv * inv) * a
    scale = LM ** (-0.25)
    valid = (lax.broadcasted_iota(jnp.int32, (rows, PAIR), 0) < length).astype(F32)
    half = taps // 2
    row = lax.broadcasted_iota(jnp.int32, (rows, rows), 0)
    col = lax.broadcasted_iota(jnp.int32, (rows, rows), 1)
    flip = (row + col == rows - 1).astype(F32).astype(BF16)
    near = (col + row <= rows - 1 + half) & (col + row >= rows - 1 - half)
    per_row = width // rows
    for p in range(pairs):
        q, k, v = [qkv_ref[i, :, sl[p]] for i in range(3)]
        ql, kl = lm_ref[0, :, sl[p]], lm_ref[1, :, sl[p]]
        kld, kd, vd = spread(kl), spread(k), spread(v)
        wide = slice(p * 2 * rows, (p + 1) * 2 * rows)
        ds2 = softmax_back(a2_ref[:, sl[p]], da_ref[:, sl[p]], ones).astype(BF16)
        a1 = a1_ref[:, sl[p]]
        da1 = nt(doh[p], spread(db_ref[1, :, sl[p]]))
        ds1 = softmax_back(a1, da1, ones).astype(BF16)
        a3 = a3_ref[:, wide]
        da3 = nt(ddh[p], vd)
        parts = []
        for j in range(2):
            a, d = a3[:, j * rows:(j + 1) * rows], da3[:, j * rows:(j + 1) * rows]
            parts.append(a * (d - jnp.sum(a * d, axis=1, keepdims=True)))
        ds3 = cat(parts, 1).astype(BF16)
        dv = pick(tn(cat([a3.astype(BF16), band_ref[p]], 0), cat([ddh[p], doh[p]], 0)))
        full = nt(spread(nn(flip, doh[p]).astype(BF16)), v)
        for j in range(2):
            m = jnp.where(near, full[j * rows:(j + 1) * rows], 0.0)
            m = pltpu.roll(m, half + 1, 1, stride=1, stride_axis=0)
            head = 2 * p + j
            line, lane = at + 2 + head // per_row, head % per_row * rows
            small_ref[line:line + 1, lane:lane + rows] = jnp.sum(m, axis=0, keepdims=True)
        dkl = pick(tn(cat([ds1, ds2], 0), cat([q, ql], 0)))
        dql = nn(cat([ds2, ds3], 1), cat([kld, kd], 0))
        dqlh, dqll = split(dql)
        dklh, dkll = split(dkl)
        dq = nn(ds1, kld) + (tn(pool, dqlh) + tn(pool, dqll))
        dk = pick(tn(ds3, ql)) + (tn(pool, dklh) + tn(pool, dkll))
        for i, m in enumerate((dq * scale, dk * scale, dv)):
            low = (m * valid).astype(BF16)
            dqkv_ref[:, pl.ds(i * width + p * PAIR, PAIR)] = low
    for i, line in ((0, at), (2, at + 1)):
        small_ref[line:line + 1, :] = jnp.sum(
            dqkv_ref[:, i * width:(i + 1) * width].astype(F32), axis=0, keepdims=True)
    hook(4)
    total = gr_ref[...]
    for i in range(3):
        total = total + nt(dqkv_ref[:, i * width:(i + 1) * width], stream.take(group + i))
        stream.release(group + i)
    return total.astype(BF16)


def post_backward(length, g, kept, vec, ys, gr_ref, do_ref, sums_ref, stream, group, hook):
    gd_ref, gu_ref, gp_ref = ys
    rows, width = g.shape
    chunks = gu_ref.shape[1] // width
    row = lambda i: vec[i:i + 1, :]

    def total(i, values):
        sums_ref[i:i + 1, :] = jnp.sum(values, axis=0, keepdims=True)

    valid = lax.broadcasted_iota(jnp.int32, (rows, width), 0) < length
    g = jnp.where(valid, g.astype(F32), 0.0)
    hat2 = kept["hat2"][...]
    total(4 + chunks, g * hat2)
    total(5 + chunks, g)
    second = norm_back(g * row(4 + chunks), hat2, kept["rstd"][:, 1:2])
    gd = second.astype(BF16)
    gd_ref[...] = gd
    hook(0)
    total(3 + chunks, gd.astype(F32))
    grad = second
    for c in range(chunks):
        lanes = slice(c * width, (c + 1) * width)
        gu = nt(gd, stream.take(group + 2 * c)) * kept["slope"][:, lanes].astype(F32)
        gu = gu.astype(BF16)
        stream.release(group + 2 * c)
        gu_ref[:, lanes] = gu
        total(3 + c, gu.astype(F32))
        grad = grad + nt(gu, stream.take(group + 2 * c + 1))
        stream.release(group + 2 * c + 1)
    hook(1)
    hat1 = kept["hat1"][...]
    total(1, grad * hat1)
    total(2, grad)
    residual = norm_back(grad * row(1), hat1, kept["rstd"][:, 0:1])
    gr_ref[...] = residual
    gp = residual.astype(BF16)
    gp_ref[...] = gp
    hook(2)
    total(0, gp.astype(F32))
    do_ref[...] = nt(gp, stream.take(group + 2 * chunks))
    stream.release(group + 2 * chunks)


class Stream:
    def __init__(self, groups, own, other, ring, sem, arrived):
        self.groups, self.own, self.other = groups, own, other
        self.ring, self.sem, self.arrived = ring, sem, arrived
        self.slots, self.cursor, self.free, self.flowing = ring.shape[0], 0, 0, False
        self.seen = set()

    def copy(self, i, refs):
        _, w, row, col = self.groups[i]
        size = self.ring.shape[1]
        source = refs[w].at[pl.ds(row * size, size), pl.ds(col * size, size)]
        slot = i % self.slots
        return pltpu.make_async_copy(source, self.ring.at[slot], self.sem.at[slot])

    def start(self, until):
        while self.cursor < min(until, len(self.groups)):
            i = self.cursor
            own = lax.axis_index("section") == self.groups[i][0]
            fresh = self.groups[i] not in self.seen
            self.seen.add(self.groups[i])

            @pl.when(own)
            def _():
                self.copy(i, self.own).start()

            @pl.when(jnp.logical_not(own))
            def _():
                if fresh:
                    self.arrived(self.groups[i])
                self.copy(i, self.other).start()

            self.cursor += 1

    def flow(self):
        self.flowing = True
        self.start(self.free + self.slots)

    def take(self, i):
        self.start(i + 1)
        self.copy(i, self.own).wait()
        return self.ring[i % self.slots]

    def release(self, i):
        self.free = i + 1
        if self.flowing:
            self.start(self.free + self.slots)


def forward_groups(layer, chunks):
    groups = [(layer, QKV, 0, i) for i in range(3)] + [(layer, OUT, 0, 0)]
    for c in range(chunks):
        groups += [(layer, EXPAND, 0, c), (layer, REDUCE, c, 0)]
    return groups


def backward_groups(layer, chunks):
    groups = []
    for c in range(chunks):
        groups += [(layer, REDUCE, c, 0), (layer, EXPAND, 0, c)]
    return groups + [(layer, OUT, 0, 0)] + [(layer, QKV, 0, i) for i in range(3)]


def partner_of(bit):
    me = lax.axis_index("batch")
    side = (me // (1 << bit)) % 2
    return me + (1 - 2 * side) * (1 << bit), side


def place_of(block, order):
    last = len(order) - 1
    return sum(((block >> bit) & 1) << (last - k) for k, bit in enumerate(order))


class Weight:
    def __init__(self, owner, order, by_rows, parts):
        self.owner, self.order, self.by_rows, self.parts = owner, order, by_rows, parts
        self.bits = len(order)
        self.batch = 1 << self.bits
        self.rest = order[1:] if by_rows else order[1:] + order[:1]
        self.stages = len(self.rest)

    def sizes(self, x, y):
        self.block = x[1] // self.batch
        self.run = (1 << self.order[0]) * self.block
        self.runs = self.batch >> (self.order[0] + 1) if self.by_rows else 1
        self.rows, self.depth, self.width = x[0], x[1], y[1]
        self.deep = self.depth // 2 if self.by_rows else self.depth
        self.wide = self.width if self.by_rows else self.width // 2
        self.blocks = self.batch // 2 if self.by_rows else self.batch
        self.step = self.wide // self.parts
        return self

    def scratch(self):
        dma = pltpu.SemaphoreType.DMA
        return [
            pltpu.VMEM((3, self.rows, self.deep), BF16), pltpu.VMEM((3, self.rows, self.wide), BF16),
            pltpu.VMEM((self.blocks, self.block, self.wide), BF16),
            pltpu.VMEM((self.blocks - 1, self.block, self.wide), BF16),
            dma((3, self.runs)), dma((3, self.runs)), dma((3, self.parts)), dma((3, self.parts)),
            dma((self.stages, self.parts)), dma((self.stages, self.parts))]

    def bind(self, x, y, out, scratch):
        self.x, self.y, self.out = x, y, out
        (self.xr, self.yr, self.sums, self.got, self.x_sent, self.x_came, self.y_sent, self.y_came,
         self.hop_sent, self.hop_came) = scratch
        return self

    def side(self):
        return partner_of(self.order[0])[1]

    def towards(self, slot):
        other, side = partner_of(self.order[0])
        if slot == 0:
            return {"section": self.owner}, side
        return {"section": self.owner, "batch": other}, 1 - side

    def x_copies(self, slot):
        target, side = self.towards(slot)
        for r in range(self.runs):
            if self.by_rows:
                start = pl.multiple_of(2 * r * self.run + side * self.run, 128)
                source, into = self.x.at[:, pl.ds(start, self.run)], pl.ds(r * self.run, self.run)
                into = self.xr.at[slot, :, into]
            else:
                source, into = self.x, self.xr.at[slot]
            yield pltpu.make_async_remote_copy(
                src_ref=source, dst_ref=into, send_sem=self.x_sent.at[slot, r],
                recv_sem=self.x_came.at[slot, r], device_id=target, device_id_type=MESH)

    def y_copy(self, slot, part):
        target, side = self.towards(slot)
        lanes = pl.ds(part * self.step, self.step)
        if self.by_rows:
            source = self.y.at[:, lanes]
        else:
            start = pl.multiple_of(side * self.wide + part * self.step, 128)
            source = self.y.at[:, pl.ds(start, self.step)]
        return pltpu.make_async_remote_copy(
            src_ref=source, dst_ref=self.yr.at[slot, :, lanes], send_sem=self.y_sent.at[slot, part],
            recv_sem=self.y_came.at[slot, part], device_id=target, device_id_type=MESH)

    def send_x(self, slots):
        for slot in slots:
            for copy in self.x_copies(slot):
                copy.start()

    def send_y(self, slots):
        for part in range(self.parts):
            for slot in slots:
                self.y_copy(slot, part).start()

    def drain_factors(self, slots):
        for slot in slots:
            for copy in self.x_copies(slot):
                copy.wait_send()
            for part in range(self.parts):
                self.y_copy(slot, part).wait_send()

    def multiply(self, part):
        if part == 0:
            for slot in range(3):
                for copy in self.x_copies(slot):
                    copy.wait_recv()
        for slot in range(3):
            self.y_copy(slot, part).wait_recv()
        side = self.side()
        lanes = slice(part * self.step, (part + 1) * self.step)
        if self.by_rows:
            near = self.y[:, lanes]
        else:
            start = pl.multiple_of(side * self.wide + part * self.step, 128)
            near = self.y[:, pl.ds(start, self.step)]
        right = cat([near] + [self.yr[s, :, lanes] for s in range(3)], 0)
        rows = self.block * 128 // math.gcd(self.block, 128)
        for base in range(0, self.deep, rows):
            if self.by_rows:
                r, inside = base // self.run, base % self.run
                spot = pl.ds(pl.multiple_of(2 * r * self.run + side * self.run + inside, 128), rows)
            else:
                spot = pl.ds(base, rows)
            left = cat([self.x[:, spot]] + [self.xr[s, :, base:base + rows] for s in range(3)], 0)
            value = tn(left, right).astype(BF16)
            for j in range(rows // self.block):
                block = base // self.block + j
                if self.by_rows:
                    low = 1 << self.order[0]
                    block = block // low * 2 * low + block % low
                self.sums[place_of(block, self.rest), :, lanes] = (
                    value[j * self.block:(j + 1) * self.block])
        self.hop(0, part).start()

    def spans(self, stage):
        half = self.blocks >> (stage + 1)
        start = 0
        for k in range(stage):
            start = start + partner_of(self.rest[k])[1] * (self.blocks >> (k + 1))
        side = partner_of(self.rest[stage])[1]
        return half, start + side * half, start + (1 - side) * half, self.blocks - 2 * half

    def hop(self, stage, part):
        half, _, away, landing = self.spans(stage)
        lanes = pl.ds(part * self.step, self.step)
        return pltpu.make_async_remote_copy(
            src_ref=self.sums.at[pl.ds(away, half), :, lanes],
            dst_ref=self.got.at[pl.ds(landing, half), :, lanes],
            send_sem=self.hop_sent.at[stage, part], recv_sem=self.hop_came.at[stage, part],
            device_id={"batch": partner_of(self.rest[stage])[0]}, device_id_type=MESH)

    def advance(self, stage, part):
        half, keep, _, landing = self.spans(stage)
        lanes = slice(part * self.step, (part + 1) * self.step)
        self.hop(stage, part).wait_recv()
        if stage + 1 < self.stages:
            def add(j, carry):
                self.sums[keep + j, :, lanes] = (
                    self.sums[keep + j, :, lanes].astype(F32)
                    + self.got[landing + j, :, lanes].astype(F32)).astype(BF16)
                return carry

            lax.fori_loop(0, half, add, 0)
            self.hop(stage + 1, part).start()
            return
        mine, theirs = self.sums[keep, :, lanes].astype(F32), self.got[landing, :, lanes].astype(F32)
        if self.by_rows:
            self.out[:, lanes] = mine + theirs
        else:
            first = self.side() == 0
            far = slice(self.wide + part * self.step, self.wide + (part + 1) * self.step)
            self.out[:, lanes] = jnp.where(first, mine, theirs)
            self.out[:, far] = jnp.where(first, theirs, mine)

    def drain(self):
        self.drain_factors((1,))
        for stage in range(self.stages):
            for part in range(self.parts):
                self.hop(stage, part).wait_send()


class Small:
    parts = 1

    def __init__(self, owner, bits):
        self.owner, self.bits, self.stages = owner, bits, bits

    def scratch(self, dims):
        dma = pltpu.SemaphoreType.DMA
        return [pltpu.VMEM((self.bits + 1,) + dims, F32), pltpu.VMEM((self.bits + 1,) + dims, F32),
                dma((self.bits + 1,)), dma((self.bits + 1,))]

    def bind(self, x, out, scratch):
        self.x, self.out = x, out
        self.got, self.sums, self.sent, self.came = scratch
        return self

    def arrive(self):
        return pltpu.make_async_remote_copy(
            src_ref=self.x, dst_ref=self.got.at[self.bits], send_sem=self.sent.at[self.bits],
            recv_sem=self.came.at[self.bits], device_id={"section": self.owner}, device_id_type=MESH)

    def hop(self, stage):
        return pltpu.make_async_remote_copy(
            src_ref=self.sums.at[stage], dst_ref=self.got.at[stage], send_sem=self.sent.at[stage],
            recv_sem=self.came.at[stage], device_id={"batch": partner_of(stage)[0]},
            device_id_type=MESH)

    def send_y(self, slots):
        if 0 in slots:
            self.arrive().start()

    def drain_factors(self, slots):
        self.arrive().wait_send()

    def multiply(self, part):
        self.arrive().wait_recv()
        self.sums[0] = self.x[...] + self.got[self.bits]
        self.hop(0).start()

    def advance(self, stage, part):
        self.hop(stage).wait_recv()
        self.sums[stage + 1] = self.sums[stage] + self.got[stage]
        if stage + 1 < self.bits:
            self.hop(stage + 1).start()
        else:
            self.out[...] = self.sums[self.bits]

    def drain(self):
        for stage in range(self.bits):
            self.hop(stage).wait_send()


def greet(bits, near):
    barrier = pltpu.get_barrier_semaphore()
    other = 1 - lax.axis_index("section")
    targets = [{"section": other}]
    targets += [{"batch": partner_of(bit)[0]} for bit in range(bits)]
    targets += [{"section": other, "batch": partner_of(bit)[0]} for bit in near]
    for target in targets:
        pl.semaphore_signal(barrier, inc=1, device_id=target, device_id_type=MESH)
    pl.semaphore_wait(barrier, len(targets))


class Take:
    def __init__(self, refs):
        self.refs, self.at = refs, 0

    def __call__(self, count):
        self.at += count
        return self.refs[self.at - count:self.at]


def residuals(rows, width, hidden):
    heads = width // LM
    return {
        "qkv": ((3, rows, width), BF16), "lm": ((2, LM, width), BF16), "a1": ((rows, width), F32),
        "a2": ((LM, width), F32), "a3": ((LM, heads * rows), F32),
        "band": ((heads // 2, rows, 2 * rows), BF16), "db": ((2, LM, width), BF16),
        "z": ((NEWTON + 1, LM, width), F32), "r": ((NEWTON + 1, LM, width), F32),
        "s": ((NEWTON, LM, width), F32), "t": ((NEWTON, LM, width), F32),
        "hat1": ((rows, width), F32), "hat2": ((rows, width), F32), "rstd": ((rows, 128), F32),
        "slope": ((rows, hidden), BF16)}


def encoder(*refs, names, plans, littles, taps, remote):
    take = Take(refs)
    (lengths_ref,) = take(1)
    input_ref, cotangent_ref, bias_ref, taps_ref = take(4)
    params = take(7)
    own = take(4)
    other_in = () if remote else take(4)
    vec_in = () if remote else take(2)
    act_out, ig_ref = take(2)
    count = len(plans[0])
    outs = take(count) if remote else ()
    small_out = take(1)[0] if remote else None
    other = take(4) if remote else other_in
    layers_out = () if remote else [take(9), take(9)]
    kept = [dict(zip(names, take(len(names)))) for _ in range(2)]
    ring, ring_sem, mid_ref, gi_ref, gr_ref, do_ref = take(6)
    work = take(3)
    (err_ref,) = take(1)
    vecs, tap_rows = take(2)
    section = lax.axis_index("section")
    rows, width = mid_ref.shape
    hidden = own[EXPAND].shape[1]
    chunks, heads = hidden // width, width // LM
    at = 6 + chunks
    err = at + 2 + heads // (width // rows)
    groups = []
    for part, layer in ((forward_groups, 0), (forward_groups, 1), (backward_groups, 1), (backward_groups, 0)):
        groups += part(layer, chunks)
    length = lengths_ref[section]
    if remote:
        factors = [take(7), take(7)]
        smalls = take(2)
        own_sent, own_came, vec_sent, vec_came, share_sent, share_came = take(6)
        scratch = [take(10) for _ in range(count)]
        small_scratch = take(4)
    else:
        factors = [layer[:7] for layer in layers_out]
        smalls = [layer[7] for layer in layers_out]
    x_ref = input_ref.at[pl.ds(section * rows, rows)]
    for layer in range(2):
        kept[layer].update(zip(("act", "first", "att"), factors[layer][:3]))
        smalls[layer][...] = jnp.zeros(smalls[layer].shape, F32)
    ys = [f[3:7] for f in factors]
    pieces = [g for g in forward_groups(0, chunks)]

    def pack(vec, taps_to):
        line = 0
        taps_to[...] = jnp.zeros(taps_to.shape, F32)
        taps_to[0:heads, 0:taps] = taps_ref[0]
        for ref in params + (bias_ref,):
            for c in range(ref.shape[1] // width):
                vec[line:line + 1, :] = ref[:, c * width:(c + 1) * width]
                line += 1

    def weight_copy(i):
        _, w, row, col = pieces[i]
        spot = (pl.ds(row * width, width), pl.ds(col * width, width))
        return pltpu.make_async_remote_copy(
            src_ref=own[w].at[spot], dst_ref=other[w].at[spot], send_sem=own_sent.at[i],
            recv_sem=own_came.at[i], device_id={"section": 1 - section}, device_id_type=MESH)

    def vec_copy(i):
        ref = (vecs, tap_rows)[i]
        return pltpu.make_async_remote_copy(
            src_ref=ref.at[section], dst_ref=ref.at[section], send_sem=vec_sent.at[i],
            recv_sem=vec_came.at[i], device_id={"section": 1 - section}, device_id_type=MESH)

    def vec_wait(i):
        ref = (vecs, tap_rows)[i]
        return pltpu.make_async_remote_copy(
            src_ref=ref.at[1 - section], dst_ref=ref.at[1 - section], send_sem=vec_sent.at[i],
            recv_sem=vec_came.at[i], device_id={"section": 1 - section}, device_id_type=MESH)

    def arrived(group):
        if remote:
            weight_copy(pieces.index((0,) + group[1:])).wait_recv()

    stream = Stream(groups, own, other, ring, ring_sem, arrived)
    if remote:
        items = []
        for layer in range(2):
            x0 = x_ref if layer == 0 else mid_ref
            f = factors[layer]
            xs, yy = (f[0], f[1], x0, f[2]), (f[3], f[4], f[6], f[5])
            items.append([w.bind(xs[i], yy[i], outs[i], scratch[i])
                          for i, w in enumerate(plans[layer])]
                         + [littles[layer].bind(smalls[layer], small_out, small_scratch)])
        greet(littles[0].bits, sorted({w.order[0] for w in plans[0]}))
        pack(vecs.at[section], tap_rows.at[section])
        for i in range(2):
            vec_copy(i).start()
        for i in range(3):
            weight_copy(i).start()
        stream.start(1)
        for i in range(2):
            vec_wait(i).wait_recv()
    else:
        vecs[...] = vec_in[0][...]
        tap_rows[...] = vec_in[1][...]

    def send(layer, which, what):
        if remote:
            for role, slots in ((section == layer, (1,)), (section != layer, (0, 2))):
                @pl.when(role)
                def _():
                    for i in which:
                        getattr(items[layer][i], what)(slots)

    def run(layer, *jobs):
        if remote:
            @pl.when(section == layer)
            def _():
                for item, stage, part in jobs:
                    if stage is None:
                        items[layer][item].multiply(part)
                    else:
                        items[layer][item].advance(stage, part)

    def both_rows(k, layer, source, target):
        def copy():
            return pltpu.make_async_remote_copy(
                src_ref=source, dst_ref=target.at[pl.ds((1 - layer) * rows, rows)],
                send_sem=share_sent.at[k], recv_sem=share_came.at[k],
                device_id={"section": layer}, device_id_type=MESH)

        if remote:
            @pl.when(section == layer)
            def _():
                target[layer * rows:(layer + 1) * rows, :] = source[...]

            @pl.when(section != layer)
            def _():
                copy().start()
        else:
            target[layer * rows:(layer + 1) * rows, :] = source[...]
        return copy

    def schedule(name, slot):
        steps = SCHEDULE.get((name, slot), ())
        for step in steps:
            if step[0] == "x":
                send(step[1], step[2], "send_x")
            elif step[0] == "y":
                send(step[1], step[2], "send_y")
            else:
                run(step[1], *step[2])

    def hook(name, slot):
        if name == "forward0" and slot == 0 and remote:
            for i in range(3):
                weight_copy(i).wait_send()
            for i in range(3, len(pieces)):
                weight_copy(i).start()
        if name == "forward0" and slot == 1:
            stream.flow()
        schedule(name, slot)

    per_layer = len(forward_groups(0, chunks))
    x = x_ref[...]
    shared = []
    for layer in range(2):
        vec = vecs[layer]
        bias = (vec[at:at + 1], None, vec[at + 1:at + 2])
        name = "forward" + str(layer)
        attention_forward(
            length, x, bias, tap_rows.at[layer], kept[layer], (smalls[layer], err, err_ref), stream,
            layer * per_layer, functools.partial(hook, name), taps)
        out = post_forward(length, x, vec, kept[layer], stream, layer * per_layer + 3)
        mid_or_out = mid_ref if layer == 0 else gi_ref.at[2]
        mid_or_out[...] = out
        shared.append((layer, both_rows(layer, layer, mid_or_out, act_out)))
        schedule(name, 3)
        x = out
    g = cotangent_ref[pl.ds(section * rows, rows), :]
    group = 2 * per_layer
    for layer in (1, 0):
        name = "backward" + str(layer)
        y = ys[layer]
        post_backward(
            length, g, kept[layer], vecs[layer], (y[0], y[1], y[2]), gr_ref, do_ref, smalls[layer],
            stream, group, functools.partial(schedule, "post" + str(layer)))
        g = attention_backward(
            length, do_ref, gr_ref, kept[layer], y[3], smalls[layer], at, work, stream,
            group + 1 + 2 * chunks, functools.partial(schedule, name), taps)
        gi_ref[layer] = g
        shared.append((layer, both_rows(2 + layer, layer, gi_ref.at[layer], ig_ref)))
        schedule(name, 5)
        group += per_layer
    if remote:
        schedule("tail", 0)
        for layer in range(2):
            @pl.when(section == layer)
            def _():
                for item in items[layer]:
                    item.drain()

            @pl.when(section != layer)
            def _():
                for item in items[layer]:
                    item.drain_factors((0, 2))
        for k, (layer, copy) in enumerate(shared):
            @pl.when(section == layer)
            def _():
                copy().wait_recv()

            @pl.when(section != layer)
            def _():
                copy().wait_send()
        for i in range(3, len(pieces)):
            weight_copy(i).wait_send()
        for i in range(2):
            vec_copy(i).wait_send()
    else:
        for layer in range(2):
            layers_out[layer][8][...] = gi_ref[2] if layer else mid_ref[...]


RED, EXP, PRO, PUT, SMALL = range(5)


def steps(layer, *jobs):
    return ("run", layer, jobs)


def mult(item, *parts):
    return tuple((item, None, part) for part in parts)


SCHEDULE = {
    ("forward0", 0): [("x", 0, (PRO,))],
    ("forward0", 2): [("x", 0, (PUT,))],
    ("forward0", 3): [("x", 1, (PRO,)), ("x", 0, (RED, EXP))],
    ("forward1", 2): [("x", 1, (PUT,))],
    ("forward1", 3): [("x", 1, (RED, EXP))],
    ("post1", 0): [("y", 1, (RED,))],
    ("post1", 1): [("y", 1, (EXP,))],
    ("post1", 2): [("y", 1, (PUT,))],
    ("backward1", 0): [steps(1, *mult(RED, 0, 1))],
    ("backward1", 1): [steps(1, *mult(PUT, 0))],
    ("backward1", 2): [steps(1, *mult(EXP, 0))],
    ("backward1", 3): [steps(1, *mult(EXP, 1), (PUT, 0, 0))],
    ("backward1", 4): [("y", 1, (PRO, SMALL)), steps(1, (RED, 0, 0))],
    ("backward1", 5): [steps(1, (EXP, 0, 0))],
    ("post0", 0): [("y", 0, (RED,))],
    ("post0", 1): [("y", 0, (EXP,)), steps(1, (PUT, 1, 0))],
    ("post0", 2): [("y", 0, (PUT,)), steps(1, (RED, 0, 1), (RED, 1, 0))],
    ("backward0", 0): [steps(1, (EXP, 0, 1), (EXP, 1, 0), (PUT, 2, 0), (SMALL, None, 0))],
    ("backward0", 1): [steps(1, (RED, 1, 1)), steps(0, *mult(PUT, 0))],
    ("backward0", 2): [steps(1, (EXP, 1, 1), (RED, 2, 0), (SMALL, 0, 0)), steps(0, *mult(RED, 0, 1))],
    ("backward0", 3): [steps(1, *mult(PRO, 0, 1), (RED, 2, 1), (EXP, 2, 0)), steps(0, *mult(EXP, 0))],
    ("backward0", 4): [
        ("y", 0, (PRO, SMALL)), steps(1, *mult(PRO, 2), (SMALL, 1, 0), (EXP, 2, 1), (PUT, 3, 0)),
        steps(0, *mult(EXP, 1), (PUT, 0, 0))],
    ("tail", 0): [
        steps(1, (PRO, 0, 0), (PRO, 0, 1), (EXP, 3, 0), (PRO, 0, 2), (EXP, 3, 1), (SMALL, 2, 0),
              (PRO, 1, 0), (PRO, 1, 1), (PRO, 1, 2), (PRO, 2, 0), (PRO, 2, 1), (SMALL, 3, 0),
              (PRO, 2, 2), (PRO, 3, 0), (PRO, 3, 1), (PRO, 3, 2)),
        steps(0, (SMALL, None, 0), (RED, 0, 0), *mult(PRO, 0, 1, 2), (EXP, 0, 0), (PUT, 1, 0),
              (RED, 0, 1), (EXP, 0, 1), (RED, 1, 0), (SMALL, 0, 0), (EXP, 1, 0), (PRO, 0, 0),
              (RED, 1, 1), (PUT, 2, 0), (EXP, 1, 1), (PRO, 0, 1), (RED, 2, 0), (SMALL, 1, 0),
              (EXP, 2, 0), (PRO, 0, 2), (RED, 2, 1), (EXP, 2, 1), (PRO, 1, 0), (PRO, 1, 1),
              (SMALL, 2, 0), (EXP, 3, 0), (PUT, 3, 0), (PRO, 1, 2), (EXP, 3, 1), (PRO, 2, 0),
              (PRO, 2, 1), (PRO, 2, 2), (SMALL, 3, 0), (PRO, 3, 0), (PRO, 3, 1), (PRO, 3, 2))],
}


def shape(dims, kind=F32):
    return jax.ShapeDtypeStruct(dims, kind)


IN_VMEM = pl.BlockSpec(memory_space=pltpu.VMEM)
IN_SMEM = pl.BlockSpec(memory_space=pltpu.SMEM)
ANYWHERE = pl.BlockSpec(memory_space=pl.ANY)
VMEM_LIMIT = 62 * 2 ** 20
RING = 6


def plan(owner, bits):
    tail = tuple(range(3, bits))
    return [Weight(owner, (1, 0, 2) + tail, True, 2), Weight(owner, (0, 1, 2) + tail, False, 2),
            Weight(owner, (1, 0, 2) + tail, False, 3), Weight(owner, (2, 1, 0) + tail, False, 1)]


def small_shape(width, hidden, heads, rows):
    lines = 6 + hidden // width + 2 + heads // (width // rows) + NEWTON
    return (lines + 7) // 8 * 8, width


def encode(remote, batch, lengths, layer_input, cotangent, bias, conv_kernel, params, weights, extra):
    rows, width = layer_input.shape[0] // 2, layer_input.shape[1]
    hidden, heads = weights[EXPAND].shape[1], width // LM
    chunks, bits = hidden // width, batch.bit_length() - 1
    dma = pltpu.SemaphoreType.DMA
    low = lambda n: ((rows, n), BF16)
    factor_shapes = [low(hidden), low(width), low(width), low(width), low(hidden), low(width), low(3 * width)]
    x_shapes = [(rows, n) for n in (hidden, width, width, width)]
    y_shapes = [(rows, n) for n in (width, hidden, 3 * width, width)]
    dims = small_shape(width, hidden, heads, rows)
    plans = littles = None
    plans, littles = [], []
    for layer in range(2):
        plans.append([w.sizes(a, b) for w, a, b in zip(plan(layer, bits), x_shapes, y_shapes)])
        littles.append(Small(layer, bits))
    both = shape((2 * rows, width), BF16)
    outs, out_specs = [both, both], [IN_VMEM] * 2
    if remote:
        outs += [shape((w.block, w.width)) for w in plans[0]] + [shape(dims)]
        out_specs += [IN_VMEM] * 5
        outs += [shape(w.shape, BF16) for w in weights]
        out_specs += [ANYWHERE] * 4
    else:
        for _ in range(2):
            outs += [shape(*f) for f in factor_shapes] + [shape(dims), shape((rows, width), BF16)]
            out_specs += [IN_VMEM] * 9
    names = residuals(rows, width, hidden)
    scratch = [pltpu.VMEM(*s) for _ in range(2) for s in names.values()]
    scratch += [pltpu.VMEM((RING, width, width), BF16), dma((RING,)), pltpu.VMEM(*low(width)),
                pltpu.VMEM((3, rows, width), BF16), pltpu.VMEM((rows, width), F32),
                pltpu.VMEM((rows, width), F32)]
    scratch += [pltpu.VMEM((LM, width), F32)] * 3 + [pltpu.VMEM((NEWTON, 1, width), F32)]
    scratch += [pltpu.VMEM((2, 16, width), F32), pltpu.VMEM((2, 16, 128), F32)]
    if remote:
        pieces = 4 + 2 * chunks
        scratch += [pltpu.VMEM(*f) for _ in range(2) for f in factor_shapes]
        scratch += [pltpu.VMEM(dims, F32)] * 2
        scratch += [dma((pieces,)), dma((pieces,)), dma((2,)), dma((2,)), dma((4,)), dma((4,))]
        scratch += [s for w in plans[0] for s in w.scratch()] + littles[0].scratch(dims)
    args = (lengths, layer_input, cotangent, bias, conv_kernel) + params + weights + extra
    ins = [IN_SMEM] + [IN_VMEM] * 11 + [ANYWHERE] * 4
    if not remote:
        ins += [ANYWHERE] * 4 + [IN_VMEM] * 2
    marks = dict(collective_id=0, has_side_effects=True) if remote else {}
    return pl.pallas_call(
        functools.partial(encoder, names=tuple(names), plans=plans, littles=littles,
                          taps=conv_kernel.shape[2], remote=remote),
        out_shape=tuple(outs), in_specs=ins, out_specs=tuple(out_specs), scratch_shapes=scratch,
        name="encoder", cost_estimate=pl.CostEstimate(
            flops=2 * 10 ** 10, bytes_accessed=10 ** 8, transcendentals=0),
        compiler_params=pltpu.CompilerParams(vmem_limit_bytes=VMEM_LIMIT, **marks))(*args)


def swap(value):
    return lax.ppermute(value, "section", [(0, 1), (1, 0)])


def encode_apart(batch, args, weights, params, bias, conv_kernel):
    section = lax.axis_index("section")
    width = args[1].shape[1]
    heads, taps = conv_kernel.shape[1:]
    vec = jnp.concatenate([p.reshape(-1, width) for p in params + (bias,)])
    vec = jnp.pad(vec, ((0, 16 - vec.shape[0]), (0, 0)))
    rows_of_taps = jnp.pad(conv_kernel[0], ((0, 16 - heads), (0, 128 - taps)))
    extra = [swap(w) for w in weights]
    for mine in (vec, rows_of_taps):
        theirs = swap(mine)
        extra.append(jnp.where(section == 0, jnp.stack([mine, theirs]), jnp.stack([theirs, mine])))
    result = encode(False, batch, *args, bias, conv_kernel, params, weights, tuple(extra))
    total = args[1].shape[0]
    rows = total // 2
    layers = [result[2:11], result[11:20]]
    inputs = [lax.dynamic_slice_in_dim(args[1], section * rows, rows, 0), layers[0][8]]
    shares = []
    for layer in range(2):
        act, first, att, gd, gu, gp, dqkv, small, _ = layers[layer]
        products = [lax.dot_general(x, y, (((0,), (0,)), ((), ())), preferred_element_type=F32)
                    for x, y in ((act, gd), (first, gu), (inputs[layer], dqkv), (att, gp))]
        shares.append([
            lax.psum_scatter(lax.psum(p, "section"), "batch", scatter_dimension=0, tiled=True)
            for p in products] + [lax.psum(small, ("section", "batch"))])
    lead = section == 0
    both = []
    for k in range(2):
        by_layer = [result[k][:rows], result[k][rows:]]
        crossed = swap(jnp.where(lead, by_layer[1], by_layer[0]))
        both.append(jnp.where(lead, jnp.concatenate([by_layer[0], crossed]),
                              jnp.concatenate([crossed, by_layer[1]])))
    return both + [jnp.where(lead, a, b) for a, b in zip(*shares)]


def body(
    layer_input, seq_lengths, cotangent, project_weight, project_bias, conv_kernel, output_weight,
    output_bias, attn_gain, attn_shift, expand_weight, expand_bias, reduce_weight, reduce_bias,
    final_gain, final_shift):
    batch = lax.axis_size("batch")
    width = layer_input.shape[1]
    rows = layer_input.shape[0] // 2
    heads, taps = conv_kernel.shape[1:]
    weights = (project_weight[0], output_weight[0], expand_weight[0], reduce_weight[0])
    params = (output_bias, attn_gain, attn_shift, expand_bias, reduce_bias, final_gain, final_shift)
    args = (seq_lengths, layer_input, cotangent)
    if batch >= 8 and all(w.shape[0] // batch % 16 == 0 for w in weights):
        result = encode(True, batch, *args, project_bias, conv_kernel, params, weights, ())
    else:
        result = encode_apart(batch, args, weights, params, project_bias, conv_kernel)
    activations, input_grads, g_red, g_exp, g_qkv, g_out, small = result[:7]
    index = lax.axis_index("batch")

    def share(first, many):
        flat = small[first:first + many].reshape(-1)
        size = flat.shape[0] // batch
        return lax.dynamic_slice_in_dim(flat, index * size, size, 0)[None]

    chunks = reduce_weight.shape[1] // width
    at = 6 + chunks
    end = at + 2 + heads // (width // rows)
    dtaps = small[at + 2:end].reshape(heads, rows)[:, :taps]
    proxies = jnp.sum(small[end:end + NEWTON], axis=1)
    return (
        activations[None], input_grads[None], g_qkv[None], share(at, 2), dtaps[None], g_out[None],
        share(0, 1), share(1, 1), share(2, 1), g_exp[None], share(3, chunks), g_red[None],
        share(3 + chunks, 1), share(4 + chunks, 1), share(5 + chunks, 1), proxies[None])


def solution(mesh):
    split_rows = P("batch", None)
    two, three = P("section", None), P("section", None, None)
    return jax.shard_map(
        body, mesh=mesh,
        in_specs=(split_rows, P("batch"), split_rows, three, two, three, three, two, two, two,
                  three, two, three, two, two, two),
        out_specs=(P("section", "batch", None), P("section", "batch", None),
                   P("section", "batch", None), P("section", "batch"), three,
                   P("section", "batch", None), P("section", "batch"), P("section", "batch"),
                   P("section", "batch"), P("section", "batch", None), P("section", "batch"),
                   P("section", "batch", None), P("section", "batch"), P("section", "batch"),
                   P("section", "batch"), two),
        check_vma=False)
```

```python
import functools
import math

import jax
import jax.numpy as jnp
from jax import lax
from jax.experimental import pallas as pl
from jax.experimental.pallas import tpu as pltpu
from jax.sharding import PartitionSpec as P

F32 = jnp.float32
BF16 = jnp.bfloat16
NEWTON = 6
LM = 64
PAIR = 128
EPS = 1e-05
MESH = pl.DeviceIdType.MESH
QKV, OUT, EXPAND, REDUCE = range(4)


def nn(a, b):
    return lax.dot_general(a, b, (((1,), (0,)), ((), ())), preferred_element_type=F32)


def nt(a, b):
    return lax.dot_general(a, b, (((1,), (1,)), ((), ())), preferred_element_type=F32)


def tn(a, b):
    return lax.dot_general(a, b, (((0,), (0,)), ((), ())), preferred_element_type=F32)


def split(x):
    high = x.astype(BF16)
    return high, (x - high.astype(F32)).astype(BF16)


def cat(parts, axis):
    return jnp.concatenate(parts, axis=axis)


def lane_is_first(rows, width=PAIR):
    return lax.broadcasted_iota(jnp.int32, (rows, width), 1) < width // 2


def spread(y):
    rows = y.shape[0]
    keep = lane_is_first(rows).astype(F32).astype(y.dtype)
    return cat([y * keep, y * (1 - keep)], 0)


def pick(x):
    rows = x.shape[0] // 2
    return jnp.where(lane_is_first(rows), x[:rows], x[rows:])


def nn3(xs, ys):
    (xh, xl), (yh, yl) = xs, ys
    dh, dl = spread(yh), spread(yl)
    return nn(cat([xh, xl], 1), cat([dh, dh], 0)) + nn(xh, dl)


def nt3(xs, ds):
    (xh, xl), (dh, dl) = xs, ds
    return nt(cat([xh, xl], 1), cat([dh, dh], 1)) + nt(xh, dl)


def half_sums(x, ones):
    high, low = split(x)
    return nn(high, ones) + nn(low, ones)


def block_ones():
    row = lax.broadcasted_iota(jnp.int32, (PAIR, PAIR), 0) < LM
    col = lax.broadcasted_iota(jnp.int32, (PAIR, PAIR), 1) < LM
    return (row == col).astype(F32).astype(BF16)


def pair_softmax(scores, ones):
    first = lane_is_first(scores.shape[0])
    top_a = jnp.max(jnp.where(first, scores, -jnp.inf), axis=1, keepdims=True)
    top_b = jnp.max(jnp.where(first, -jnp.inf, scores), axis=1, keepdims=True)
    e = jnp.exp(scores - jnp.where(first, top_a, top_b))
    return e / half_sums(e, ones)


def pair_transpose(x):
    t = x.T
    return cat([t[:LM], t[LM:]], 1)


def pair_eye():
    row = lax.broadcasted_iota(jnp.int32, (LM, PAIR), 0)
    col = lax.broadcasted_iota(jnp.int32, (LM, PAIR), 1)
    return (row == col % LM).astype(F32)


def pool_matrix(length, rows):
    landmark = lax.broadcasted_iota(jnp.int32, (LM, rows), 0)
    row = lax.broadcasted_iota(jnp.int32, (LM, rows), 1)
    segment = length // LM
    inside = (row >= landmark * segment) & (row < (landmark + 1) * segment)
    weight = 1.0 / jnp.full((LM, rows), segment, jnp.int32).astype(F32)
    return jnp.where(inside, weight, 0.0).astype(BF16)


def toeplitz(taps_row, rows, taps):
    half = taps // 2
    wide = jnp.broadcast_to(taps_row, (rows, rows))
    wide = pltpu.roll(wide, rows - half, 1, stride=1, stride_axis=0)
    row = lax.broadcasted_iota(jnp.int32, (rows, rows), 0)
    col = lax.broadcasted_iota(jnp.int32, (rows, rows), 1)
    near = (col - row <= half) & (row - col <= half)
    return jnp.where(near, wide, 0.0)


def attention_forward(length, x, bias, taps_ref, kept, err_at, stream, group, hook, taps):
    rows, width = x.shape
    pairs = width // PAIR
    z_ref, r_ref, s_ref, t_ref = kept["z"], kept["r"], kept["s"], kept["t"]
    a1_ref, a2_ref, a3_ref, band_ref = kept["a1"], kept["a2"], kept["a3"], kept["band"]
    qkv_ref, lm_ref, db_ref = kept["qkv"], kept["lm"], kept["db"]
    ones = block_ones()
    pool = pool_matrix(length, rows)
    eye = pair_eye()
    sl = [pl.ds(p * PAIR, PAIR) for p in range(pairs)]
    valid = (lax.broadcasted_iota(jnp.int32, (rows, width), 0) < length).astype(F32)
    scale = LM ** (-0.25)
    qkv = []
    for i in range(3):
        y = nn(x, stream.take(group + i))
        if bias[i] is not None:
            y = y + bias[i]
        qkv.append(y * (valid * scale if i < 2 else valid))
        stream.release(group + i)
    q, k, v = [[m[:, p * PAIR:(p + 1) * PAIR] for p in range(pairs)] for m in qkv]
    qs = [split(m) for m in q]
    ks = [split(m) for m in k]
    vs = [split(m) for m in v]
    for i, ms in enumerate((qs, ks, vs)):
        for p in range(pairs):
            qkv_ref[i, :, sl[p]] = ms[p][0]
    qls = [split(nn(pool, h) + nn(pool, l)) for h, l in qs]
    kls = [split(nn(pool, h) + nn(pool, l)) for h, l in ks]
    for p in range(pairs):
        lm_ref[0, :, sl[p]] = qls[p][0]
        lm_ref[1, :, sl[p]] = kls[p][0]
    kld = [(spread(h), spread(l)) for h, l in kls]
    for p in range(pairs):
        a2_ref[:, sl[p]] = pair_softmax(nt3(qls[p], kld[p]), ones)
    first = lane_is_first(LM)
    for p in range(pairs):
        a = a2_ref[:, sl[p]]
        squares = jnp.sum(a * a, axis=0, keepdims=True)
        fro_a = jnp.sum(jnp.where(first[:1], squares, 0.0), axis=1, keepdims=True)
        fro_b = jnp.sum(jnp.where(first[:1], 0.0, squares), axis=1, keepdims=True)
        z_ref[0, :, sl[p]] = pair_transpose(a) / jnp.where(first[:1], fro_a, fro_b)
    for p in range(pairs):
        z = split(z_ref[0, :, sl[p]])
        r_ref[0, :, sl[p]] = eye - nn3(split(a2_ref[:, sl[p]]), z)
    hook(0)
    small_ref, line, err_ref = err_at

    def newton_step(step, carry):
        s_all, t_all = [], []
        for p in range(pairs):
            r = r_ref[step, :, sl[p]]
            rs = split(r)
            s = nn3(rs, rs)
            s_ref[step, :, sl[p]] = s
            s_all.append((r, rs, s))
        for p in range(pairs):
            r, rs, s = s_all[p]
            t = nn3(split(s), rs)
            t_ref[step, :, sl[p]] = t
            t_all.append(eye + r + s + 0.25 * t)
        for p in range(pairs):
            zn = nn3(split(z_ref[step, :, sl[p]]), split(t_all[p]))
            z_ref[step + 1, :, sl[p]] = zn
            rn = eye - nn3(split(a2_ref[:, sl[p]]), split(zn))
            r_ref[step + 1, :, sl[p]] = rn
            err_ref[step, :, sl[p]] = jnp.sum(rn * rn, axis=0, keepdims=True)
        return carry

    lax.fori_loop(0, NEWTON, newton_step, 0)
    for i in range(NEWTON):
        small_ref[line + i:line + i + 1, :] = err_ref[i]
    hook(1)
    for p in range(pairs):
        wide = slice(p * 2 * rows, (p + 1) * 2 * rows)
        score = nt3(qls[p], (spread(ks[p][0]), spread(ks[p][1])))
        key = lax.broadcasted_iota(jnp.int32, (LM, rows), 1)
        halves = []
        for j in range(2):
            sc = jnp.where(key < length, score[:, j * rows:(j + 1) * rows], -1e30)
            e = jnp.exp(sc - jnp.max(sc, axis=1, keepdims=True))
            halves.append(e / jnp.sum(e, axis=1, keepdims=True))
        a3 = cat(halves, 1)
        a3_ref[:, wide] = a3
        a3h, a3l = split(a3)
        vh, vl = spread(vs[p][0]), spread(vs[p][1])
        d = nn(a3h, vh) + (nn(a3l, vh) + nn(a3h, vl))
        z = split(z_ref[NEWTON, :, sl[p]])
        ds = split(d)
        b = nn3(z, ds)
        bs = split(b)
        db_ref[0, :, sl[p]] = ds[0]
        db_ref[1, :, sl[p]] = bs[0]
        a1 = pair_softmax(nt3(qs[p], kld[p]), ones)
        a1_ref[:, sl[p]] = a1
        band = cat([toeplitz(taps_ref[2 * p + j:2 * p + j + 1, :], rows, taps) for j in range(2)], 1)
        th, tl = split(band)
        band_ref[p] = th
        o = nn3(split(a1), bs) + nn(cat([th, tl], 1), cat([vh, vh], 0)) + nn(th, vl)
        kept["att"][:, sl[p]] = o.astype(BF16)
    hook(2)


def norm_forward(values):
    center = values - jnp.mean(values, axis=1, keepdims=True)
    rstd = lax.rsqrt(jnp.mean(center * center, axis=1, keepdims=True) + EPS)
    return center * rstd, rstd


def norm_back(grad, hat, rstd):
    mean = jnp.mean(grad, axis=1, keepdims=True)
    slope = jnp.mean(grad * hat, axis=1, keepdims=True)
    return rstd * (grad - mean - hat * slope)


def post_forward(length, x, vec, kept, stream, group):
    rows, width = x.shape
    chunks = kept["act"].shape[1] // width
    row = lambda i: vec[i:i + 1, :]
    hidden = x.astype(F32) + (nn(kept["att"][...], stream.take(group)) + row(0))
    stream.release(group)
    hat, rstd = norm_forward(hidden)
    kept["hat1"][...] = hat
    kept["rstd"][:, 0:1] = rstd
    first = hat * row(1) + row(2)
    low = first.astype(BF16)
    kept["first"][...] = low
    down = first + row(3 + chunks)
    for c in range(chunks):
        lanes = slice(c * width, (c + 1) * width)
        up = nn(low, stream.take(group + 1 + 2 * c)) + row(3 + c)
        stream.release(group + 1 + 2 * c)
        cdf = 0.5 * (1.0 + lax.erf(up * (2.0 ** -0.5)))
        act = (up * cdf).astype(BF16)
        slope = cdf + up * (jnp.exp(-0.5 * up * up) * 0.3989422804014327)
        kept["slope"][:, lanes] = slope.astype(kept["slope"].dtype)
        kept["act"][:, lanes] = act
        down = down + nn(act, stream.take(group + 2 + 2 * c))
        stream.release(group + 2 + 2 * c)
    hat, rstd = norm_forward(down)
    kept["hat2"][...] = hat
    kept["rstd"][:, 1:2] = rstd
    valid = lax.broadcasted_iota(jnp.int32, (rows, width), 0) < length
    return jnp.where(valid, hat * row(4 + chunks) + row(5 + chunks), 0.0).astype(BF16)


def softmax_back(a, da, ones):
    return a * (da - half_sums(a * da, ones))


def attention_backward(
    length, do_ref, gr_ref, kept, dqkv_ref, small_ref, at, work, stream, group, hook, taps):
    dz_ref, dr_ref, da_ref = work
    a1_ref, a2_ref, a3_ref, band_ref = kept["a1"], kept["a2"], kept["a3"], kept["band"]
    qkv_ref, lm_ref, db_ref = kept["qkv"], kept["lm"], kept["db"]
    rows, width = do_ref.shape
    pairs = width // PAIR
    ones = block_ones()
    eye = pair_eye()
    pool = pool_matrix(length, rows)
    sl = [pl.ds(p * PAIR, PAIR) for p in range(pairs)]
    doh = [do_ref[:, sl[p]].astype(BF16) for p in range(pairs)]
    ddh = []
    for p in range(pairs):
        a1 = a1_ref[:, sl[p]].astype(BF16)
        db = pick(tn(a1, doh[p]))
        dbh = db.astype(BF16)
        z = kept["z"][NEWTON, :, sl[p]].astype(BF16)
        dz_ref[:, sl[p]] = nt(dbh, spread(db_ref[0, :, sl[p]]))
        dr_ref[:, sl[p]] = jnp.zeros((LM, PAIR), F32)
        ddh.append(pick(tn(z, dbh)).astype(BF16))
    hook(0)

    def newton_back(index, carry):
        step = NEWTON - 1 - index
        keep = []
        for p in range(pairs):
            z = kept["z"][step, :, sl[p]]
            zh, zl = split(z)
            dz = dz_ref[:, sl[p]]
            gh, gl = split(dz)
            full = tn(cat([zh, zh, zl], 0), cat([gh, gl, gh], 0))
            df = pick(full + full.T) * 0.5
            keep.append((df, (gh, gl)))
        for p in range(pairs):
            df, g = keep[p]
            r, s, t = [kept[n][step, :, sl[p]] for n in ("r", "s", "t")]
            dz_ref[:, sl[p]] = nn3(g, split(eye + r + s + 0.25 * t))
            dr = dr_ref[:, sl[p]]
            dt = 0.25 * df + 0.75 * dr
            rs, ss, dts, drs = split(r), split(s), split(dt), split(0.5 * dr)
            m = nn3(dts, rs) + nn3(drs, ss)
            keep[p] = (df, dts, m, rs, ss)
        for p in range(pairs):
            df, dts, m, rs, ss = keep[p]
            ds = 2.0 * df + (m + pair_transpose(m))
            m = nn3(dts, ss) + nn3(split(ds), rs)
            dr_ref[:, sl[p]] = df + 0.5 * (m + pair_transpose(m))
        return carry

    for third in range(3):
        lax.fori_loop(third * NEWTON // 3, (third + 1) * NEWTON // 3, newton_back, 0)
        hook(1 + third)
    first = lane_is_first(1)
    for p in range(pairs):
        a = a2_ref[:, sl[p]]
        turned = pair_transpose(a)
        dz = dz_ref[:, sl[p]]
        g = nn3(split(dr_ref[:, sl[p]]), split(a))

        def halves(m):
            c = jnp.sum(m, axis=0, keepdims=True)
            ca = jnp.sum(jnp.where(first, c, 0.0), axis=1, keepdims=True)
            cb = jnp.sum(jnp.where(first, 0.0, c), axis=1, keepdims=True)
            return jnp.where(first, ca, cb)

        inv = 1.0 / halves(a * a)
        dc = halves(dz * turned) - halves(g * a)
        da_ref[:, sl[p]] = inv * (pair_transpose(dz) - 2.0 * g) - (2.0 * dc * inv * inv) * a
    scale = LM ** (-0.25)
    valid = (lax.broadcasted_iota(jnp.int32, (rows, PAIR), 0) < length).astype(F32)
    half = taps // 2
    row = lax.broadcasted_iota(jnp.int32, (rows, rows), 0)
    col = lax.broadcasted_iota(jnp.int32, (rows, rows), 1)
    flip = (row + col == rows - 1).astype(F32).astype(BF16)
    near = (col + row <= rows - 1 + half) & (col + row >= rows - 1 - half)
    per_row = width // rows
    for p in range(pairs):
        q, k, v = [qkv_ref[i, :, sl[p]] for i in range(3)]
        ql, kl = lm_ref[0, :, sl[p]], lm_ref[1, :, sl[p]]
        kld, kd, vd = spread(kl), spread(k), spread(v)
        wide = slice(p * 2 * rows, (p + 1) * 2 * rows)
        ds2 = softmax_back(a2_ref[:, sl[p]], da_ref[:, sl[p]], ones).astype(BF16)
        a1 = a1_ref[:, sl[p]]
        da1 = nt(doh[p], spread(db_ref[1, :, sl[p]]))
        ds1 = softmax_back(a1, da1, ones).astype(BF16)
        a3 = a3_ref[:, wide]
        da3 = nt(ddh[p], vd)
        parts = []
        for j in range(2):
            a, d = a3[:, j * rows:(j + 1) * rows], da3[:, j * rows:(j + 1) * rows]
            parts.append(a * (d - jnp.sum(a * d, axis=1, keepdims=True)))
        ds3 = cat(parts, 1).astype(BF16)
        dv = pick(tn(cat([a3.astype(BF16), band_ref[p]], 0), cat([ddh[p], doh[p]], 0)))
        full = nt(spread(nn(flip, doh[p]).astype(BF16)), v)
        for j in range(2):
            m = jnp.where(near, full[j * rows:(j + 1) * rows], 0.0)
            m = pltpu.roll(m, half + 1, 1, stride=1, stride_axis=0)
            head = 2 * p + j
            line, lane = at + 2 + head // per_row, head % per_row * rows
            small_ref[line:line + 1, lane:lane + rows] = jnp.sum(m, axis=0, keepdims=True)
        dkl = pick(tn(cat([ds1, ds2], 0), cat([q, ql], 0)))
        dql = nn(cat([ds2, ds3], 1), cat([kld, kd], 0))
        dqlh, dqll = split(dql)
        dklh, dkll = split(dkl)
        dq = nn(ds1, kld) + (tn(pool, dqlh) + tn(pool, dqll))
        dk = pick(tn(ds3, ql)) + (tn(pool, dklh) + tn(pool, dkll))
        for i, m in enumerate((dq * scale, dk * scale, dv)):
            low = (m * valid).astype(BF16)
            dqkv_ref[:, pl.ds(i * width + p * PAIR, PAIR)] = low
        if p in (1, 3):
            hook(4 + p // 2)
    for i, line in ((0, at), (2, at + 1)):
        small_ref[line:line + 1, :] = jnp.sum(
            dqkv_ref[:, i * width:(i + 1) * width].astype(F32), axis=0, keepdims=True)
    hook(6)
    total = gr_ref[...]
    for i in range(3):
        total = total + nt(dqkv_ref[:, i * width:(i + 1) * width], stream.take(group + i))
        stream.release(group + i)
    return total.astype(BF16)


def post_backward(length, g, kept, vec, ys, gr_ref, do_ref, sums_ref, stream, group, hook):
    gd_ref, gu_ref, gp_ref = ys
    rows, width = g.shape
    chunks = gu_ref.shape[1] // width
    row = lambda i: vec[i:i + 1, :]

    def total(i, values):
        sums_ref[i:i + 1, :] = jnp.sum(values, axis=0, keepdims=True)

    valid = lax.broadcasted_iota(jnp.int32, (rows, width), 0) < length
    g = jnp.where(valid, g.astype(F32), 0.0)
    hat2 = kept["hat2"][...]
    total(4 + chunks, g * hat2)
    total(5 + chunks, g)
    second = norm_back(g * row(4 + chunks), hat2, kept["rstd"][:, 1:2])
    gd = second.astype(BF16)
    gd_ref[...] = gd
    hook(0)
    total(3 + chunks, gd.astype(F32))
    grad = second
    for c in range(chunks):
        lanes = slice(c * width, (c + 1) * width)
        gu = nt(gd, stream.take(group + 2 * c)) * kept["slope"][:, lanes].astype(F32)
        gu = gu.astype(BF16)
        stream.release(group + 2 * c)
        gu_ref[:, lanes] = gu
        total(3 + c, gu.astype(F32))
        grad = grad + nt(gu, stream.take(group + 2 * c + 1))
        stream.release(group + 2 * c + 1)
        hook(1 + c)
    hat1 = kept["hat1"][...]
    total(1, grad * hat1)
    total(2, grad)
    residual = norm_back(grad * row(1), hat1, kept["rstd"][:, 0:1])
    gr_ref[...] = residual
    gp = residual.astype(BF16)
    gp_ref[...] = gp
    hook(5)
    total(0, gp.astype(F32))
    do_ref[...] = nt(gp, stream.take(group + 2 * chunks))
    stream.release(group + 2 * chunks)


class Stream:
    def __init__(self, groups, own, other, ring, sem, arrived):
        self.groups, self.own, self.other = groups, own, other
        self.ring, self.sem, self.arrived = ring, sem, arrived
        self.slots, self.cursor, self.free, self.flowing = ring.shape[0], 0, 0, False
        self.seen = set()

    def copy(self, i, refs):
        _, w, row, col = self.groups[i]
        size = self.ring.shape[1]
        source = refs[w].at[pl.ds(row * size, size), pl.ds(col * size, size)]
        slot = i % self.slots
        return pltpu.make_async_copy(source, self.ring.at[slot], self.sem.at[slot])

    def start(self, until):
        while self.cursor < min(until, len(self.groups)):
            i = self.cursor
            own = lax.axis_index("section") == self.groups[i][0]
            fresh = self.groups[i] not in self.seen
            self.seen.add(self.groups[i])

            @pl.when(own)
            def _():
                self.copy(i, self.own).start()

            @pl.when(jnp.logical_not(own))
            def _():
                if fresh:
                    self.arrived(self.groups[i])
                self.copy(i, self.other).start()

            self.cursor += 1

    def flow(self):
        self.flowing = True
        self.start(self.free + self.slots)

    def take(self, i):
        self.start(i + 1)
        self.copy(i, self.own).wait()
        return self.ring[i % self.slots]

    def release(self, i):
        self.free = i + 1
        if self.flowing:
            self.start(self.free + self.slots)


def forward_groups(layer, chunks):
    groups = [(layer, QKV, 0, i) for i in range(3)] + [(layer, OUT, 0, 0)]
    for c in range(chunks):
        groups += [(layer, EXPAND, 0, c), (layer, REDUCE, c, 0)]
    return groups


def backward_groups(layer, chunks):
    groups = []
    for c in range(chunks):
        groups += [(layer, REDUCE, c, 0), (layer, EXPAND, 0, c)]
    return groups + [(layer, OUT, 0, 0)] + [(layer, QKV, 0, i) for i in range(3)]


def partner_of(bit):
    me = lax.axis_index("batch")
    side = (me // (1 << bit)) % 2
    return me + (1 - 2 * side) * (1 << bit), side


def place_of(block, order):
    last = len(order) - 1
    return sum(((block >> bit) & 1) << (last - k) for k, bit in enumerate(order))


class Weight:
    def __init__(self, owner, order, by_rows, parts):
        self.owner, self.order, self.by_rows, self.parts = owner, order, by_rows, parts
        self.bits = len(order)
        self.batch = 1 << self.bits
        self.rest = order[1:] if by_rows else order[1:] + order[:1]
        self.stages = len(self.rest)

    def sizes(self, x, y):
        self.block = x[1] // self.batch
        self.run = (1 << self.order[0]) * self.block
        self.runs = self.batch >> (self.order[0] + 1) if self.by_rows else 1
        self.rows, self.depth, self.width = x[0], x[1], y[1]
        self.deep = self.depth // 2 if self.by_rows else self.depth
        self.wide = self.width if self.by_rows else self.width // 2
        self.blocks = self.batch // 2 if self.by_rows else self.batch
        self.step = self.wide // self.parts
        return self

    def scratch(self):
        dma = pltpu.SemaphoreType.DMA
        return [
            pltpu.VMEM((3, self.rows, self.deep), BF16), pltpu.VMEM((3, self.rows, self.wide), BF16),
            pltpu.VMEM((self.blocks, self.block, self.wide), BF16),
            pltpu.VMEM((self.blocks - 1, self.block, self.wide), BF16),
            dma((3, self.runs)), dma((3, self.runs)), dma((3, self.parts)), dma((3, self.parts)),
            dma((self.stages, self.parts)), dma((self.stages, self.parts))]

    def bind(self, x, y, out, scratch):
        self.x, self.y, self.out = x, y, out
        (self.xr, self.yr, self.sums, self.got, self.x_sent, self.x_came, self.y_sent, self.y_came,
         self.hop_sent, self.hop_came) = scratch
        return self

    def side(self):
        return partner_of(self.order[0])[1]

    def towards(self, slot):
        other, side = partner_of(self.order[0])
        if slot == 0:
            return {"section": self.owner}, side
        return {"section": self.owner, "batch": other}, 1 - side

    def x_copies(self, slot):
        target, side = self.towards(slot)
        for r in range(self.runs):
            if self.by_rows:
                start = pl.multiple_of(2 * r * self.run + side * self.run, 128)
                source, into = self.x.at[:, pl.ds(start, self.run)], pl.ds(r * self.run, self.run)
                into = self.xr.at[slot, :, into]
            else:
                source, into = self.x, self.xr.at[slot]
            yield pltpu.make_async_remote_copy(
                src_ref=source, dst_ref=into, send_sem=self.x_sent.at[slot, r],
                recv_sem=self.x_came.at[slot, r], device_id=target, device_id_type=MESH)

    def y_copy(self, slot, part):
        target, side = self.towards(slot)
        lanes = pl.ds(part * self.step, self.step)
        if self.by_rows:
            source = self.y.at[:, lanes]
        else:
            start = pl.multiple_of(side * self.wide + part * self.step, 128)
            source = self.y.at[:, pl.ds(start, self.step)]
        return pltpu.make_async_remote_copy(
            src_ref=source, dst_ref=self.yr.at[slot, :, lanes], send_sem=self.y_sent.at[slot, part],
            recv_sem=self.y_came.at[slot, part], device_id=target, device_id_type=MESH)

    def send_x(self, slots):
        for slot in slots:
            for copy in self.x_copies(slot):
                copy.start()

    def send_y(self, slots):
        for part in range(self.parts):
            for slot in slots:
                self.y_copy(slot, part).start()

    def drain_factors(self, slots):
        for slot in slots:
            for copy in self.x_copies(slot):
                copy.wait_send()
            for part in range(self.parts):
                self.y_copy(slot, part).wait_send()

    def multiply(self, part):
        if part == 0:
            for slot in range(3):
                for copy in self.x_copies(slot):
                    copy.wait_recv()
        for slot in range(3):
            self.y_copy(slot, part).wait_recv()
        side = self.side()
        lanes = slice(part * self.step, (part + 1) * self.step)
        if self.by_rows:
            near = self.y[:, lanes]
        else:
            start = pl.multiple_of(side * self.wide + part * self.step, 128)
            near = self.y[:, pl.ds(start, self.step)]
        right = cat([near] + [self.yr[s, :, lanes] for s in range(3)], 0)
        rows = self.block * 128 // math.gcd(self.block, 128)
        for base in range(0, self.deep, rows):
            if self.by_rows:
                r, inside = base // self.run, base % self.run
                spot = pl.ds(pl.multiple_of(2 * r * self.run + side * self.run + inside, 128), rows)
            else:
                spot = pl.ds(base, rows)
            left = cat([self.x[:, spot]] + [self.xr[s, :, base:base + rows] for s in range(3)], 0)
            value = tn(left, right).astype(BF16)
            for j in range(rows // self.block):
                block = base // self.block + j
                if self.by_rows:
                    low = 1 << self.order[0]
                    block = block // low * 2 * low + block % low
                self.sums[place_of(block, self.rest), :, lanes] = (
                    value[j * self.block:(j + 1) * self.block])
        self.hop(0, part).start()

    def spans(self, stage):
        half = self.blocks >> (stage + 1)
        start = 0
        for k in range(stage):
            start = start + partner_of(self.rest[k])[1] * (self.blocks >> (k + 1))
        side = partner_of(self.rest[stage])[1]
        return half, start + side * half, start + (1 - side) * half, self.blocks - 2 * half

    def hop(self, stage, part):
        half, _, away, landing = self.spans(stage)
        lanes = pl.ds(part * self.step, self.step)
        return pltpu.make_async_remote_copy(
            src_ref=self.sums.at[pl.ds(away, half), :, lanes],
            dst_ref=self.got.at[pl.ds(landing, half), :, lanes],
            send_sem=self.hop_sent.at[stage, part], recv_sem=self.hop_came.at[stage, part],
            device_id={"batch": partner_of(self.rest[stage])[0]}, device_id_type=MESH)

    def advance(self, stage, part):
        half, keep, _, landing = self.spans(stage)
        lanes = slice(part * self.step, (part + 1) * self.step)
        self.hop(stage, part).wait_recv()
        if stage + 1 < self.stages:
            def add(j, carry):
                self.sums[keep + j, :, lanes] = (
                    self.sums[keep + j, :, lanes].astype(F32)
                    + self.got[landing + j, :, lanes].astype(F32)).astype(BF16)
                return carry

            lax.fori_loop(0, half, add, 0)
            self.hop(stage + 1, part).start()
            return
        mine, theirs = self.sums[keep, :, lanes].astype(F32), self.got[landing, :, lanes].astype(F32)
        if self.by_rows:
            self.out[:, lanes] = mine + theirs
        else:
            first = self.side() == 0
            far = slice(self.wide + part * self.step, self.wide + (part + 1) * self.step)
            self.out[:, lanes] = jnp.where(first, mine, theirs)
            self.out[:, far] = jnp.where(first, theirs, mine)

    def drain(self):
        self.drain_factors((1,))
        for stage in range(self.stages):
            for part in range(self.parts):
                self.hop(stage, part).wait_send()


class Small:
    parts = 1

    def __init__(self, owner, bits):
        self.owner, self.bits, self.stages = owner, bits, bits

    def scratch(self, dims):
        dma = pltpu.SemaphoreType.DMA
        return [pltpu.VMEM((self.bits + 1,) + dims, F32), pltpu.VMEM((self.bits + 1,) + dims, F32),
                dma((self.bits + 1,)), dma((self.bits + 1,))]

    def bind(self, x, out, scratch):
        self.x, self.out = x, out
        self.got, self.sums, self.sent, self.came = scratch
        return self

    def arrive(self):
        return pltpu.make_async_remote_copy(
            src_ref=self.x, dst_ref=self.got.at[self.bits], send_sem=self.sent.at[self.bits],
            recv_sem=self.came.at[self.bits], device_id={"section": self.owner}, device_id_type=MESH)

    def hop(self, stage):
        return pltpu.make_async_remote_copy(
            src_ref=self.sums.at[stage], dst_ref=self.got.at[stage], send_sem=self.sent.at[stage],
            recv_sem=self.came.at[stage], device_id={"batch": partner_of(stage)[0]},
            device_id_type=MESH)

    def send_y(self, slots):
        if 0 in slots:
            self.arrive().start()

    def drain_factors(self, slots):
        self.arrive().wait_send()

    def multiply(self, part):
        self.arrive().wait_recv()
        self.sums[0] = self.x[...] + self.got[self.bits]
        self.hop(0).start()

    def advance(self, stage, part):
        self.hop(stage).wait_recv()
        self.sums[stage + 1] = self.sums[stage] + self.got[stage]
        if stage + 1 < self.bits:
            self.hop(stage + 1).start()
        else:
            self.out[...] = self.sums[self.bits]

    def drain(self):
        for stage in range(self.bits):
            self.hop(stage).wait_send()


def greet(bits, near):
    barrier = pltpu.get_barrier_semaphore()
    other = 1 - lax.axis_index("section")
    targets = [{"section": other}]
    targets += [{"batch": partner_of(bit)[0]} for bit in range(bits)]
    targets += [{"section": other, "batch": partner_of(bit)[0]} for bit in near]
    for target in targets:
        pl.semaphore_signal(barrier, inc=1, device_id=target, device_id_type=MESH)
    pl.semaphore_wait(barrier, len(targets))


class Take:
    def __init__(self, refs):
        self.refs, self.at = refs, 0

    def __call__(self, count):
        self.at += count
        return self.refs[self.at - count:self.at]


def residuals(rows, width, hidden):
    heads = width // LM
    return {
        "qkv": ((3, rows, width), BF16), "lm": ((2, LM, width), BF16), "a1": ((rows, width), F32),
        "a2": ((LM, width), F32), "a3": ((LM, heads * rows), F32),
        "band": ((heads // 2, rows, 2 * rows), BF16), "db": ((2, LM, width), BF16),
        "z": ((NEWTON + 1, LM, width), F32), "r": ((NEWTON + 1, LM, width), F32),
        "s": ((NEWTON, LM, width), F32), "t": ((NEWTON, LM, width), F32),
        "hat1": ((rows, width), F32), "hat2": ((rows, width), F32), "rstd": ((rows, 128), F32),
        "slope": ((rows, hidden), BF16)}


def encoder(*refs, names, plans, littles, taps, remote):
    take = Take(refs)
    (lengths_ref,) = take(1)
    input_ref, cotangent_ref, bias_ref, taps_ref = take(4)
    params = take(7)
    own = take(4)
    other_in = () if remote else take(4)
    vec_in = () if remote else take(2)
    act_out, ig_ref = take(2)
    count = len(plans[0])
    outs = take(count) if remote else ()
    small_out = take(1)[0] if remote else None
    other = take(4) if remote else other_in
    layers_out = () if remote else [take(9), take(9)]
    kept = [dict(zip(names, take(len(names)))) for _ in range(2)]
    ring, ring_sem, mid_ref, gi_ref, gr_ref, do_ref = take(6)
    work = take(3)
    (err_ref,) = take(1)
    vecs, tap_rows = take(2)
    section = lax.axis_index("section")
    rows, width = mid_ref.shape
    hidden = own[EXPAND].shape[1]
    chunks, heads = hidden // width, width // LM
    at = 6 + chunks
    err = at + 2 + heads // (width // rows)
    groups = []
    for part, layer in ((forward_groups, 0), (forward_groups, 1), (backward_groups, 1), (backward_groups, 0)):
        groups += part(layer, chunks)
    length = lengths_ref[section]
    if remote:
        factors = [take(7), take(7)]
        smalls = take(2)
        own_sent, own_came, vec_sent, vec_came, share_sent, share_came = take(6)
        scratch = [take(10) for _ in range(count)]
        small_scratch = take(4)
    else:
        factors = [layer[:7] for layer in layers_out]
        smalls = [layer[7] for layer in layers_out]
    x_ref = input_ref.at[pl.ds(section * rows, rows)]
    for layer in range(2):
        kept[layer].update(zip(("act", "first", "att"), factors[layer][:3]))
        smalls[layer][...] = jnp.zeros(smalls[layer].shape, F32)
    ys = [f[3:7] for f in factors]
    pieces = [g for g in forward_groups(0, chunks)]

    def pack(vec, taps_to):
        line = 0
        taps_to[...] = jnp.zeros(taps_to.shape, F32)
        for h in range(heads):
            taps_to[h:h + 1, 0:taps] = taps_ref[h]
        for ref in params + (bias_ref,):
            for c in range(ref.shape[1] // width):
                vec[line:line + 1, :] = ref[:, c * width:(c + 1) * width]
                line += 1

    def weight_copy(i):
        _, w, row, col = pieces[i]
        spot = (pl.ds(row * width, width), pl.ds(col * width, width))
        return pltpu.make_async_remote_copy(
            src_ref=own[w].at[spot], dst_ref=other[w].at[spot], send_sem=own_sent.at[i],
            recv_sem=own_came.at[i], device_id={"section": 1 - section}, device_id_type=MESH)

    def vec_copy(i):
        ref = (vecs, tap_rows)[i]
        return pltpu.make_async_remote_copy(
            src_ref=ref.at[section], dst_ref=ref.at[section], send_sem=vec_sent.at[i],
            recv_sem=vec_came.at[i], device_id={"section": 1 - section}, device_id_type=MESH)

    def vec_wait(i):
        ref = (vecs, tap_rows)[i]
        return pltpu.make_async_remote_copy(
            src_ref=ref.at[1 - section], dst_ref=ref.at[1 - section], send_sem=vec_sent.at[i],
            recv_sem=vec_came.at[i], device_id={"section": 1 - section}, device_id_type=MESH)

    def arrived(group):
        if remote:
            weight_copy(pieces.index((0,) + group[1:])).wait_recv()

    stream = Stream(groups, own, other, ring, ring_sem, arrived)
    if remote:
        items = []
        for layer in range(2):
            x0 = x_ref if layer == 0 else mid_ref
            f = factors[layer]
            xs, yy = (f[0], f[1], x0, f[2]), (f[3], f[4], f[6], f[5])
            items.append([w.bind(xs[i], yy[i], outs[i], scratch[i])
                          for i, w in enumerate(plans[layer])]
                         + [littles[layer].bind(smalls[layer], small_out, small_scratch)])
        greet(littles[0].bits, sorted({w.order[0] for w in plans[0]}))
        pack(vecs.at[section], tap_rows.at[section])
        for i in range(2):
            vec_copy(i).start()
        for i in range(3):
            weight_copy(i).start()
        stream.start(1)
        for i in range(2):
            vec_wait(i).wait_recv()
    else:
        vecs[...] = vec_in[0][...]
        tap_rows[...] = vec_in[1][...]

    def send(layer, which, what):
        if remote:
            for role, slots in ((section == layer, (1,)), (section != layer, (0, 2))):
                @pl.when(role)
                def _():
                    for i in which:
                        getattr(items[layer][i], what)(slots)

    def run(layer, *jobs):
        if remote:
            @pl.when(section == layer)
            def _():
                for item, stage, part in jobs:
                    if stage is None:
                        items[layer][item].multiply(part)
                    else:
                        items[layer][item].advance(stage, part)

    def both_rows(k, layer, source, target):
        def copy():
            return pltpu.make_async_remote_copy(
                src_ref=source, dst_ref=target.at[pl.ds((1 - layer) * rows, rows)],
                send_sem=share_sent.at[k], recv_sem=share_came.at[k],
                device_id={"section": layer}, device_id_type=MESH)

        if remote:
            @pl.when(section == layer)
            def _():
                target[layer * rows:(layer + 1) * rows, :] = source[...]

            @pl.when(section != layer)
            def _():
                copy().start()
        else:
            target[layer * rows:(layer + 1) * rows, :] = source[...]
        return copy

    def schedule(name, slot):
        steps = SCHEDULE.get((name, slot), ())
        for step in steps:
            if step[0] == "x":
                send(step[1], step[2], "send_x")
            elif step[0] == "y":
                send(step[1], step[2], "send_y")
            else:
                run(step[1], *step[2])

    def hook(name, slot):
        if name == "forward0" and slot == 0 and remote:
            for i in range(3):
                weight_copy(i).wait_send()
            for i in range(3, len(pieces)):
                weight_copy(i).start()
        if name == "forward0" and slot == 1:
            stream.flow()
        schedule(name, slot)

    per_layer = len(forward_groups(0, chunks))
    x = x_ref[...]
    shared = []
    for layer in range(2):
        vec = vecs[layer]
        bias = (vec[at:at + 1], None, vec[at + 1:at + 2])
        name = "forward" + str(layer)
        attention_forward(
            length, x, bias, tap_rows.at[layer], kept[layer], (smalls[layer], err, err_ref), stream,
            layer * per_layer, functools.partial(hook, name), taps)
        out = post_forward(length, x, vec, kept[layer], stream, layer * per_layer + 3)
        mid_or_out = mid_ref if layer == 0 else gi_ref.at[2]
        mid_or_out[...] = out
        shared.append((layer, both_rows(layer, layer, mid_or_out, act_out)))
        schedule(name, 3)
        x = out
    g = cotangent_ref[pl.ds(section * rows, rows), :]
    group = 2 * per_layer
    for layer in (1, 0):
        name = "backward" + str(layer)
        y = ys[layer]
        post_backward(
            length, g, kept[layer], vecs[layer], (y[0], y[1], y[2]), gr_ref, do_ref, smalls[layer],
            stream, group, functools.partial(schedule, "post" + str(layer)))
        g = attention_backward(
            length, do_ref, gr_ref, kept[layer], y[3], smalls[layer], at, work, stream,
            group + 1 + 2 * chunks, functools.partial(schedule, name), taps)
        gi_ref[layer] = g
        shared.append((layer, both_rows(2 + layer, layer, gi_ref.at[layer], ig_ref)))
        schedule(name, 7)
        group += per_layer
    if remote:
        schedule("tail", 0)
        for layer in range(2):
            @pl.when(section == layer)
            def _():
                for item in items[layer]:
                    item.drain()

            @pl.when(section != layer)
            def _():
                for item in items[layer]:
                    item.drain_factors((0, 2))
        for k, (layer, copy) in enumerate(shared):
            @pl.when(section == layer)
            def _():
                copy().wait_recv()

            @pl.when(section != layer)
            def _():
                copy().wait_send()
        for i in range(3, len(pieces)):
            weight_copy(i).wait_send()
        for i in range(2):
            vec_copy(i).wait_send()
    else:
        for layer in range(2):
            layers_out[layer][8][...] = gi_ref[2] if layer else mid_ref[...]


RED, EXP, PRO, PUT, SMALL = range(5)


def steps(layer, *jobs):
    return ("run", layer, jobs)


def mult(item, *parts):
    return tuple((item, None, part) for part in parts)


SCHEDULE = {
    ("forward0", 0): [("x", 0, (PRO,))],
    ("forward0", 2): [("x", 0, (PUT,))],
    ("forward0", 3): [("x", 1, (PRO,)), ("x", 0, (RED, EXP))],
    ("forward1", 2): [("x", 1, (PUT,))],
    ("forward1", 3): [("x", 1, (RED, EXP))],
    ("post1", 0): [("y", 1, (RED,))],
    ("post1", 4): [("y", 1, (EXP,))],
    ("post1", 5): [("y", 1, (PUT,))],
    ("backward1", 0): [steps(1, (RED, None, 0), (RED, None, 1))],
    ("backward1", 1): [steps(1, (PUT, None, 0))],
    ("backward1", 2): [steps(1, (EXP, None, 0))],
    ("backward1", 3): [steps(1, (RED, 0, 0), (PUT, 0, 0), (EXP, None, 1))],
    ("backward1", 6): [("y", 1, (PRO, SMALL,)), steps(1, (RED, 0, 1), (SMALL, None, 0), (RED, 1, 0), (EXP, 0, 0), (PUT, 1, 0))],
    ("post0", 0): [("y", 0, (RED,)), steps(1, (PRO, None, 0))],
    ("post0", 1): [steps(1, (RED, 1, 1), (PRO, None, 1), (RED, 2, 0), (SMALL, 0, 0), (PRO, None, 2), (EXP, 0, 1), (PUT, 2, 0))],
    ("post0", 3): [steps(1, (EXP, 1, 0))],
    ("post0", 4): [("y", 0, (EXP,)), steps(1, (RED, 2, 1))],
    ("post0", 5): [("y", 0, (PUT,))],
    ("backward0", 0): [steps(1, (PRO, 0, 0), (EXP, 1, 1), (PUT, 3, 0))],
    ("backward0", 1): [steps(1, (PRO, 0, 1), (EXP, 2, 0), (SMALL, 1, 0))],
    ("backward0", 2): [steps(1, (PRO, 0, 2), (EXP, 2, 1), (PRO, 1, 0)), steps(0, (RED, None, 0), (RED, None, 1))],
    ("backward0", 3): [steps(1, (EXP, 3, 0), (PRO, 1, 1), (SMALL, 2, 0), (PRO, 2, 0))],
    ("backward0", 5): [steps(1, (PRO, 2, 1))],
    ("backward0", 6): [("y", 0, (PRO, SMALL,)), steps(1, (EXP, 3, 1), (SMALL, 3, 0), (PRO, 1, 2), (PRO, 3, 0)), steps(0, (EXP, None, 0))],
    ("backward0", 7): [steps(0, (EXP, None, 1))],
    ("tail", 0): [steps(1, (PRO, 3, 1), (PRO, 2, 2), (PRO, 3, 2)), steps(0, (RED, 0, 0), (EXP, 0, 0), (RED, 0, 1), (PUT, None, 0), (RED, 1, 0), (EXP, 0, 1), (SMALL, None, 0), (RED, 2, 0), (EXP, 1, 0), (PUT, 0, 0), (PRO, None, 0), (RED, 1, 1), (PRO, None, 1), (PRO, None, 2), (EXP, 2, 0), (EXP, 1, 1), (PUT, 1, 0), (PRO, 0, 0), (SMALL, 0, 0), (RED, 2, 1), (EXP, 3, 0), (PRO, 0, 1), (EXP, 2, 1), (PRO, 0, 2), (PRO, 1, 0), (PUT, 2, 0), (SMALL, 1, 0), (PRO, 1, 1), (EXP, 3, 1), (PUT, 3, 0), (PRO, 1, 2), (PRO, 2, 0), (SMALL, 2, 0), (PRO, 2, 1), (PRO, 3, 0), (PRO, 2, 2), (PRO, 3, 1), (SMALL, 3, 0), (PRO, 3, 2))],
}


def shape(dims, kind=F32):
    return jax.ShapeDtypeStruct(dims, kind)


IN_VMEM = pl.BlockSpec(memory_space=pltpu.VMEM)
IN_SMEM = pl.BlockSpec(memory_space=pltpu.SMEM)
ANYWHERE = pl.BlockSpec(memory_space=pl.ANY)
VMEM_LIMIT = 62 * 2 ** 20
RING = 6


def plan(owner, bits):
    tail = tuple(range(3, bits))
    return [Weight(owner, (1, 0, 2) + tail, True, 2), Weight(owner, (2, 1, 0) + tail, False, 2),
            Weight(owner, (0, 1, 2) + tail, False, 3), Weight(owner, (0, 1, 2) + tail, False, 1)]


def small_shape(width, hidden, heads, rows):
    lines = 6 + hidden // width + 2 + heads // (width // rows) + NEWTON
    return (lines + 7) // 8 * 8, width


def encode(remote, batch, lengths, layer_input, cotangent, bias, conv_kernel, params, weights, extra):
    rows, width = layer_input.shape[0] // 2, layer_input.shape[1]
    hidden, heads = weights[EXPAND].shape[1], width // LM
    chunks, bits = hidden // width, batch.bit_length() - 1
    dma = pltpu.SemaphoreType.DMA
    low = lambda n: ((rows, n), BF16)
    factor_shapes = [low(hidden), low(width), low(width), low(width), low(hidden), low(width), low(3 * width)]
    x_shapes = [(rows, n) for n in (hidden, width, width, width)]
    y_shapes = [(rows, n) for n in (width, hidden, 3 * width, width)]
    dims = small_shape(width, hidden, heads, rows)
    plans = littles = None
    plans, littles = [], []
    for layer in range(2):
        plans.append([w.sizes(a, b) for w, a, b in zip(plan(layer, bits), x_shapes, y_shapes)])
        littles.append(Small(layer, bits))
    both = shape((2 * rows, width), BF16)
    outs, out_specs = [both, both], [IN_VMEM] * 2
    if remote:
        outs += [shape((w.block, w.width)) for w in plans[0]] + [shape(dims)]
        out_specs += [IN_VMEM] * 5
        outs += [shape(w.shape, BF16) for w in weights]
        out_specs += [ANYWHERE] * 4
    else:
        for _ in range(2):
            outs += [shape(*f) for f in factor_shapes] + [shape(dims), shape((rows, width), BF16)]
            out_specs += [IN_VMEM] * 9
    names = residuals(rows, width, hidden)
    scratch = [pltpu.VMEM(*s) for _ in range(2) for s in names.values()]
    scratch += [pltpu.VMEM((RING, width, width), BF16), dma((RING,)), pltpu.VMEM(*low(width)),
                pltpu.VMEM((3, rows, width), BF16), pltpu.VMEM((rows, width), F32),
                pltpu.VMEM((rows, width), F32)]
    scratch += [pltpu.VMEM((LM, width), F32)] * 3 + [pltpu.VMEM((NEWTON, 1, width), F32)]
    scratch += [pltpu.VMEM((2, 16, width), F32), pltpu.VMEM((2, 16, 128), F32)]
    if remote:
        pieces = 4 + 2 * chunks
        scratch += [pltpu.VMEM(*f) for _ in range(2) for f in factor_shapes]
        scratch += [pltpu.VMEM(dims, F32)] * 2
        scratch += [dma((pieces,)), dma((pieces,)), dma((2,)), dma((2,)), dma((4,)), dma((4,))]
        scratch += [s for w in plans[0] for s in w.scratch()] + littles[0].scratch(dims)
    args = (lengths, layer_input, cotangent, bias, conv_kernel) + params + weights + extra
    ins = [IN_SMEM] + [IN_VMEM] * 11 + [ANYWHERE] * 4
    if not remote:
        ins += [ANYWHERE] * 4 + [IN_VMEM] * 2
    marks = dict(collective_id=0, has_side_effects=True) if remote else {}
    return pl.pallas_call(
        functools.partial(encoder, names=tuple(names), plans=plans, littles=littles,
                          taps=conv_kernel.shape[-1], remote=remote),
        out_shape=tuple(outs), in_specs=ins, out_specs=tuple(out_specs), scratch_shapes=scratch,
        name="encoder", cost_estimate=pl.CostEstimate(
            flops=2 * 10 ** 10, bytes_accessed=10 ** 8, transcendentals=0),
        compiler_params=pltpu.CompilerParams(vmem_limit_bytes=VMEM_LIMIT, **marks))(*args)


def finish(act, ig, red, exp, pro, put, small_ref, *refs, taps):
    whole, rest, sem = refs[:6], refs[6:-1], refs[-1]
    copies = [pltpu.make_async_copy(a, b, sem.at[i])
              for i, (a, b) in enumerate(zip((act, ig, pro, put, exp, red), whole))]
    for copy in copies:
        copy.start()
    bias, conv, out_bias, gain1, shift1, up_bias, down_bias, gain2, shift2, proxies = rest
    width = small_ref.shape[1]
    chunks = exp.shape[1] // width
    rows, heads = act.shape[0] // 2, conv.shape[0]
    at, per_row = 6 + chunks, width // rows
    batch = width // out_bias.shape[1]
    index = lax.axis_index("batch")
    small = small_ref[...]
    turned = {}

    def share(out, first, many):
        size = out.shape[1]
        if size not in turned:
            turned[size] = pltpu.roll(small, lax.rem(width - lax.rem(index * size, width), width), 1)
        line = index * size // width
        value = turned[size][first:first + 1]
        for r in range(1, many):
            value = jnp.where(line == r, turned[size][first + r:first + r + 1], value)
        out[...] = value[:, :size]

    share(bias, at, 2)
    for out, first, many in ((out_bias, 0, 1), (gain1, 1, 1), (shift1, 2, 1), (up_bias, 3, chunks),
                             (down_bias, 3 + chunks, 1), (gain2, 4 + chunks, 1), (shift2, 5 + chunks, 1)):
        share(out, first, many)
    for h in range(heads):
        line, lane = at + 2 + h // per_row, h % per_row * rows
        conv[h] = small[line:line + 1, lane:lane + taps]
    end = at + 2 + heads // per_row
    sums = jnp.sum(small[end:end + NEWTON], axis=1, keepdims=True)
    spot = lax.broadcasted_iota(jnp.int32, (1, NEWTON), 1)
    value = jnp.zeros((1, NEWTON), F32)
    for i in range(NEWTON):
        value = jnp.where(spot == i, sums[i:i + 1], value)
    proxies[...] = value
    for copy in copies:
        copy.wait()


def finish_call(results, batch, width, hidden, heads, taps):
    act, ig, red, exp, pro, put, small = results
    part = lambda n: shape((1, n // batch))
    outs = [jax.ShapeDtypeStruct(r.shape, r.dtype) for r in (act, ig, pro, put, exp, red)]
    outs += [part(2 * width), shape((heads, 1, taps)), part(width), part(width), part(width),
             part(hidden), part(width), part(width), part(width), shape((1, NEWTON))]
    return pl.pallas_call(
        functools.partial(finish, taps=taps), out_shape=tuple(outs),
        in_specs=[ANYWHERE] * 6 + [IN_VMEM], out_specs=tuple([ANYWHERE] * 6 + [IN_VMEM] * 10),
        scratch_shapes=[pltpu.SemaphoreType.DMA((6,))], name="finish")(
            act, ig, red, exp, pro, put, small)


def swap(value):
    return lax.ppermute(value, "section", [(0, 1), (1, 0)])


def encode_apart(batch, args, weights, params, bias, conv_kernel):
    section = lax.axis_index("section")
    width = args[1].shape[1]
    heads, _, taps = conv_kernel.shape
    vec = jnp.concatenate([p.reshape(-1, width) for p in params + (bias,)])
    vec = jnp.pad(vec, ((0, 16 - vec.shape[0]), (0, 0)))
    rows_of_taps = jnp.pad(conv_kernel[:, 0], ((0, 16 - heads), (0, 128 - taps)))
    extra = [swap(w) for w in weights]
    for mine in (vec, rows_of_taps):
        theirs = swap(mine)
        extra.append(jnp.where(section == 0, jnp.stack([mine, theirs]), jnp.stack([theirs, mine])))
    result = encode(False, batch, *args, bias, conv_kernel, params, weights, tuple(extra))
    total = args[1].shape[0]
    rows = total // 2
    layers = [result[2:11], result[11:20]]
    inputs = [lax.dynamic_slice_in_dim(args[1], section * rows, rows, 0), layers[0][8]]
    shares = []
    for layer in range(2):
        act, first, att, gd, gu, gp, dqkv, small, _ = layers[layer]
        products = [lax.dot_general(x, y, (((0,), (0,)), ((), ())), preferred_element_type=F32)
                    for x, y in ((act, gd), (first, gu), (inputs[layer], dqkv), (att, gp))]
        shares.append([
            lax.psum_scatter(lax.psum(p, "section"), "batch", scatter_dimension=0, tiled=True)
            for p in products] + [lax.psum(small, ("section", "batch"))])
    lead = section == 0
    both = []
    for k in range(2):
        by_layer = [result[k][:rows], result[k][rows:]]
        crossed = swap(jnp.where(lead, by_layer[1], by_layer[0]))
        both.append(jnp.where(lead, jnp.concatenate([by_layer[0], crossed]),
                              jnp.concatenate([crossed, by_layer[1]])))
    return both + [jnp.where(lead, a, b) for a, b in zip(*shares)]


def body(
    layer_input, seq_lengths, cotangent, project_weight, project_bias, conv_kernel, output_weight,
    output_bias, attn_gain, attn_shift, expand_weight, expand_bias, reduce_weight, reduce_bias,
    final_gain, final_shift):
    batch = lax.axis_size("batch")
    width = layer_input.shape[1]
    heads, taps = conv_kernel.shape[1:]
    weights = (project_weight[0], output_weight[0], expand_weight[0], reduce_weight[0])
    params = (output_bias, attn_gain, attn_shift, expand_bias, reduce_bias, final_gain, final_shift)
    args = (seq_lengths, layer_input, cotangent)
    conv_kernel = conv_kernel.transpose(1, 0, 2)
    if batch >= 8 and all(w.shape[0] // batch % 16 == 0 for w in weights):
        result = encode(True, batch, *args, project_bias, conv_kernel, params, weights, ())
    else:
        result = encode_apart(batch, args, weights, params, project_bias, conv_kernel)
    hidden = reduce_weight.shape[1]
    act, ig, pro, put, exp, red, bias, conv, *rest = finish_call(
        result[:7], batch, width, hidden, heads, taps)
    out_bias, gain1, shift1, up_bias, down_bias, gain2, shift2, proxies = rest
    return (
        act[None], ig[None], pro[None], bias, conv.transpose(1, 0, 2), put[None], out_bias, gain1,
        shift1, exp[None], up_bias, red[None], down_bias, gain2, shift2, proxies)


def solution(mesh):
    split_rows = P("batch", None)
    two, three = P("section", None), P("section", None, None)
    return jax.shard_map(
        body, mesh=mesh,
        in_specs=(split_rows, P("batch"), split_rows, three, two, three, three, two, two, two,
                  three, two, three, two, two, two),
        out_specs=(P("section", "batch", None), P("section", "batch", None),
                   P("section", "batch", None), P("section", "batch"), three,
                   P("section", "batch", None), P("section", "batch"), P("section", "batch"),
                   P("section", "batch"), P("section", "batch", None), P("section", "batch"),
                   P("section", "batch", None), P("section", "batch"), P("section", "batch"),
                   P("section", "batch"), two),
        check_vma=False)
```

```python
import functools
import math

import jax
import jax.numpy as jnp
from jax import lax
from jax.experimental import pallas as pl
from jax.experimental.pallas import tpu as pltpu
from jax.sharding import PartitionSpec as P

F32 = jnp.float32
BF16 = jnp.bfloat16
NEWTON = 6
LM = 64
PAIR = 128
EPS = 1e-05
MESH = pl.DeviceIdType.MESH
QKV, OUT, EXPAND, REDUCE = range(4)


def nn(a, b):
    return lax.dot_general(a, b, (((1,), (0,)), ((), ())), preferred_element_type=F32)


def nt(a, b):
    return lax.dot_general(a, b, (((1,), (1,)), ((), ())), preferred_element_type=F32)


def tn(a, b):
    return lax.dot_general(a, b, (((0,), (0,)), ((), ())), preferred_element_type=F32)


def split(x):
    high = x.astype(BF16)
    return high, (x - high.astype(F32)).astype(BF16)


def cat(parts, axis):
    return jnp.concatenate(parts, axis=axis)


def lane_is_first(rows, width=PAIR):
    return lax.broadcasted_iota(jnp.int32, (rows, width), 1) < width // 2


def spread(y):
    rows = y.shape[0]
    keep = lane_is_first(rows).astype(F32).astype(y.dtype)
    return cat([y * keep, y * (1 - keep)], 0)


def pick(x):
    rows = x.shape[0] // 2
    return jnp.where(lane_is_first(rows), x[:rows], x[rows:])


def nn3(xs, ys):
    (xh, xl), (yh, yl) = xs, ys
    dh, dl = spread(yh), spread(yl)
    return nn(cat([xh, xl], 1), cat([dh, dh], 0)) + nn(xh, dl)


def nt3(xs, ds):
    (xh, xl), (dh, dl) = xs, ds
    return nt(cat([xh, xl], 1), cat([dh, dh], 1)) + nt(xh, dl)


def half_sums(x, ones):
    high, low = split(x)
    return nn(high, ones) + nn(low, ones)


def block_ones():
    row = lax.broadcasted_iota(jnp.int32, (PAIR, PAIR), 0) < LM
    col = lax.broadcasted_iota(jnp.int32, (PAIR, PAIR), 1) < LM
    return (row == col).astype(F32).astype(BF16)


def pair_softmax(scores, ones):
    first = lane_is_first(scores.shape[0])
    top_a = jnp.max(jnp.where(first, scores, -jnp.inf), axis=1, keepdims=True)
    top_b = jnp.max(jnp.where(first, -jnp.inf, scores), axis=1, keepdims=True)
    e = jnp.exp(scores - jnp.where(first, top_a, top_b))
    return e / half_sums(e, ones)


def pair_transpose(x):
    t = x.T
    return cat([t[:LM], t[LM:]], 1)


def pair_eye():
    row = lax.broadcasted_iota(jnp.int32, (LM, PAIR), 0)
    col = lax.broadcasted_iota(jnp.int32, (LM, PAIR), 1)
    return (row == col % LM).astype(F32)


def pool_matrix(length, rows):
    landmark = lax.broadcasted_iota(jnp.int32, (LM, rows), 0)
    row = lax.broadcasted_iota(jnp.int32, (LM, rows), 1)
    segment = length // LM
    inside = (row >= landmark * segment) & (row < (landmark + 1) * segment)
    weight = 1.0 / jnp.full((LM, rows), segment, jnp.int32).astype(F32)
    return jnp.where(inside, weight, 0.0).astype(BF16)


def toeplitz(taps_row, rows, taps):
    half = taps // 2
    wide = jnp.broadcast_to(taps_row, (rows, rows))
    wide = pltpu.roll(wide, rows - half, 1, stride=1, stride_axis=0)
    row = lax.broadcasted_iota(jnp.int32, (rows, rows), 0)
    col = lax.broadcasted_iota(jnp.int32, (rows, rows), 1)
    near = (col - row <= half) & (row - col <= half)
    return jnp.where(near, wide, 0.0)


def attention_forward(
    length, x, bias, taps_ref, kept, err_at, work, stream, group, hook, taps):
    low_ref, lm_low_ref, digest_low_ref, conv_ref = work
    rows, width = x.shape
    pairs = width // PAIR
    z_ref, r_ref, s_ref, t_ref = kept["z"], kept["r"], kept["s"], kept["t"]
    a1_ref, a2_ref, a3_ref, band_ref = kept["a1"], kept["a2"], kept["a3"], kept["band"]
    qkv_ref, lm_ref, db_ref = kept["qkv"], kept["lm"], kept["db"]
    ones = block_ones()
    pool = pool_matrix(length, rows)
    eye = pair_eye()
    sl = [pl.ds(p * PAIR, PAIR) for p in range(pairs)]
    valid = (lax.broadcasted_iota(jnp.int32, (rows, width), 0) < length).astype(F32)
    scale = LM ** (-0.25)
    qkv = []
    for i in range(3):
        y = nn(x, stream.take(group + i))
        if bias[i] is not None:
            y = y + bias[i]
        qkv.append(y * (valid * scale if i < 2 else valid))
        stream.release(group + i)
    for i in range(3):
        high, rest = split(qkv[i])
        qkv_ref[i] = high
        low_ref[i] = rest
    qls, kls = [], []
    for i, into in ((0, qls), (1, kls)):
        for p in range(pairs):
            high, rest = split(nn(pool, qkv_ref[i, :, sl[p]]) + nn(pool, low_ref[i, :, sl[p]]))
            lm_ref[i, :, sl[p]] = high
            lm_low_ref[i, :, sl[p]] = rest
            into.append((high, rest))
    kld = [(spread(h), spread(l)) for h, l in kls]
    for p in range(pairs):
        a2_ref[:, sl[p]] = pair_softmax(nt3(qls[p], kld[p]), ones)
    first = lane_is_first(LM)
    for p in range(pairs):
        a = a2_ref[:, sl[p]]
        squares = jnp.sum(a * a, axis=0, keepdims=True)
        fro_a = jnp.sum(jnp.where(first[:1], squares, 0.0), axis=1, keepdims=True)
        fro_b = jnp.sum(jnp.where(first[:1], 0.0, squares), axis=1, keepdims=True)
        z_ref[0, :, sl[p]] = pair_transpose(a) / jnp.where(first[:1], fro_a, fro_b)
    for p in range(pairs):
        z = split(z_ref[0, :, sl[p]])
        r_ref[0, :, sl[p]] = eye - nn3(split(a2_ref[:, sl[p]]), z)
    hook(0)
    small_ref, line, err_ref = err_at

    def beside(p):
        lanes = pl.ds(pl.multiple_of(p * PAIR, PAIR), PAIR)
        q, k, v = [(qkv_ref[i, :, lanes], low_ref[i, :, lanes]) for i in range(3)]
        ql, kl = [(lm_ref[i, :, lanes], lm_low_ref[i, :, lanes]) for i in range(2)]
        score1 = nt3(q, (spread(kl[0]), spread(kl[1])))
        score3 = nt3(ql, (spread(k[0]), spread(k[1])))
        vh, vl = spread(v[0]), spread(v[1])
        band = cat([toeplitz(taps_ref[2 * p + j], rows, taps) for j in range(2)], 1)
        th, tl = split(band)
        band_ref[p] = th
        conv_ref[:, lanes] = nn(cat([th, tl], 1), cat([vh, vh], 0)) + nn(th, vl)
        yield
        a1_ref[:, lanes] = pair_softmax(score1, ones)
        key = lax.broadcasted_iota(jnp.int32, (LM, rows), 1)
        halves = []
        for j in range(2):
            sc = jnp.where(key < length, score3[:, j * rows:(j + 1) * rows], -1e30)
            e = jnp.exp(sc - jnp.max(sc, axis=1, keepdims=True))
            halves.append(e / jnp.sum(e, axis=1, keepdims=True))
        a3 = cat(halves, 1)
        a3_ref[:, pl.ds(pl.multiple_of(p * 2 * rows, 2 * rows), 2 * rows)] = a3
        yield
        a3h, a3l = split(a3)
        high, rest = split(nn(a3h, vh) + (nn(a3l, vh) + nn(a3h, vl)))
        db_ref[0, :, lanes] = high
        digest_low_ref[:, lanes] = rest
        yield

    each = -(-pairs // NEWTON)

    def newton_step(step, carry):
        s_all, t_all, z_all = [], [], []
        others = [beside(jnp.minimum(step * each + j, pairs - 1)) for j in range(each)]

        def fill():
            for other in others:
                next(other)

        for p in range(pairs):
            r = r_ref[step, :, sl[p]]
            rs = split(r)
            s = nn3(rs, rs)
            s_ref[step, :, sl[p]] = s
            s_all.append((r, rs, s))
        fill()
        for p in range(pairs):
            r, rs, s = s_all[p]
            t = nn3(split(s), rs)
            t_ref[step, :, sl[p]] = t
            t_all.append(eye + r + s + 0.25 * t)
        fill()
        for p in range(pairs):
            zn = nn3(split(z_ref[step, :, sl[p]]), split(t_all[p]))
            z_ref[step + 1, :, sl[p]] = zn
            z_all.append(zn)
        fill()
        for p in range(pairs):
            rn = eye - nn3(split(a2_ref[:, sl[p]]), split(z_all[p]))
            r_ref[step + 1, :, sl[p]] = rn
            err_ref[step, :, sl[p]] = jnp.sum(rn * rn, axis=0, keepdims=True)
        return carry

    lax.fori_loop(0, NEWTON, newton_step, 0)
    for i in range(NEWTON):
        small_ref[line + i:line + i + 1, :] = err_ref[i]
    hook(1)
    blended = []
    for p in range(pairs):
        z = split(z_ref[NEWTON, :, sl[p]])
        bs = split(nn3(z, (db_ref[0, :, sl[p]], digest_low_ref[:, sl[p]])))
        db_ref[1, :, sl[p]] = bs[0]
        blended.append(bs)
    for p in range(pairs):
        o = nn3(split(a1_ref[:, sl[p]]), blended[p]) + conv_ref[:, sl[p]]
        kept["att"][:, sl[p]] = o.astype(BF16)
    hook(2)


def norm_forward(values):
    center = values - jnp.mean(values, axis=1, keepdims=True)
    rstd = lax.rsqrt(jnp.mean(center * center, axis=1, keepdims=True) + EPS)
    return center * rstd, rstd


def norm_back(grad, hat, rstd):
    mean = jnp.mean(grad, axis=1, keepdims=True)
    slope = jnp.mean(grad * hat, axis=1, keepdims=True)
    return rstd * (grad - mean - hat * slope)


def normal_law(u):
    e = jnp.exp(-0.5 * u * u)
    t = 1.0 / (1.0 + 0.231641888 * jnp.abs(u))
    tail = e * (t * (0.127414796 + t * (-0.142248368 + t * (
        0.7107068705 + t * (-0.7265760135 + t * 0.5307027145)))))
    return jnp.where(u < 0.0, tail, 1.0 - tail), e * 0.3989422804014327


def post_forward(length, x, vec, kept, stream, group):
    rows, width = x.shape
    chunks = kept["act"].shape[1] // width
    row = lambda i: vec[i:i + 1, :]
    hidden = x.astype(F32) + (nn(kept["att"][...], stream.take(group)) + row(0))
    stream.release(group)
    hat, rstd = norm_forward(hidden)
    kept["hat1"][...] = hat
    kept["rstd"][:, 0:1] = rstd
    first = hat * row(1) + row(2)
    low = first.astype(BF16)
    kept["first"][...] = low
    down = first + row(3 + chunks)
    for c in range(chunks):
        lanes = slice(c * width, (c + 1) * width)
        up = nn(low, stream.take(group + 1 + 2 * c)) + row(3 + c)
        stream.release(group + 1 + 2 * c)
        cdf, density = normal_law(up)
        act = (up * cdf).astype(BF16)
        slope = cdf + up * density
        kept["slope"][:, lanes] = slope.astype(kept["slope"].dtype)
        kept["act"][:, lanes] = act
        down = down + nn(act, stream.take(group + 2 + 2 * c))
        stream.release(group + 2 + 2 * c)
    hat, rstd = norm_forward(down)
    kept["hat2"][...] = hat
    kept["rstd"][:, 1:2] = rstd
    valid = lax.broadcasted_iota(jnp.int32, (rows, width), 0) < length
    return jnp.where(valid, hat * row(4 + chunks) + row(5 + chunks), 0.0).astype(BF16)


def softmax_back(a, da, ones):
    return a * (da - half_sums(a * da, ones))


def attention_backward(
    length, do_ref, gr_ref, kept, dqkv_ref, small_ref, at, work, stream, group, hook, taps):
    dz_ref, dr_ref, da_ref, dd_ref, dq_ref, dk_ref, dql_ref, dkl_ref, dtaps_ref = work
    a1_ref, a2_ref, a3_ref, band_ref = kept["a1"], kept["a2"], kept["a3"], kept["band"]
    qkv_ref, lm_ref, db_ref = kept["qkv"], kept["lm"], kept["db"]
    rows, width = do_ref.shape
    pairs = width // PAIR
    ones = block_ones()
    eye = pair_eye()
    pool = pool_matrix(length, rows)
    sl = [pl.ds(p * PAIR, PAIR) for p in range(pairs)]
    for p in range(pairs):
        a1 = a1_ref[:, sl[p]].astype(BF16)
        dbh = pick(tn(a1, do_ref[:, sl[p]])).astype(BF16)
        z = kept["z"][NEWTON, :, sl[p]].astype(BF16)
        dz_ref[:, sl[p]] = nt(dbh, spread(db_ref[0, :, sl[p]]))
        dr_ref[:, sl[p]] = jnp.zeros((LM, PAIR), F32)
        dd_ref[:, sl[p]] = pick(tn(z, dbh)).astype(BF16)
    hook(0)

    scale = LM ** (-0.25)
    valid = (lax.broadcasted_iota(jnp.int32, (rows, PAIR), 0) < length).astype(F32)
    half = taps // 2
    row = lax.broadcasted_iota(jnp.int32, (rows, rows), 0)
    col = lax.broadcasted_iota(jnp.int32, (rows, rows), 1)
    flip = (row + col == rows - 1).astype(F32).astype(BF16)
    near = (col + row <= rows - 1 + half) & (col + row >= rows - 1 - half)

    def beside(p):
        at_lane = lambda start, size: pl.ds(pl.multiple_of(start + p * size, PAIR), size)
        lanes = at_lane(0, PAIR)
        do = do_ref[:, lanes]
        q, k, v = [qkv_ref[i, :, lanes] for i in range(3)]
        ql, kl = lm_ref[0, :, lanes], lm_ref[1, :, lanes]
        a3 = a3_ref[:, at_lane(0, 2 * rows)]
        dd = dd_ref[:, lanes]
        turned = nn(flip, do).astype(BF16)
        da1 = nt(do, spread(db_ref[1, :, lanes]))
        da3 = nt(dd, spread(v))
        dv = pick(tn(cat([a3.astype(BF16), band_ref[p]], 0), cat([dd, do], 0)))
        dqkv_ref[:, at_lane(2 * width, PAIR)] = (dv * valid).astype(BF16)
        yield
        ds1 = softmax_back(a1_ref[:, lanes], da1, ones).astype(BF16)
        parts = []
        for j in range(2):
            a, d = a3[:, j * rows:(j + 1) * rows], da3[:, j * rows:(j + 1) * rows]
            parts.append(a * (d - jnp.sum(a * d, axis=1, keepdims=True)))
        ds3 = cat(parts, 1).astype(BF16)
        full = nt(spread(turned), v)
        for j in range(2):
            m = jnp.where(near, full[j * rows:(j + 1) * rows], 0.0)
            m = pltpu.roll(m, half + 1, 1, stride=1, stride_axis=0)
            dtaps_ref[2 * p + j] = jnp.sum(m, axis=0, keepdims=True)
        yield
        dq_ref[:, lanes] = nn(ds1, spread(kl))
        dk_ref[:, lanes] = pick(tn(ds3, ql))
        dql_ref[:, lanes] = nn(ds3, spread(k))
        dkl_ref[:, lanes] = pick(tn(ds1, q))
        yield

    each = -(-pairs // NEWTON)

    def newton_back(index, carry):
        step = NEWTON - 1 - index
        keep = []
        others = [beside(jnp.minimum(index * each + j, pairs - 1)) for j in range(each)]

        def fill():
            for other in others:
                next(other)

        for p in range(pairs):
            z = kept["z"][step, :, sl[p]]
            zh, zl = split(z)
            dz = dz_ref[:, sl[p]]
            gh, gl = split(dz)
            full = tn(cat([zh, zh, zl], 0), cat([gh, gl, gh], 0))
            df = pick(full + full.T) * 0.5
            keep.append((df, (gh, gl)))
        fill()
        for p in range(pairs):
            df, g = keep[p]
            r, s, t = [kept[n][step, :, sl[p]] for n in ("r", "s", "t")]
            dz_ref[:, sl[p]] = nn3(g, split(eye + r + s + 0.25 * t))
            dr = dr_ref[:, sl[p]]
            dt = 0.25 * df + 0.75 * dr
            rs, ss, dts, drs = split(r), split(s), split(dt), split(0.5 * dr)
            m = nn3(dts, rs) + nn3(drs, ss)
            keep[p] = (df, dts, m, rs, ss)
        fill()
        for p in range(pairs):
            df, dts, m, rs, ss = keep[p]
            ds = 2.0 * df + (m + pair_transpose(m))
            m = nn3(dts, ss) + nn3(split(ds), rs)
            dr_ref[:, sl[p]] = df + 0.5 * (m + pair_transpose(m))
        fill()
        return carry

    for third in range(3):
        lax.fori_loop(third * NEWTON // 3, (third + 1) * NEWTON // 3, newton_back, 0)
        hook(1 + third)
    first = lane_is_first(1)
    for p in range(pairs):
        a = a2_ref[:, sl[p]]
        turned = pair_transpose(a)
        dz = dz_ref[:, sl[p]]
        g = nn3(split(dr_ref[:, sl[p]]), split(a))

        def halves(m):
            c = jnp.sum(m, axis=0, keepdims=True)
            ca = jnp.sum(jnp.where(first, c, 0.0), axis=1, keepdims=True)
            cb = jnp.sum(jnp.where(first, 0.0, c), axis=1, keepdims=True)
            return jnp.where(first, ca, cb)

        inv = 1.0 / halves(a * a)
        dc = halves(dz * turned) - halves(g * a)
        da_ref[:, sl[p]] = inv * (pair_transpose(dz) - 2.0 * g) - (2.0 * dc * inv * inv) * a
    hook(4)
    per_row = width // rows
    for p in range(pairs):
        for j in range(2):
            head = 2 * p + j
            line, lane = at + 2 + head // per_row, head % per_row * rows
            small_ref[line:line + 1, lane:lane + rows] = dtaps_ref[head]
    for p in range(pairs):
        ql, kl = lm_ref[0, :, sl[p]], lm_ref[1, :, sl[p]]
        ds2 = softmax_back(a2_ref[:, sl[p]], da_ref[:, sl[p]], ones).astype(BF16)
        dkl = dkl_ref[:, sl[p]] + pick(tn(ds2, ql))
        dql = dql_ref[:, sl[p]] + nn(ds2, spread(kl))
        dqlh, dqll = split(dql)
        dklh, dkll = split(dkl)
        dq = dq_ref[:, sl[p]] + (tn(pool, dqlh) + tn(pool, dqll))
        dk = dk_ref[:, sl[p]] + (tn(pool, dklh) + tn(pool, dkll))
        for i, m in enumerate((dq, dk)):
            dqkv_ref[:, pl.ds(i * width + p * PAIR, PAIR)] = (m * (valid * scale)).astype(BF16)
    hook(5)
    for i, line in ((0, at), (2, at + 1)):
        small_ref[line:line + 1, :] = jnp.sum(
            dqkv_ref[:, i * width:(i + 1) * width].astype(F32), axis=0, keepdims=True)
    hook(6)
    total = gr_ref[...]
    for i in range(3):
        total = total + nt(dqkv_ref[:, i * width:(i + 1) * width], stream.take(group + i))
        stream.release(group + i)
    return total.astype(BF16)


def post_backward(length, g, kept, vec, ys, gr_ref, do_ref, sums_ref, stream, group, hook):
    gd_ref, gu_ref, gp_ref = ys
    rows, width = g.shape
    chunks = gu_ref.shape[1] // width
    row = lambda i: vec[i:i + 1, :]

    def total(i, values):
        sums_ref[i:i + 1, :] = jnp.sum(values, axis=0, keepdims=True)

    valid = lax.broadcasted_iota(jnp.int32, (rows, width), 0) < length
    g = jnp.where(valid, g.astype(F32), 0.0)
    hat2 = kept["hat2"][...]
    total(4 + chunks, g * hat2)
    total(5 + chunks, g)
    second = norm_back(g * row(4 + chunks), hat2, kept["rstd"][:, 1:2])
    gd = second.astype(BF16)
    gd_ref[...] = gd
    hook(0)
    total(3 + chunks, gd.astype(F32))
    grad = second
    for c in range(chunks):
        lanes = slice(c * width, (c + 1) * width)
        gu = nt(gd, stream.take(group + 2 * c)) * kept["slope"][:, lanes].astype(F32)
        gu = gu.astype(BF16)
        stream.release(group + 2 * c)
        gu_ref[:, lanes] = gu
        total(3 + c, gu.astype(F32))
        grad = grad + nt(gu, stream.take(group + 2 * c + 1))
        stream.release(group + 2 * c + 1)
        hook(1 + c)
    hat1 = kept["hat1"][...]
    total(1, grad * hat1)
    total(2, grad)
    residual = norm_back(grad * row(1), hat1, kept["rstd"][:, 0:1])
    gr_ref[...] = residual
    gp = residual.astype(BF16)
    gp_ref[...] = gp
    hook(5)
    total(0, gp.astype(F32))
    do_ref[...] = nt(gp, stream.take(group + 2 * chunks)).astype(BF16)
    stream.release(group + 2 * chunks)


class Stream:
    def __init__(self, groups, own, other, ring, sem, arrived):
        self.groups, self.own, self.other = groups, own, other
        self.ring, self.sem, self.arrived = ring, sem, arrived
        self.slots, self.cursor, self.free, self.flowing = ring.shape[0], 0, 0, False
        self.seen = set()

    def copy(self, i, refs):
        _, w, row, col = self.groups[i]
        size = self.ring.shape[1]
        source = refs[w].at[pl.ds(row * size, size), pl.ds(col * size, size)]
        slot = i % self.slots
        return pltpu.make_async_copy(source, self.ring.at[slot], self.sem.at[slot])

    def start(self, until):
        while self.cursor < min(until, len(self.groups)):
            i = self.cursor
            own = lax.axis_index("section") == self.groups[i][0]
            fresh = self.groups[i] not in self.seen
            self.seen.add(self.groups[i])

            @pl.when(own)
            def _():
                self.copy(i, self.own).start()

            @pl.when(jnp.logical_not(own))
            def _():
                if fresh:
                    self.arrived(self.groups[i])
                self.copy(i, self.other).start()

            self.cursor += 1

    def flow(self):
        self.flowing = True
        self.start(self.free + self.slots)

    def take(self, i):
        self.start(i + 1)
        self.copy(i, self.own).wait()
        return self.ring[i % self.slots]

    def release(self, i):
        self.free = i + 1
        if self.flowing:
            self.start(self.free + self.slots)


def forward_groups(layer, chunks):
    groups = [(layer, QKV, 0, i) for i in range(3)] + [(layer, OUT, 0, 0)]
    for c in range(chunks):
        groups += [(layer, EXPAND, 0, c), (layer, REDUCE, c, 0)]
    return groups


def backward_groups(layer, chunks):
    groups = []
    for c in range(chunks):
        groups += [(layer, REDUCE, c, 0), (layer, EXPAND, 0, c)]
    return groups + [(layer, OUT, 0, 0)] + [(layer, QKV, 0, i) for i in range(3)]


def partner_of(bit):
    me = lax.axis_index("batch")
    side = (me // (1 << bit)) % 2
    return me + (1 - 2 * side) * (1 << bit), side


def place_of(block, order):
    last = len(order) - 1
    return sum(((block >> bit) & 1) << (last - k) for k, bit in enumerate(order))


class Weight:
    def __init__(self, owner, order, by_rows, parts):
        self.owner, self.order, self.by_rows, self.parts = owner, order, by_rows, parts
        self.bits = len(order)
        self.batch = 1 << self.bits
        self.rest = order[1:] if by_rows else order[1:] + order[:1]
        self.stages = len(self.rest)

    def sizes(self, x, y):
        self.block = x[1] // self.batch
        self.run = (1 << self.order[0]) * self.block
        self.runs = self.batch >> (self.order[0] + 1) if self.by_rows else 1
        self.rows, self.depth, self.width = x[0], x[1], y[1]
        self.deep = self.depth // 2 if self.by_rows else self.depth
        self.wide = self.width if self.by_rows else self.width // 2
        self.blocks = self.batch // 2 if self.by_rows else self.batch
        self.step = self.wide // self.parts
        return self

    def scratch(self):
        dma = pltpu.SemaphoreType.DMA
        return [
            pltpu.VMEM((3, self.rows, self.deep), BF16), pltpu.VMEM((3, self.rows, self.wide), BF16),
            pltpu.VMEM((self.blocks, self.block, self.wide), BF16),
            pltpu.VMEM((self.blocks - 1, self.block, self.wide), BF16),
            dma((3, self.runs)), dma((3, self.runs)), dma((3, self.parts)), dma((3, self.parts)),
            dma((self.stages, self.parts)), dma((self.stages, self.parts))]

    def bind(self, x, y, out, scratch):
        self.x, self.y, self.out = x, y, out
        (self.xr, self.yr, self.sums, self.got, self.x_sent, self.x_came, self.y_sent, self.y_came,
         self.hop_sent, self.hop_came) = scratch
        return self

    def side(self):
        return partner_of(self.order[0])[1]

    def towards(self, slot):
        other, side = partner_of(self.order[0])
        if slot == 0:
            return {"section": self.owner}, side
        return {"section": self.owner, "batch": other}, 1 - side

    def x_copies(self, slot):
        target, side = self.towards(slot)
        for r in range(self.runs):
            if self.by_rows:
                start = pl.multiple_of(2 * r * self.run + side * self.run, 128)
                source, into = self.x.at[:, pl.ds(start, self.run)], pl.ds(r * self.run, self.run)
                into = self.xr.at[slot, :, into]
            else:
                source, into = self.x, self.xr.at[slot]
            yield pltpu.make_async_remote_copy(
                src_ref=source, dst_ref=into, send_sem=self.x_sent.at[slot, r],
                recv_sem=self.x_came.at[slot, r], device_id=target, device_id_type=MESH)

    def y_copy(self, slot, part):
        target, side = self.towards(slot)
        lanes = pl.ds(part * self.step, self.step)
        if self.by_rows:
            source = self.y.at[:, lanes]
        else:
            start = pl.multiple_of(side * self.wide + part * self.step, 128)
            source = self.y.at[:, pl.ds(start, self.step)]
        return pltpu.make_async_remote_copy(
            src_ref=source, dst_ref=self.yr.at[slot, :, lanes], send_sem=self.y_sent.at[slot, part],
            recv_sem=self.y_came.at[slot, part], device_id=target, device_id_type=MESH)

    def send_x(self, slots):
        for slot in slots:
            for copy in self.x_copies(slot):
                copy.start()

    def send_y(self, slots):
        for part in range(self.parts):
            for slot in slots:
                self.y_copy(slot, part).start()

    def drain_factors(self, slots):
        for slot in slots:
            for copy in self.x_copies(slot):
                copy.wait_send()
            for part in range(self.parts):
                self.y_copy(slot, part).wait_send()

    def multiply(self, part):
        if part == 0:
            for slot in range(3):
                for copy in self.x_copies(slot):
                    copy.wait_recv()
        for slot in range(3):
            self.y_copy(slot, part).wait_recv()
        side = self.side()
        lanes = slice(part * self.step, (part + 1) * self.step)
        if self.by_rows:
            near = self.y[:, lanes]
        else:
            start = pl.multiple_of(side * self.wide + part * self.step, 128)
            near = self.y[:, pl.ds(start, self.step)]
        right = cat([near] + [self.yr[s, :, lanes] for s in range(3)], 0)
        rows = self.block * 128 // math.gcd(self.block, 128)
        for base in range(0, self.deep, rows):
            if self.by_rows:
                r, inside = base // self.run, base % self.run
                spot = pl.ds(pl.multiple_of(2 * r * self.run + side * self.run + inside, 128), rows)
            else:
                spot = pl.ds(base, rows)
            left = cat([self.x[:, spot]] + [self.xr[s, :, base:base + rows] for s in range(3)], 0)
            value = tn(left, right).astype(BF16)
            for j in range(rows // self.block):
                block = base // self.block + j
                if self.by_rows:
                    low = 1 << self.order[0]
                    block = block // low * 2 * low + block % low
                self.sums[place_of(block, self.rest), :, lanes] = (
                    value[j * self.block:(j + 1) * self.block])
        self.hop(0, part).start()

    def spans(self, stage):
        half = self.blocks >> (stage + 1)
        start = 0
        for k in range(stage):
            start = start + partner_of(self.rest[k])[1] * (self.blocks >> (k + 1))
        side = partner_of(self.rest[stage])[1]
        return half, start + side * half, start + (1 - side) * half, self.blocks - 2 * half

    def hop(self, stage, part):
        half, _, away, landing = self.spans(stage)
        lanes = pl.ds(part * self.step, self.step)
        return pltpu.make_async_remote_copy(
            src_ref=self.sums.at[pl.ds(away, half), :, lanes],
            dst_ref=self.got.at[pl.ds(landing, half), :, lanes],
            send_sem=self.hop_sent.at[stage, part], recv_sem=self.hop_came.at[stage, part],
            device_id={"batch": partner_of(self.rest[stage])[0]}, device_id_type=MESH)

    def advance(self, stage, part):
        half, keep, _, landing = self.spans(stage)
        lanes = slice(part * self.step, (part + 1) * self.step)
        self.hop(stage, part).wait_recv()
        if stage + 1 < self.stages:
            def add(j, carry):
                self.sums[keep + j, :, lanes] = (
                    self.sums[keep + j, :, lanes].astype(F32)
                    + self.got[landing + j, :, lanes].astype(F32)).astype(BF16)
                return carry

            lax.fori_loop(0, half, add, 0)
            self.hop(stage + 1, part).start()
            return
        mine, theirs = self.sums[keep, :, lanes].astype(F32), self.got[landing, :, lanes].astype(F32)
        if self.by_rows:
            self.out[:, lanes] = mine + theirs
        else:
            first = self.side() == 0
            far = slice(self.wide + part * self.step, self.wide + (part + 1) * self.step)
            self.out[:, lanes] = jnp.where(first, mine, theirs)
            self.out[:, far] = jnp.where(first, theirs, mine)

    def drain(self):
        self.drain_factors((1,))
        for stage in range(self.stages):
            for part in range(self.parts):
                self.hop(stage, part).wait_send()


class Small:
    parts = 1

    def __init__(self, owner, bits):
        self.owner, self.bits, self.stages = owner, bits, bits

    def scratch(self, dims):
        dma = pltpu.SemaphoreType.DMA
        return [pltpu.VMEM((self.bits + 1,) + dims, F32), pltpu.VMEM((self.bits + 1,) + dims, F32),
                dma((self.bits + 1,)), dma((self.bits + 1,))]

    def bind(self, x, out, scratch):
        self.x, self.out = x, out
        self.got, self.sums, self.sent, self.came = scratch
        return self

    def arrive(self):
        return pltpu.make_async_remote_copy(
            src_ref=self.x, dst_ref=self.got.at[self.bits], send_sem=self.sent.at[self.bits],
            recv_sem=self.came.at[self.bits], device_id={"section": self.owner}, device_id_type=MESH)

    def hop(self, stage):
        return pltpu.make_async_remote_copy(
            src_ref=self.sums.at[stage], dst_ref=self.got.at[stage], send_sem=self.sent.at[stage],
            recv_sem=self.came.at[stage], device_id={"batch": partner_of(stage)[0]},
            device_id_type=MESH)

    def send_y(self, slots):
        if 0 in slots:
            self.arrive().start()

    def drain_factors(self, slots):
        self.arrive().wait_send()

    def multiply(self, part):
        self.arrive().wait_recv()
        self.sums[0] = self.x[...] + self.got[self.bits]
        self.hop(0).start()

    def advance(self, stage, part):
        self.hop(stage).wait_recv()
        self.sums[stage + 1] = self.sums[stage] + self.got[stage]
        if stage + 1 < self.bits:
            self.hop(stage + 1).start()
        else:
            self.out[...] = self.sums[self.bits]

    def drain(self):
        for stage in range(self.bits):
            self.hop(stage).wait_send()


def greet(bits, near):
    barrier = pltpu.get_barrier_semaphore()
    other = 1 - lax.axis_index("section")
    targets = [{"section": other}]
    targets += [{"batch": partner_of(bit)[0]} for bit in range(bits)]
    targets += [{"section": other, "batch": partner_of(bit)[0]} for bit in near]
    for target in targets:
        pl.semaphore_signal(barrier, inc=1, device_id=target, device_id_type=MESH)
    pl.semaphore_wait(barrier, len(targets))


class Take:
    def __init__(self, refs):
        self.refs, self.at = refs, 0

    def __call__(self, count):
        self.at += count
        return self.refs[self.at - count:self.at]


def residuals(rows, width, hidden):
    heads = width // LM
    return {
        "qkv": ((3, rows, width), BF16), "lm": ((2, LM, width), BF16), "a1": ((rows, width), F32),
        "a2": ((LM, width), F32), "a3": ((LM, heads * rows), F32),
        "band": ((heads // 2, rows, 2 * rows), BF16), "db": ((2, LM, width), BF16),
        "z": ((NEWTON + 1, LM, width), F32), "r": ((NEWTON + 1, LM, width), F32),
        "s": ((NEWTON, LM, width), F32), "t": ((NEWTON, LM, width), F32),
        "hat1": ((rows, width), F32), "hat2": ((rows, width), F32), "rstd": ((rows, 128), F32),
        "slope": ((rows, hidden), BF16)}


def encoder(*refs, names, plans, littles, taps, remote):
    take = Take(refs)
    (lengths_ref,) = take(1)
    input_ref, cotangent_ref, bias_ref, taps_ref = take(4)
    params = take(7)
    own = take(4)
    other_in = () if remote else take(4)
    vec_in = () if remote else take(2)
    act_out, ig_ref = take(2)
    count = len(plans[0])
    outs = take(4) if remote else ()
    small_out = take(1)[0] if remote else None
    other = take(4) if remote else other_in
    layers_out = () if remote else [take(9), take(9)]
    kept = [dict(zip(names, take(len(names)))) for _ in range(2)]
    ring, ring_sem, mid_ref, gi_ref, gr_ref, do_ref = take(6)
    forward_work, work = take(4), take(9)
    (err_ref,) = take(1)
    vecs, tap_rows = take(2)
    section = lax.axis_index("section")
    rows, width = mid_ref.shape
    hidden = own[EXPAND].shape[1]
    chunks, heads = hidden // width, width // LM
    at = 6 + chunks
    err = at + 2 + heads // (width // rows)
    groups = []
    for part, layer in ((forward_groups, 0), (forward_groups, 1), (backward_groups, 1), (backward_groups, 0)):
        groups += part(layer, chunks)
    length = lengths_ref[section]
    if remote:
        factors = [take(7), take(7)]
        smalls = take(2)
        own_sent, own_came, vec_sent, vec_came, share_sent, share_came = take(6)
        scratch = [take(10) for _ in range(count)]
        small_scratch = take(4)
    else:
        factors = [layer[:7] for layer in layers_out]
        smalls = [layer[7] for layer in layers_out]
    x_ref = input_ref.at[pl.ds(section * rows, rows)]
    for layer in range(2):
        kept[layer].update(zip(("act", "first", "att"), factors[layer][:3]))
        smalls[layer][...] = jnp.zeros(smalls[layer].shape, F32)
    ys = [f[3:7] for f in factors]
    pieces = [g for g in forward_groups(0, chunks)]

    def pack(vec, taps_to):
        line = 0
        taps_to[...] = jnp.zeros(taps_to.shape, F32)
        for h in range(heads):
            taps_to[h, :, 0:taps] = taps_ref[h]
        for ref in params + (bias_ref,):
            for c in range(ref.shape[1] // width):
                vec[line:line + 1, :] = ref[:, c * width:(c + 1) * width]
                line += 1

    def weight_copy(i):
        _, w, row, col = pieces[i]
        spot = (pl.ds(row * width, width), pl.ds(col * width, width))
        return pltpu.make_async_remote_copy(
            src_ref=own[w].at[spot], dst_ref=other[w].at[spot], send_sem=own_sent.at[i],
            recv_sem=own_came.at[i], device_id={"section": 1 - section}, device_id_type=MESH)

    def vec_copy(i):
        ref = (vecs, tap_rows)[i]
        return pltpu.make_async_remote_copy(
            src_ref=ref.at[section], dst_ref=ref.at[section], send_sem=vec_sent.at[i],
            recv_sem=vec_came.at[i], device_id={"section": 1 - section}, device_id_type=MESH)

    def vec_wait(i):
        ref = (vecs, tap_rows)[i]
        return pltpu.make_async_remote_copy(
            src_ref=ref.at[1 - section], dst_ref=ref.at[1 - section], send_sem=vec_sent.at[i],
            recv_sem=vec_came.at[i], device_id={"section": 1 - section}, device_id_type=MESH)

    def arrived(group):
        if remote:
            weight_copy(pieces.index((0,) + group[1:])).wait_recv()

    stream = Stream(groups, own, other, ring, ring_sem, arrived)
    if remote:
        items = []
        for layer in range(2):
            x0 = x_ref if layer == 0 else mid_ref
            f = factors[layer]
            third = [pl.ds(i * width, width) for i in range(3)]
            xs = (f[0], f[1], x0, x0, x0, f[2])
            yy = (f[3], f[4]) + tuple(f[6].at[:, t] for t in third) + (f[5],)
            to = outs[:2] + tuple(outs[2].at[:, t] for t in third) + outs[3:]
            items.append([w.bind(xs[i], yy[i], to[i], scratch[i])
                          for i, w in enumerate(plans[layer])]
                         + [littles[layer].bind(smalls[layer], small_out, small_scratch)])
        greet(littles[0].bits, sorted({w.order[0] for w in plans[0]}))
        pack(vecs.at[section], tap_rows.at[section])
        for i in range(2):
            vec_copy(i).start()
        for i in range(3):
            weight_copy(i).start()
        stream.start(1)
        for i in range(2):
            vec_wait(i).wait_recv()
    else:
        vecs[...] = vec_in[0][...]
        tap_rows[...] = vec_in[1][...]

    def send(layer, which, what):
        if remote:
            for role, slots in ((section == layer, (1,)), (section != layer, (0, 2))):
                @pl.when(role)
                def _():
                    for i in which:
                        getattr(items[layer][i], what)(slots)

    def run(layer, *jobs):
        if remote:
            @pl.when(section == layer)
            def _():
                for item, stage, part in jobs:
                    if stage is None:
                        items[layer][item].multiply(part)
                    else:
                        items[layer][item].advance(stage, part)

    def both_rows(k, layer, source, target):
        def copy():
            return pltpu.make_async_remote_copy(
                src_ref=source, dst_ref=target.at[pl.ds((1 - layer) * rows, rows)],
                send_sem=share_sent.at[k], recv_sem=share_came.at[k],
                device_id={"section": layer}, device_id_type=MESH)

        if remote:
            @pl.when(section == layer)
            def _():
                target[layer * rows:(layer + 1) * rows, :] = source[...]

            @pl.when(section != layer)
            def _():
                copy().start()
        else:
            target[layer * rows:(layer + 1) * rows, :] = source[...]
        return copy

    def schedule(name, slot):
        steps = SCHEDULE.get((name, slot), ())
        for step in steps:
            if step[0] == "x":
                send(step[1], step[2], "send_x")
            elif step[0] == "y":
                send(step[1], step[2], "send_y")
            else:
                run(step[1], *step[2])

    def hook(name, slot):
        if name == "forward0" and slot == 0 and remote:
            for i in range(3):
                weight_copy(i).wait_send()
            for i in range(3, len(pieces)):
                weight_copy(i).start()
        if name == "forward0" and slot == 1:
            stream.flow()
        schedule(name, slot)

    per_layer = len(forward_groups(0, chunks))
    x = x_ref[...]
    shared = []
    for layer in range(2):
        vec = vecs[layer]
        bias = (vec[at:at + 1], None, vec[at + 1:at + 2])
        name = "forward" + str(layer)
        attention_forward(
            length, x, bias, tap_rows.at[layer], kept[layer], (smalls[layer], err, err_ref),
            forward_work, stream,
            layer * per_layer, functools.partial(hook, name), taps)
        out = post_forward(length, x, vec, kept[layer], stream, layer * per_layer + 3)
        mid_or_out = mid_ref if layer == 0 else gi_ref.at[2]
        mid_or_out[...] = out
        shared.append((layer, both_rows(layer, layer, mid_or_out, act_out)))
        schedule(name, 3)
        x = out
    g = cotangent_ref[pl.ds(section * rows, rows), :]
    group = 2 * per_layer
    for layer in (1, 0):
        name = "backward" + str(layer)
        y = ys[layer]
        post_backward(
            length, g, kept[layer], vecs[layer], (y[0], y[1], y[2]), gr_ref, do_ref, smalls[layer],
            stream, group, functools.partial(schedule, "post" + str(layer)))
        g = attention_backward(
            length, do_ref, gr_ref, kept[layer], y[3], smalls[layer], at, work, stream,
            group + 1 + 2 * chunks, functools.partial(schedule, name), taps)
        gi_ref[layer] = g
        shared.append((layer, both_rows(2 + layer, layer, gi_ref.at[layer], ig_ref)))
        schedule(name, 7)
        group += per_layer
    if remote:
        schedule("tail", 0)
        for layer in range(2):
            @pl.when(section == layer)
            def _():
                for item in items[layer]:
                    item.drain()

            @pl.when(section != layer)
            def _():
                for item in items[layer]:
                    item.drain_factors((0, 2))
        for k, (layer, copy) in enumerate(shared):
            @pl.when(section == layer)
            def _():
                copy().wait_recv()

            @pl.when(section != layer)
            def _():
                copy().wait_send()
        for i in range(3, len(pieces)):
            weight_copy(i).wait_send()
        for i in range(2):
            vec_copy(i).wait_send()
    else:
        for layer in range(2):
            layers_out[layer][8][...] = gi_ref[2] if layer else mid_ref[...]


RED, EXP, PRQ, PRK, PRV, PUT, SMALL = range(7)


def steps(layer, *jobs):
    return ("run", layer, jobs)


def mult(item, *parts):
    return tuple((item, None, part) for part in parts)


SCHEDULE = {
    ("forward0", 0): [("x", 0, (PRQ, PRK, PRV))],
    ("forward0", 2): [("x", 0, (PUT,))],
    ("forward0", 3): [("x", 1, (PRQ, PRK, PRV)), ("x", 0, (RED, EXP))],
    ("forward1", 2): [("x", 1, (PUT,))],
    ("forward1", 3): [("x", 1, (RED, EXP))],
    ("post1", 0): [("y", 1, (RED,))],
    ("post1", 4): [("y", 1, (EXP,))],
    ("post1", 5): [("y", 1, (PUT,))],
    ("backward1", 0): [steps(1, (RED, None, 0))],
    ("backward1", 1): [steps(1, (RED, None, 1), (PUT, None, 0))],
    ("backward1", 2): [steps(1, (EXP, None, 0), (EXP, None, 1), (EXP, None, 2), (RED, 0, 0))],
    ("backward1", 3): [steps(1, (PUT, 0, 0))],
    ("backward1", 5): [steps(1, (RED, 1, 0), (RED, 0, 1), (EXP, 0, 0))],
    ("backward1", 6): [("y", 1, (PRV, PRQ, PRK, SMALL,)), steps(1, (SMALL, None, 0))],
    ("backward1", 7): [steps(1, (PUT, 1, 0))],
    ("post0", 0): [("y", 0, (RED,))],
    ("post0", 1): [steps(1, (EXP, 0, 1))],
    ("post0", 2): [steps(1, (EXP, 1, 0))],
    ("post0", 3): [steps(1, (PRV, None, 0), (RED, 2, 0), (RED, 1, 1), (PUT, 2, 0), (EXP, 0, 2), (SMALL, 0, 0), (PRQ, None, 0))],
    ("post0", 4): [("y", 0, (EXP,))],
    ("post0", 5): [("y", 0, (PUT,))],
    ("backward0", 0): [steps(1, (EXP, 2, 0), (EXP, 1, 1), (PRK, None, 0), (PUT, 3, 0))],
    ("backward0", 1): [steps(1, (EXP, 1, 2), (RED, 2, 1), (EXP, 2, 1), (PRV, 0, 0))],
    ("backward0", 2): [steps(1, (SMALL, 1, 0), (EXP, 2, 2), (PRK, 0, 0), (EXP, 3, 0), (PRQ, 0, 0), (EXP, 3, 1)), steps(0, (RED, None, 0))],
    ("backward0", 3): [steps(1, (PRV, 1, 0), (EXP, 3, 2), (PRK, 1, 0), (SMALL, 2, 0)), steps(0, (PUT, None, 0), (EXP, None, 0), (EXP, None, 1), (RED, None, 1))],
    ("backward0", 4): [steps(1, (PRQ, 1, 0)), steps(0, (EXP, None, 2))],
    ("backward0", 6): [("y", 0, (PRV, PRQ, PRK, SMALL,))],
    ("backward0", 7): [steps(1, (PRV, 2, 0))],
    ("tail", 0): [steps(1, (PRK, 2, 0), (SMALL, 3, 0), (PRQ, 2, 0), (PRV, 3, 0), (PRK, 3, 0), (PRQ, 3, 0)), steps(0, (RED, 0, 0), (PUT, 0, 0), (EXP, 0, 0), (RED, 0, 1), (RED, 1, 0), (SMALL, None, 0), (EXP, 0, 1), (PUT, 1, 0), (EXP, 1, 0), (PRV, None, 0), (PRQ, None, 0), (EXP, 0, 2), (SMALL, 0, 0), (PRK, None, 0), (RED, 1, 1), (RED, 2, 0), (EXP, 1, 1), (PUT, 2, 0), (PRV, 0, 0), (EXP, 1, 2), (EXP, 2, 0), (PRQ, 0, 0), (PRK, 0, 0), (PUT, 3, 0), (SMALL, 1, 0), (RED, 2, 1), (PRV, 1, 0), (EXP, 2, 1), (EXP, 3, 0), (PRQ, 1, 0), (EXP, 2, 2), (PRK, 1, 0), (PRV, 2, 0), (SMALL, 2, 0), (EXP, 3, 1), (PRQ, 2, 0), (PRV, 3, 0), (EXP, 3, 2), (PRK, 2, 0), (PRQ, 3, 0), (SMALL, 3, 0), (PRK, 3, 0))],
}


def shape(dims, kind=F32):
    return jax.ShapeDtypeStruct(dims, kind)


IN_VMEM = pl.BlockSpec(memory_space=pltpu.VMEM)
IN_SMEM = pl.BlockSpec(memory_space=pltpu.SMEM)
ANYWHERE = pl.BlockSpec(memory_space=pl.ANY)
VMEM_LIMIT = 62 * 2 ** 20
RING = 6


def plan(owner, bits):
    tail = tuple(range(3, bits))
    return [Weight(owner, (1, 0, 2) + tail, True, 2), Weight(owner, (2, 1, 0) + tail, False, 3),
            Weight(owner, (0, 1, 2) + tail, False, 1), Weight(owner, (1, 0, 2) + tail, False, 1),
            Weight(owner, (0, 1, 2) + tail, False, 1), Weight(owner, (0, 1, 2) + tail, False, 1)]


def small_shape(width, hidden, heads, rows):
    lines = 6 + hidden // width + 2 + heads // (width // rows) + NEWTON
    return (lines + 7) // 8 * 8, width


def encode(remote, batch, lengths, layer_input, cotangent, bias, conv_kernel, params, weights, extra):
    rows, width = layer_input.shape[0] // 2, layer_input.shape[1]
    hidden, heads = weights[EXPAND].shape[1], width // LM
    chunks, bits = hidden // width, batch.bit_length() - 1
    dma = pltpu.SemaphoreType.DMA
    low = lambda n: ((rows, n), BF16)
    factor_shapes = [low(hidden), low(width), low(width), low(width), low(hidden), low(width), low(3 * width)]
    x_shapes = [(rows, n) for n in (hidden, width, width, width, width, width)]
    y_shapes = [(rows, n) for n in (width, hidden, width, width, width, width)]
    dims = small_shape(width, hidden, heads, rows)
    plans = littles = None
    plans, littles = [], []
    for layer in range(2):
        plans.append([w.sizes(a, b) for w, a, b in zip(plan(layer, bits), x_shapes, y_shapes)])
        littles.append(Small(layer, bits))
    both = shape((2 * rows, width), BF16)
    outs, out_specs = [both, both], [IN_VMEM] * 2
    if remote:
        outs += [shape((w.shape[0] // batch, w.shape[1])) for w in (
            weights[REDUCE], weights[EXPAND], weights[QKV], weights[OUT])] + [shape(dims)]
        out_specs += [IN_VMEM] * 5
        outs += [shape(w.shape, BF16) for w in weights]
        out_specs += [ANYWHERE] * 4
    else:
        for _ in range(2):
            outs += [shape(*f) for f in factor_shapes] + [shape(dims), shape((rows, width), BF16)]
            out_specs += [IN_VMEM] * 9
    names = residuals(rows, width, hidden)
    scratch = [pltpu.VMEM(*s) for _ in range(2) for s in names.values()]
    scratch += [pltpu.VMEM((RING, width, width), BF16), dma((RING,)), pltpu.VMEM(*low(width)),
                pltpu.VMEM((3, rows, width), BF16), pltpu.VMEM((rows, width), F32),
                pltpu.VMEM(*low(width))]
    scratch += [pltpu.VMEM((3, rows, width), BF16), pltpu.VMEM((2, LM, width), BF16),
                pltpu.VMEM((LM, width), BF16), pltpu.VMEM((rows, width), F32)]
    scratch += [pltpu.VMEM((LM, width), F32)] * 3 + [
        pltpu.VMEM((LM, width), BF16), pltpu.VMEM((rows, width), F32), pltpu.VMEM((rows, width), F32),
        pltpu.VMEM((LM, width), F32), pltpu.VMEM((LM, width), F32), pltpu.VMEM((16, 1, rows), F32)]
    scratch += [pltpu.VMEM((NEWTON, 1, width), F32)]
    scratch += [pltpu.VMEM((2, 16, width), F32), pltpu.VMEM((2, 16, 1, 128), F32)]
    if remote:
        pieces = 4 + 2 * chunks
        scratch += [pltpu.VMEM(*f) for _ in range(2) for f in factor_shapes]
        scratch += [pltpu.VMEM(dims, F32)] * 2
        scratch += [dma((pieces,)), dma((pieces,)), dma((2,)), dma((2,)), dma((4,)), dma((4,))]
        scratch += [s for w in plans[0] for s in w.scratch()] + littles[0].scratch(dims)
    args = (lengths, layer_input, cotangent, bias, conv_kernel) + params + weights + extra
    ins = [IN_SMEM] + [IN_VMEM] * 11 + [ANYWHERE] * 4
    if not remote:
        ins += [ANYWHERE] * 4 + [IN_VMEM] * 2
    marks = dict(collective_id=0, has_side_effects=True) if remote else {}
    return pl.pallas_call(
        functools.partial(encoder, names=tuple(names), plans=plans, littles=littles,
                          taps=conv_kernel.shape[-1], remote=remote),
        out_shape=tuple(outs), in_specs=ins, out_specs=tuple(out_specs), scratch_shapes=scratch,
        name="encoder", cost_estimate=pl.CostEstimate(
            flops=2 * 10 ** 10, bytes_accessed=10 ** 8, transcendentals=0),
        compiler_params=pltpu.CompilerParams(vmem_limit_bytes=VMEM_LIMIT, **marks))(*args)


def finish(act, ig, red, exp, pro, put, small_ref, *refs, taps):
    whole, rest = refs[:6], refs[6:]
    for source, target in zip((act, ig, pro, put, exp, red), whole):
        target[...] = source[...]
    bias, conv, out_bias, gain1, shift1, up_bias, down_bias, gain2, shift2, proxies = rest
    width = small_ref.shape[1]
    chunks = exp.shape[1] // width
    rows, heads = act.shape[0] // 2, conv.shape[0]
    at, per_row = 6 + chunks, width // rows
    batch = width // out_bias.shape[1]
    index = lax.axis_index("batch")
    small = small_ref[...]
    turned = {}

    def share(out, first, many):
        size = out.shape[1]
        if size not in turned:
            turned[size] = pltpu.roll(small, lax.rem(width - lax.rem(index * size, width), width), 1)
        line = index * size // width
        value = turned[size][first:first + 1]
        for r in range(1, many):
            value = jnp.where(line == r, turned[size][first + r:first + r + 1], value)
        out[...] = value[:, :size]

    share(bias, at, 2)
    for out, first, many in ((out_bias, 0, 1), (gain1, 1, 1), (shift1, 2, 1), (up_bias, 3, chunks),
                             (down_bias, 3 + chunks, 1), (gain2, 4 + chunks, 1), (shift2, 5 + chunks, 1)):
        share(out, first, many)
    for h in range(heads):
        line, lane = at + 2 + h // per_row, h % per_row * rows
        conv[h] = small[line:line + 1, lane:lane + taps]
    end = at + 2 + heads // per_row
    sums = jnp.sum(small[end:end + NEWTON], axis=1, keepdims=True)
    spot = lax.broadcasted_iota(jnp.int32, (1, NEWTON), 1)
    value = jnp.zeros((1, NEWTON), F32)
    for i in range(NEWTON):
        value = jnp.where(spot == i, sums[i:i + 1], value)
    proxies[...] = value


def finish_call(results, batch, width, hidden, heads, taps):
    act, ig, red, exp, pro, put, small = results
    part = lambda n: shape((1, n // batch))
    outs = [jax.ShapeDtypeStruct(r.shape, r.dtype) for r in (act, ig, pro, put, exp, red)]
    outs += [part(2 * width), shape((heads, 1, taps)), part(width), part(width), part(width),
             part(hidden), part(width), part(width), part(width), shape((1, NEWTON))]
    return pl.pallas_call(
        functools.partial(finish, taps=taps), out_shape=tuple(outs),
        in_specs=[IN_VMEM] * 7, out_specs=(IN_VMEM,) * 16, name="finish",
        compiler_params=pltpu.CompilerParams(vmem_limit_bytes=VMEM_LIMIT))(
            act, ig, red, exp, pro, put, small)


def swap(value):
    return lax.ppermute(value, "section", [(0, 1), (1, 0)])


def encode_apart(batch, args, weights, params, bias, conv_kernel):
    section = lax.axis_index("section")
    width = args[1].shape[1]
    heads, _, taps = conv_kernel.shape
    vec = jnp.concatenate([p.reshape(-1, width) for p in params + (bias,)])
    vec = jnp.pad(vec, ((0, 16 - vec.shape[0]), (0, 0)))
    rows_of_taps = jnp.pad(conv_kernel, ((0, 16 - heads), (0, 0), (0, 128 - taps)))
    extra = [swap(w) for w in weights]
    for mine in (vec, rows_of_taps):
        theirs = swap(mine)
        extra.append(jnp.where(section == 0, jnp.stack([mine, theirs]), jnp.stack([theirs, mine])))
    result = encode(False, batch, *args, bias, conv_kernel, params, weights, tuple(extra))
    total = args[1].shape[0]
    rows = total // 2
    layers = [result[2:11], result[11:20]]
    inputs = [lax.dynamic_slice_in_dim(args[1], section * rows, rows, 0), layers[0][8]]
    shares = []
    for layer in range(2):
        act, first, att, gd, gu, gp, dqkv, small, _ = layers[layer]
        products = [lax.dot_general(x, y, (((0,), (0,)), ((), ())), preferred_element_type=F32)
                    for x, y in ((act, gd), (first, gu), (inputs[layer], dqkv), (att, gp))]
        shares.append([
            lax.psum_scatter(lax.psum(p, "section"), "batch", scatter_dimension=0, tiled=True)
            for p in products] + [lax.psum(small, ("section", "batch"))])
    lead = section == 0
    both = []
    for k in range(2):
        by_layer = [result[k][:rows], result[k][rows:]]
        crossed = swap(jnp.where(lead, by_layer[1], by_layer[0]))
        both.append(jnp.where(lead, jnp.concatenate([by_layer[0], crossed]),
                              jnp.concatenate([crossed, by_layer[1]])))
    return both + [jnp.where(lead, a, b) for a, b in zip(*shares)]


def body(
    layer_input, seq_lengths, cotangent, project_weight, project_bias, conv_kernel, output_weight,
    output_bias, attn_gain, attn_shift, expand_weight, expand_bias, reduce_weight, reduce_bias,
    final_gain, final_shift):
    batch = lax.axis_size("batch")
    width = layer_input.shape[1]
    heads, taps = conv_kernel.shape[1:]
    weights = (project_weight[0], output_weight[0], expand_weight[0], reduce_weight[0])
    params = (output_bias, attn_gain, attn_shift, expand_bias, reduce_bias, final_gain, final_shift)
    args = (seq_lengths, layer_input, cotangent)
    conv_kernel = conv_kernel.transpose(1, 0, 2)
    if batch >= 8 and all(w.shape[0] // batch % 16 == 0 for w in weights):
        result = encode(True, batch, *args, project_bias, conv_kernel, params, weights, ())
    else:
        result = encode_apart(batch, args, weights, params, project_bias, conv_kernel)
    hidden = reduce_weight.shape[1]
    act, ig, pro, put, exp, red, bias, conv, *rest = finish_call(
        result[:7], batch, width, hidden, heads, taps)
    out_bias, gain1, shift1, up_bias, down_bias, gain2, shift2, proxies = rest
    return (
        act[None], ig[None], pro[None], bias, conv.transpose(1, 0, 2), put[None], out_bias, gain1,
        shift1, exp[None], up_bias, red[None], down_bias, gain2, shift2, proxies)


def solution(mesh):
    split_rows = P("batch", None)
    two, three = P("section", None), P("section", None, None)
    return jax.shard_map(
        body, mesh=mesh,
        in_specs=(split_rows, P("batch"), split_rows, three, two, three, three, two, two, two,
                  three, two, three, two, two, two),
        out_specs=(P("section", "batch", None), P("section", "batch", None),
                   P("section", "batch", None), P("section", "batch"), three,
                   P("section", "batch", None), P("section", "batch"), P("section", "batch"),
                   P("section", "batch"), P("section", "batch", None), P("section", "batch"),
                   P("section", "batch", None), P("section", "batch"), P("section", "batch"),
                   P("section", "batch"), two),
        check_vma=False)
```
